32 devices in a mesh: dp: 4 (over z), ep: 8 (over y, x, core).
Axes of the slice: x: 2, y: 2, z: 4, core: 2. Of those that a mesh axis runs over, the one named last changes fastest.
Arguments:
- tokens: bfloat16 [16384, 1024], P(('dp', 'ep')), may hold values from -6 to 6
- bucket: int32 [32], P(('dp', 'ep')), may hold values from 0 to 1
- expert_ids: int32 [16384, 1], P(('dp', 'ep')), may hold values from 0 to 7
- ln1_gain: float32 [1024], replicated, may hold values from 0.5 to 1.5
- qkv_weight: bfloat16 [1024, 3072], P('ep'), may hold values from -0.1875 to 0.1875
- out_weight: bfloat16 [1024, 1024], P('ep'), may hold values from -0.75 to 0.75
- ln2_gain: float32 [1024], replicated, may hold values from 0.5 to 1.5
- up_weight: bfloat16 [1024, 4096], P('ep'), may hold values from -0.1875 to 0.1875
- down_weight: bfloat16 [4096, 1024], P('ep'), may hold values from -0.1875 to 0.1875
- mix_weight: bfloat16 [1024, 2], replicated, may hold values from -0.1875 to 0.1875
- expert_up: bfloat16 [8, 1024, 4096], P('ep', None, 'dp'), may hold values from -0.1875 to 0.1875
- expert_down: bfloat16 [8, 4096, 1024], P('ep', 'dp'), may hold values from -0.1875 to 0.1875
- cotangent: bfloat16 [16384, 1024], P(('dp', 'ep')), may hold values from -6 to 6
Outputs:
- output: bfloat16 [16384, 1024], P(('dp', 'ep'))
- tokens_grad: float32 [16384, 1024], P(('dp', 'ep'))
- ln1_gain_grad: float32 [1024], replicated
- qkv_weight_grad: float32 [1024, 3072], P('ep')
- out_weight_grad: float32 [1024, 1024], P('ep')
- ln2_gain_grad: float32 [1024], replicated
- up_weight_grad: float32 [1024, 4096], P('ep')
- down_weight_grad: float32 [4096, 1024], P('ep')
- mix_weight_grad: float32 [1024, 2], replicated
- expert_up_grad: float32 [8, 1024, 4096], P('ep', None, 'dp')
- expert_down_grad: float32 [8, 4096, 1024], P('ep', 'dp')
The draws below stay inside these ranges and needn't reach their ends.
All inputs are finite; a program needn't handle non-finite values.
Results may differ from the reference program's by a relative error of at most 0.02.
Values may be sent and summed in bfloat16 or wider, within the bound.
A program may use at most 320 MiB of HBM per device.

```python
import jax
import jax.numpy as jnp
from jax import lax

D = 1024
HEADS = 16
HEAD = 64
FF = 4096
TOK_DEV = 512
SHORT_SEQS = 4
EXPERTS = 8
CAP_DEV = 80
BLOCKS = 32
TOKENS = 16384


def plant(entries, key, least, largest):
    index_at = [jax.random.randint(jax.random.fold_in(key, axis), (), 0, length) for axis, length in enumerate(entries.shape)]
    main_axis = entries.shape.index(max(entries.shape))
    neighbour = index_at[:main_axis] + [(index_at[main_axis] + 1) % entries.shape[main_axis]] + index_at[main_axis + 1:]
    return entries.at[tuple(index_at)].set(least).at[tuple(neighbour)].set(largest)


def raised(array, rng, source, target, parts, factor):
    owner, partner = [(jnp.arange(array.shape[axis_at]) // (array.shape[axis_at] // parts)).reshape([-1 if axis == axis_at else 1 for axis in range(array.ndim)]) for axis_at in (source, target)]
    chosen = jax.random.permutation(rng, parts)[partner]
    strong = (owner == chosen) | (owner == (partner + parts // 2) % parts)
    return jnp.where(strong, factor * array, array)


def shard_levels(rng, dims, shards, smallest, largest):
    gain, own = 1.0, jax.random.fold_in(rng, 6)
    for dim, parts in shards:
        heights = jnp.exp(jax.random.uniform(jax.random.fold_in(own, dim), (parts,), jnp.float32, smallest / len(shards), largest / len(shards)))
        gain = gain * jnp.repeat(heights, dims[dim] // parts).reshape([-1 if axis == dim else 1 for axis in range(len(dims))])
    return gain


def different_ones(rng, rows, amount, top, lift):
    ranking = jax.random.permutation(jax.random.fold_in(rng, 1), amount)
    boost = ranking
    for power in range(3):
        boost = boost * boost // amount
    boost = boost * lift // amount
    chance = jax.random.randint(jax.random.fold_in(rng, 2), (rows, amount), 0, 4096) + boost
    holders = jax.random.permutation(jax.random.fold_in(rng, 3), rows)[jnp.arange(amount) % rows]
    chance = jnp.where(jnp.arange(rows)[:, None] == holders[None, :], 1 << 14, chance)
    merit = chance * amount + jnp.arange(amount)
    return lax.top_k(merit.astype(jnp.int32), top)[1].astype(jnp.int32)


def noise(stream_key, extent, deviation, reach, split=(), kind=jnp.bfloat16):
    values = jax.random.normal(stream_key, extent, jnp.float32) * deviation
    if len(split) > 0:
        values = shard_levels(stream_key, extent, split, -0.22, 0.18) * values
    return jnp.clip(values, min=-reach, max=reach).astype(kind)


def bell_draw_with(key, extent, spread, most, shards, heavy, kind=jnp.bfloat16):
    drawn = spread * jax.random.normal(key, extent, jnp.float32)
    if shards:
        drawn = drawn * shard_levels(key, extent, shards, -0.22, 0.18)
    return jnp.clip(raised(drawn, jax.random.fold_in(key, 3), *heavy), -most, most).astype(kind)


def setup_inputs(seed: int = 0) -> dict:
    streams_of = jax.random.split(jax.random.key(seed), 14)
    tokens = bell_draw_with(streams_of[0], (TOKENS, D), 1.0, 6.0, ((0, 32),), (0, 1, 32, 2.75))
    bucket = plant(jax.random.randint(streams_of[1], (BLOCKS,), 0, 2), jax.random.fold_in(streams_of[1], 1), 0, 1).astype(jnp.int32)
    expert_ids = different_ones(streams_of[2], TOKENS, EXPERTS, 1, 1024)
    ln1_gain = jnp.clip(1.0 + 0.1 * jax.random.normal(streams_of[3], (D,), jnp.float32), 0.5, 1.5)
    qkv_weight = noise(streams_of[4], (D, 3 * D), D ** -0.5, 0.1875, ((0, 8),))
    out_weight = noise(streams_of[5], (D, D), (D // 16) ** -0.5, 0.75, ((0, 8),))
    ln2_gain = jnp.clip(1.0 + 0.1 * jax.random.normal(streams_of[6], (D,), jnp.float32), 0.5, 1.5)
    up_weight = noise(streams_of[7], (D, FF), D ** -0.5, 0.1875, ((0, 8),))
    down_weight = noise(streams_of[8], (FF, D), (FF // 4) ** -0.5, 0.1875, ((0, 8),))
    mix_weight = noise(streams_of[9], (D, 2), D ** -0.5, 0.1875)
    expert_up = noise(streams_of[10], (EXPERTS, D, FF), D ** -0.5, 0.1875, ((0, 8), (2, 4)))
    expert_down = noise(streams_of[11], (EXPERTS, FF, D), (FF // 4) ** -0.5, 0.1875, ((0, 8), (1, 4)))
    cotangent = noise(streams_of[12], (TOKENS, D), 1.0, 6.0, ((0, 32),))
    return {"tokens": tokens, "bucket": bucket, "expert_ids": expert_ids, "ln1_gain": ln1_gain, "qkv_weight": qkv_weight, "out_weight": out_weight, "ln2_gain": ln2_gain, "up_weight": up_weight, "down_weight": down_weight, "mix_weight": mix_weight, "expert_up": expert_up, "expert_down": expert_down, "cotangent": cotangent}


@jax.custom_vjp
def low(v):
    return lax.optimization_barrier(v.astype(jnp.bfloat16)).astype(jnp.float32)

@jax.custom_vjp
def low_back(v):
    return v

def low_keep(v):
    return (low(v), None)

def low_pass(kept, grad):
    return (grad,)

def back_keep(v):
    return (v, None)

def back_low(kept, grad):
    return (low(grad),)
low.defvjp(low_keep, low_pass)
low_back.defvjp(back_keep, back_low)

def layer_norm(values_in, gain_vec):
    centred = values_in - lax.optimization_barrier(jnp.mean(values_in, axis=-1, keepdims=True))
    inverse = lax.rsqrt(lax.optimization_barrier(jnp.mean(centred * centred, axis=-1, keepdims=True)) + 1e-05)
    return centred * inverse * gain_vec

def sequence_mask(bucket_flag, length):
    position = jnp.arange(length, dtype=jnp.int32)
    sequence = jnp.where(bucket_flag == 1, 0, position // (length // SHORT_SEQS)).astype(jnp.int32)
    same_seq = sequence[:, None] == sequence[None, :]
    return jnp.logical_and(same_seq, position[None, :] <= position[:, None])

def softmax_last(scores):
    row_peak = lax.optimization_barrier(jnp.max(scores, axis=-1, keepdims=True))
    weights = jnp.exp(scores - row_peak)
    return weights / lax.optimization_barrier(jnp.sum(weights, axis=-1, keepdims=True))

def attend_block(packed):
    qkv_rows, bucket_flag = packed
    length = qkv_rows.shape[0]
    query_rows = qkv_rows[:, :D].reshape(length, HEADS, HEAD)
    key_rows = qkv_rows[:, D:2 * D].reshape(length, HEADS, HEAD)
    value_rows = qkv_rows[:, 2 * D:].reshape(length, HEADS, HEAD)
    scores = jnp.einsum('qhd,khd->hqk', query_rows, key_rows, precision=lax.Precision.HIGHEST) * HEAD ** (-0.5)
    scores = low_back(scores)
    scores = jnp.where(sequence_mask(bucket_flag, length)[None], scores, -1e+30)
    prob_low = low(softmax_last(scores))
    mixed_rows = jnp.einsum('hqk,khd->qhd', prob_low, value_rows, precision=lax.Precision.HIGHEST)
    return mixed_rows.reshape(length, D)

def expert_block(packed):
    slot_rows, up_matrix, down_matrix = packed
    pre_act = low_back(jnp.dot(slot_rows, up_matrix, precision=lax.Precision.HIGHEST))
    hidden_act = low(jax.nn.gelu(pre_act))
    return jnp.dot(hidden_act, down_matrix, precision=lax.Precision.HIGHEST)

def forward(token_rows, ln1_gain, qkv_weight, out_weight, ln2_gain, up_weight, down_weight, mix_weight, expert_up, expert_down, bucket, expert_ids):
    total_rows = token_rows.shape[0]
    blocks = total_rows // TOK_DEV
    normed_in = low(layer_norm(token_rows, ln1_gain))
    qkv_all = low_back(low(jnp.dot(normed_in, qkv_weight, precision=lax.Precision.HIGHEST)))
    attended = lax.map(jax.checkpoint(attend_block), (qkv_all.reshape(blocks, TOK_DEV, 3 * D), bucket))
    attended = low_back(low(attended.reshape(total_rows, D)))
    attn_out = low_back(jnp.dot(attended, out_weight, precision=lax.Precision.HIGHEST))
    hidden_res = token_rows + attn_out
    mid_low = low(layer_norm(hidden_res, ln2_gain))
    dense_pre = low_back(jnp.dot(mid_low, up_weight, precision=lax.Precision.HIGHEST))
    dense_act = low(jax.nn.gelu(dense_pre))
    dense_out = low_back(jnp.dot(dense_act, down_weight, precision=lax.Precision.HIGHEST))
    mixing = softmax_last(low_back(jnp.dot(mid_low, mix_weight, precision=lax.Precision.HIGHEST)))
    chosen = expert_ids.reshape(total_rows).astype(jnp.int32)
    one_hot = (chosen.reshape(blocks, TOK_DEV, 1) == jnp.arange(EXPERTS, dtype=jnp.int32)).astype(jnp.int32)
    running = (jnp.cumsum(one_hot, axis=1) - 1).astype(jnp.int32)
    slot_index = lax.optimization_barrier(jnp.sum(one_hot * running, axis=2)).astype(jnp.int32).reshape(total_rows)
    source = (jnp.arange(total_rows, dtype=jnp.int32) // TOK_DEV).astype(jnp.int32)
    dump_row = EXPERTS * blocks * CAP_DEV
    target = jnp.where(slot_index < CAP_DEV, chosen * (blocks * CAP_DEV) + source * CAP_DEV + slot_index, dump_row).astype(jnp.int32)
    buffer_in = jnp.zeros((dump_row + 1, D), jnp.float32).at[target].add(mid_low)
    slot_rows = low_back(buffer_in[:dump_row].reshape(EXPERTS, blocks * CAP_DEV, D))
    returned = lax.map(jax.checkpoint(expert_block), (slot_rows, expert_up, expert_down))
    returned = low_back(low(returned)).reshape(dump_row, D)
    padded = jnp.concatenate([returned, jnp.zeros((1, D), jnp.float32)], axis=0)
    expert_out = padded[target]
    return hidden_res + mixing[:, 0:1] * dense_out + mixing[:, 1:2] * expert_out

def reference(tokens, bucket, expert_ids, ln1_gain, qkv_weight, out_weight, ln2_gain, up_weight, down_weight, mix_weight, expert_up, expert_down, cotangent):
    params = tuple((array_in.astype(jnp.float32) for array_in in (tokens, ln1_gain, qkv_weight, out_weight, ln2_gain, up_weight, down_weight, mix_weight, expert_up, expert_down)))

    def closed(token_rows, gain_first, qkv_mat, out_mat, gain_second, up_mat, down_mat, mix_mat, up_stack, down_stack):
        return forward(token_rows, gain_first, qkv_mat, out_mat, gain_second, up_mat, down_mat, mix_mat, up_stack, down_stack, bucket, expert_ids)
    result, pullback = jax.vjp(closed, *params)
    grads = pullback(cotangent.astype(jnp.float32))
    return (result.astype(jnp.bfloat16), grads[0], grads[1], grads[2], grads[3], grads[4], grads[5], grads[6], grads[7], grads[8], grads[9])
```

```python
import functools

import jax
import jax.numpy as jnp
from jax import lax
from jax.experimental import pallas as pl
from jax.experimental.pallas import tpu as pltpu
from jax.sharding import PartitionSpec as P

HEAD = 64
SHORT_SEQS = 4
PAIR = 2 * HEAD
NEG = -1e30
ROOT = 0.7978845608028654
CUBE = 0.044715
F32 = jnp.float32
BF16 = jnp.bfloat16


def dot_nn(a, b):
    return lax.dot_general(a, b, (((1,), (0,)), ((), ())), preferred_element_type=F32)


def dot_nt(a, b):
    return lax.dot_general(a, b, (((1,), (1,)), ((), ())), preferred_element_type=F32)


def dot_tn(a, b):
    return lax.dot_general(a, b, (((0,), (0,)), ((), ())), preferred_element_type=F32)


def gelu_pair(v):
    sq = v * v
    t = jnp.tanh(v * (ROOT + (ROOT * CUBE) * sq))
    half = 0.5 * (1.0 + t)
    slope = half + (0.5 * v) * (1.0 - t * t) * (ROOT + (3.0 * ROOT * CUBE) * sq)
    return v * half, slope


def params(vmem_mib):
    return pltpu.CompilerParams(vmem_limit_bytes=vmem_mib << 20)


def cost(flops, nbytes):
    return pl.CostEstimate(flops=int(flops), bytes_accessed=int(nbytes), transcendentals=0)


def allowed_block(flag, row0, rows, cols, short):
    r = row0 + lax.broadcasted_iota(jnp.int32, (rows, cols), 0)
    c = lax.broadcasted_iota(jnp.int32, (rows, cols), 1)
    shift = short.bit_length() - 1
    same = jnp.logical_or(flag == 1, lax.shift_right_logical(r, shift) == lax.shift_right_logical(c, shift))
    return jnp.logical_and(c <= r, same)


def attn_fwd_kernel(tile, flag_ref, q_ref, k_ref, v_ref, o_ref, lse_ref):
    length = q_ref.shape[0]
    flag = flag_ref[0]
    lane = lax.broadcasted_iota(jnp.int32, (1, PAIR), 1)
    first = lane < HEAD
    scale = HEAD ** (-0.5)
    for row0 in range(0, length, tile):
        cols = row0 + tile
        ok = allowed_block(flag, row0, tile, cols, length // SHORT_SEQS)
        q = q_ref[row0 : row0 + tile, :]
        k = k_ref[0:cols, :]
        v = v_ref[0:cols, :]
        outs, lses = [], []
        for h in range(2):
            qh = jnp.where(first if h == 0 else jnp.logical_not(first), q, jnp.zeros_like(q))
            s = jnp.where(ok, dot_nt(qh, k) * scale, NEG)
            peak = jnp.max(s, axis=-1, keepdims=True)
            p = jnp.exp(s - peak)
            total = jnp.sum(p, axis=-1, keepdims=True)
            outs.append(dot_nn((p * (1.0 / total)).astype(BF16), v))
            lses.append(peak + jnp.log(total))
        o_ref[row0 : row0 + tile, :] = jnp.where(first, outs[0], outs[1]).astype(BF16)
        lse_ref[row0 : row0 + tile, :] = jnp.where(first, lses[0], lses[1])


def attention_forward(qkv, flag, tile=256):
    length, width = qkv.shape[0], qkv.shape[1] // 3
    pairs = width // PAIR
    spec = lambda off: pl.BlockSpec((length, PAIR), lambda j: (0, off + j))
    return pl.pallas_call(
        functools.partial(attn_fwd_kernel, tile),
        grid=(pairs,),
        in_specs=[pl.BlockSpec(memory_space=pltpu.SMEM), spec(0), spec(pairs), spec(2 * pairs)],
        out_specs=[spec(0), spec(0)],
        out_shape=[jax.ShapeDtypeStruct((length, width), BF16), jax.ShapeDtypeStruct((length, width), F32)],
        compiler_params=params(32),
        cost_estimate=cost(8 * length * length * width, 10 * length * width),
        name="attn_fwd",
    )(flag, qkv, qkv, qkv)


def attn_bwd_kernel(tile, flag_ref, q_ref, k_ref, v_ref, g_ref, lse_ref, o_ref):
    length = q_ref.shape[0]
    width = o_ref.shape[1] // 3
    flag = flag_ref[0]
    lane = lax.broadcasted_iota(jnp.int32, (1, PAIR), 1)
    first = lane < HEAD
    scale = HEAD ** (-0.5)
    starts = list(range(0, length, tile))
    dk = [None] * len(starts)
    dv = [None] * len(starts)
    col = pl.multiple_of(pl.program_id(0) * PAIR, PAIR)
    for i, row0 in enumerate(starts):
        cols = row0 + tile
        ok = allowed_block(flag, row0, tile, cols, length // SHORT_SEQS)
        q = q_ref[row0 : row0 + tile, :]
        g = g_ref[row0 : row0 + tile, :]
        lse = lse_ref[row0 : row0 + tile, :]
        k = k_ref[0:cols, :]
        v = v_ref[0:cols, :]
        dqs, dks, dvs = [], [], []
        for h in range(2):
            mine = first if h == 0 else jnp.logical_not(first)
            qh = jnp.where(mine, q, jnp.zeros_like(q))
            gh = jnp.where(mine, g, jnp.zeros_like(g))
            s = jnp.where(ok, dot_nt(qh, k) * scale, NEG)
            p = jnp.exp(s - lse[:, h * HEAD : h * HEAD + 1])
            dp = dot_nt(gh, v)
            centre = jnp.sum(p * dp, axis=-1, keepdims=True)
            ds = (p * (dp - centre)).astype(BF16)
            dqs.append(dot_nn(ds, k))
            dks.append(dot_tn(ds, qh))
            dvs.append(dot_tn(p.astype(BF16), gh))
        o_ref[row0 : row0 + tile, pl.ds(col, PAIR)] = (
            jnp.where(first, dqs[0], dqs[1]) * scale
        ).astype(BF16)
        dk_all = dks[0] + dks[1]
        dv_all = dvs[0] + dvs[1]
        for j in range(i + 1):
            part_k = dk_all[j * tile : (j + 1) * tile]
            part_v = dv_all[j * tile : (j + 1) * tile]
            dk[j] = part_k if dk[j] is None else dk[j] + part_k
            dv[j] = part_v if dv[j] is None else dv[j] + part_v
    for j, row0 in enumerate(starts):
        o_ref[row0 : row0 + tile, pl.ds(width + col, PAIR)] = (dk[j] * scale).astype(BF16)
        o_ref[row0 : row0 + tile, pl.ds(2 * width + col, PAIR)] = dv[j].astype(BF16)


def attention_backward(qkv, flag, grad, lse, tile=256):
    length, width = qkv.shape[0], qkv.shape[1] // 3
    pairs = width // PAIR
    spec = lambda off: pl.BlockSpec((length, PAIR), lambda j: (0, off + j))
    return pl.pallas_call(
        functools.partial(attn_bwd_kernel, tile),
        grid=(pairs,),
        in_specs=[
            pl.BlockSpec(memory_space=pltpu.SMEM),
            spec(0),
            spec(pairs),
            spec(2 * pairs),
            spec(0),
            spec(0),
        ],
        out_specs=pl.BlockSpec((length, 3 * width), lambda j: (0, 0)),
        out_shape=jax.ShapeDtypeStruct((length, 3 * width), BF16),
        compiler_params=params(40),
        cost_estimate=cost(20 * length * length * width, 20 * length * width),
        name="attn_bwd",
    )(flag, qkv, qkv, qkv, grad, lse)


def dense_kernel(mid_ref, dg_ref, up_ref, down_ref, out_ref, mg_ref, wu_ref, wd_ref):
    mid = mid_ref[...]
    dg = dg_ref[...]
    up = up_ref[...]
    down = down_ref[...]
    act, slope = gelu_pair(dot_nn(mid, up))
    act = act.astype(BF16)
    pg = (dot_nt(dg, down) * slope).astype(BF16)
    out = dot_nn(act, down)
    mg = dot_nt(pg, up)
    wu_ref[...] = dot_tn(mid, pg).astype(BF16)
    wd_ref[...] = dot_tn(act, dg).astype(BF16)

    @pl.when(pl.program_id(0) == 0)
    def _():
        out_ref[...] = out
        mg_ref[...] = mg

    @pl.when(pl.program_id(0) > 0)
    def _():
        out_ref[...] += out
        mg_ref[...] += mg


def dense_branch(mid, dg, up, down, tile=512):
    length, width = mid.shape
    ff = up.shape[1]
    whole = pl.BlockSpec((length, width), lambda j: (0, 0))
    cols = pl.BlockSpec((width, tile), lambda j: (0, j))
    rows = pl.BlockSpec((tile, width), lambda j: (j, 0))
    return pl.pallas_call(
        dense_kernel,
        grid=(ff // tile,),
        in_specs=[whole, whole, cols, rows],
        out_specs=[whole, whole, cols, rows],
        out_shape=[
            jax.ShapeDtypeStruct((length, width), F32),
            jax.ShapeDtypeStruct((length, width), F32),
            jax.ShapeDtypeStruct((width, ff), BF16),
            jax.ShapeDtypeStruct((ff, width), BF16),
        ],
        compiler_params=params(48),
        cost_estimate=cost(12 * length * width * ff, 8 * width * ff + 12 * length * width),
        name="dense_branch",
    )(mid, dg, up, down)


def expert_kernel(mid_ref, g_ref, mix_ref, up_ref, down_ref, po_ref, pi_ref, act_ref, pg_ref, eg_ref, dot_ref):
    mid = mid_ref[...]
    g = g_ref[...].astype(F32)
    logits = dot_nn(mid, mix_ref[...])
    share = 1.0 / (1.0 + jnp.exp(logits[:, 0:1] - logits[:, 1:2]))
    eg = (share * g).astype(BF16)
    eg_ref[...] = eg
    act, slope = gelu_pair(dot_nn(mid, up_ref[...]))
    act = act.astype(BF16)
    act_ref[...] = act
    pg = (dot_nt(eg, down_ref[...]) * slope).astype(BF16)
    pg_ref[...] = pg
    pi_ref[...] = dot_nt(pg, up_ref[...]).astype(BF16)
    po = dot_nn(act, down_ref[...])
    po_ref[...] = po.astype(BF16)
    dot_ref[...] = jnp.sum(po * g, axis=-1, keepdims=True)


def expert_chunk(mid, g, mix_pad, up, down, tile=320):
    rows, width = mid.shape
    hidden = up.shape[1]
    block = pl.BlockSpec((tile, width), lambda i: (i, 0))
    hblock = pl.BlockSpec((tile, hidden), lambda i: (i, 0))
    full = lambda a: pl.BlockSpec(a.shape, lambda i: (0, 0))
    return pl.pallas_call(
        expert_kernel,
        grid=(rows // tile,),
        in_specs=[block, block, full(mix_pad), full(up), full(down)],
        out_specs=[block, block, hblock, hblock, block, pl.BlockSpec((tile, 1), lambda i: (i, 0))],
        out_shape=[
            jax.ShapeDtypeStruct((rows, width), BF16),
            jax.ShapeDtypeStruct((rows, width), BF16),
            jax.ShapeDtypeStruct((rows, hidden), BF16),
            jax.ShapeDtypeStruct((rows, hidden), BF16),
            jax.ShapeDtypeStruct((rows, width), BF16),
            jax.ShapeDtypeStruct((rows, 1), F32),
        ],
        compiler_params=params(48),
        cost_estimate=cost(8 * rows * width * hidden, 14 * rows * width + 4 * width * hidden),
        name="expert_chunk",
    )(mid, g, mix_pad, up, down)


def expert_grad_kernel(count, *refs):
    mids, pgs, acts, egs = (refs[i * count : (i + 1) * count] for i in range(4))
    du_ref, dd_ref = refs[4 * count :]
    up_sum = dot_tn(mids[0][...], pgs[0][...])
    down_sum = dot_tn(acts[0][...], egs[0][...])
    for i in range(1, count):
        up_sum += dot_tn(mids[i][...], pgs[i][...])
        down_sum += dot_tn(acts[i][...], egs[i][...])
    du_ref[...] = up_sum
    dd_ref[...] = down_sum


def expert_weight_grads(mids, pgs, acts, egs, tile=256):
    count = len(mids)
    rows, width = mids[0].shape
    hidden = pgs[0].shape[1]
    full = lambda a: pl.BlockSpec(a.shape, lambda j: (0, 0))
    cols = lambda a: pl.BlockSpec((a.shape[0], tile), lambda j: (0, j))
    return pl.pallas_call(
        functools.partial(expert_grad_kernel, count),
        grid=(hidden // tile,),
        in_specs=[full(a) for a in mids]
        + [cols(a) for a in pgs]
        + [cols(a) for a in acts]
        + [full(a) for a in egs],
        out_specs=[
            pl.BlockSpec((width, tile), lambda j: (0, j)),
            pl.BlockSpec((tile, width), lambda j: (j, 0)),
        ],
        out_shape=[jax.ShapeDtypeStruct((width, hidden), F32), jax.ShapeDtypeStruct((hidden, width), F32)],
        compiler_params=params(48),
        cost_estimate=cost(4 * count * rows * width * hidden, 8 * count * rows * width + 8 * width * hidden),
        name="expert_weight_grads",
    )(*mids, *pgs, *acts, *egs)


def normalise(values_in):
    centred = values_in - jnp.mean(values_in, axis=-1, keepdims=True)
    inverse = lax.rsqrt(jnp.mean(centred * centred, axis=-1, keepdims=True) + 1e-05)
    return centred * inverse, inverse


def norm_backward(grad, gain_vec, unit, inverse):
    m = grad * gain_vec
    return inverse * (
        m
        - jnp.mean(m, axis=-1, keepdims=True)
        - unit * jnp.mean(m * unit, axis=-1, keepdims=True)
    )


def shifted(rows, step):
    size = lax.axis_size("dp")
    return lax.ppermute(rows, "dp", [((i + step) % size, i) for i in range(size)])


def on_device(
    tokens,
    bucket,
    expert_ids,
    ln1_gain,
    qkv_weight,
    out_weight,
    ln2_gain,
    up_weight,
    down_weight,
    mix_weight,
    expert_up,
    expert_down,
    cotangent,
):
    length, width = tokens.shape
    groups = lax.axis_size("ep")
    layers = lax.axis_size("dp")
    experts = groups * expert_up.shape[0]
    capacity = 5 * length // (4 * experts)
    slots = experts * capacity
    gather = lambda w: lax.all_gather(w, "ep", axis=0, tiled=True)
    exchange_out = lambda a: lax.all_to_all(a, "ep", split_axis=0, concat_axis=1, tiled=True)
    qkv_full, out_full, up_full, down_full = (
        gather(qkv_weight),
        gather(out_weight),
        gather(up_weight),
        gather(down_weight),
    )
    expert_up2 = expert_up[0]
    expert_down2 = expert_down[0]
    mix_pad = jnp.pad(mix_weight, ((0, 0), (0, 126)))

    chosen = expert_ids[:, 0]
    one_hot = chosen[:, None] == jnp.arange(experts, dtype=jnp.int32)[None, :]
    place = jnp.arange(length, dtype=jnp.int32)
    earlier = (place[None, :] < place[:, None]).astype(BF16)
    before = dot_nn(earlier, one_hot.astype(BF16))
    slot_index = jnp.sum(jnp.where(one_hot, before, 0.0), axis=1).astype(jnp.int32)
    target = jnp.where(slot_index < capacity, chosen * capacity + slot_index, -1)
    table = (target[:, None] == jnp.arange(slots, dtype=jnp.int32)[None, :]).astype(BF16)

    def dispatch(rows):
        sent = dot_tn(table, rows).astype(BF16)
        return exchange_out(sent.reshape(experts, capacity, width)).reshape(groups * capacity, width)

    g_own = dispatch(cotangent)
    gs = [g_own] + [shifted(g_own, k) for k in range(1, layers)]

    token_rows = tokens.astype(F32)
    unit1, inverse1 = normalise(token_rows)
    normed_in = (unit1 * ln1_gain).astype(BF16)
    qkv_rows = dot_nn(normed_in, qkv_full).astype(BF16)
    attended, lse = attention_forward(qkv_rows, bucket)
    hidden_res = token_rows + dot_nn(attended, out_full)
    unit2, inverse2 = normalise(hidden_res)
    mid_low = (unit2 * ln2_gain).astype(BF16)
    mid_own = dispatch(mid_low)
    mids = [mid_own] + [shifted(mid_own, k) for k in range(1, layers)]

    grad_out = cotangent.astype(F32)
    logits = dot_nn(mid_low, mix_weight)
    mix1 = 1.0 / (1.0 + jnp.exp(logits[:, 0:1] - logits[:, 1:2]))
    mix0 = 1.0 / (1.0 + jnp.exp(logits[:, 1:2] - logits[:, 0:1]))
    dense_grad = (mix0 * grad_out).astype(BF16)
    dense_out, mid_grad_dense, up_grad, down_grad = dense_branch(mid_low, dense_grad, up_full, down_full)

    chunks = [
        expert_chunk(mids[k], gs[k], mix_pad, expert_up2, expert_down2) for k in range(layers)
    ]
    back = lambda k, a: shifted(a, layers - k) if k else a
    ins = [back(k, chunks[k][1]) for k in range(layers)]
    dots = [back(k, chunks[k][5].reshape(groups, capacity)) for k in range(layers)]
    outs = [back(k, chunks[k][0]) for k in range(layers)]
    expert_up_grad, expert_down_grad = expert_weight_grads(
        mids, [c[3] for c in chunks], [c[2] for c in chunks], [c[4] for c in chunks]
    )

    def total(parts):
        acc = parts[0].astype(F32)
        for part in parts[1:]:
            acc = acc + part.astype(F32)
        return acc

    dot_sum = total(dots)
    dot_high = lax.reduce_precision(dot_sum, 8, 7)
    dot_low = dot_sum - dot_high
    extra = jnp.stack([dot_high, dot_low], axis=1)
    extra = jnp.pad(extra, ((0, 0), (0, 14), (0, width - capacity)))
    in_sum = total(ins).reshape(groups, capacity, width)
    packed = jnp.concatenate([in_sum, extra], axis=1).astype(BF16)
    returned = lax.all_to_all(packed, "ep", split_axis=0, concat_axis=0, tiled=True)
    in_rows = returned[:, :capacity].reshape(slots, width)
    dot_back = (
        returned[:, capacity, :capacity].astype(F32) + returned[:, capacity + 1, :capacity].astype(F32)
    ).reshape(1, slots)
    mix_dot1 = jnp.sum(table.astype(F32) * dot_back, axis=1, keepdims=True)
    mix_dot0 = jnp.sum(grad_out * dense_out, axis=-1, keepdims=True)
    mean_dot = mix0 * mix_dot0 + mix1 * mix_dot1
    logit_grad = jnp.concatenate(
        [mix0 * (mix_dot0 - mean_dot), mix1 * (mix_dot1 - mean_dot)], axis=1
    ).astype(BF16)
    mix_weight_grad = dot_tn(mid_low, logit_grad)
    mid_grad = mid_grad_dense + dot_nt(logit_grad, mix_weight) + dot_nn(table, in_rows)
    ln2_gain_grad = jnp.sum(mid_grad * unit2, axis=0)
    res_grad = grad_out + norm_backward(mid_grad, ln2_gain, unit2, inverse2)
    attn_out_grad = res_grad.astype(BF16)
    out_weight_grad = dot_tn(attended, attn_out_grad)
    attended_grad = dot_nt(attn_out_grad, out_full).astype(BF16)
    qkv_grad = attention_backward(qkv_rows, bucket, attended_grad, lse)
    qkv_weight_grad = dot_tn(normed_in, qkv_grad)
    normed_grad = dot_nt(qkv_grad, qkv_full)
    ln1_gain_grad = jnp.sum(normed_grad * unit1, axis=0)
    tokens_grad = res_grad + norm_backward(normed_grad, ln1_gain, unit1, inverse1)

    out_sum = total(outs).astype(BF16).reshape(groups, capacity, width)
    out_back = lax.all_to_all(out_sum, "ep", split_axis=0, concat_axis=0, tiled=True)
    expert_out = dot_nn(table, out_back.reshape(slots, width))
    result = (hidden_res + mix0 * dense_out + mix1 * expert_out).astype(BF16)

    scatter = lambda a: lax.psum_scatter(a.astype(BF16), "ep", scatter_dimension=0, tiled=True)
    merge = lambda a: lax.psum(a, "dp").astype(F32)
    up_shard, down_shard = scatter(up_grad), scatter(down_grad)
    out_shard, qkv_shard = scatter(out_weight_grad), scatter(qkv_weight_grad)
    small_sums = lax.psum((ln1_gain_grad, ln2_gain_grad, mix_weight_grad), ("dp", "ep"))
    return (
        result,
        tokens_grad,
        small_sums[0],
        merge(qkv_shard),
        merge(out_shard),
        small_sums[1],
        merge(up_shard),
        merge(down_shard),
        small_sums[2],
        expert_up_grad[None],
        expert_down_grad[None],
    )


def solution(mesh):
    placed = (
        P(("dp", "ep"), None),
        P(("dp", "ep")),
        P(("dp", "ep"), None),
        P(),
        P("ep", None),
        P("ep", None),
        P(),
        P("ep", None),
        P("ep", None),
        P(),
        P("ep", None, "dp"),
        P("ep", "dp", None),
        P(("dp", "ep"), None),
    )
    return jax.shard_map(
        on_device,
        mesh=mesh,
        in_specs=placed,
        out_specs=(
            P(("dp", "ep"), None),
            P(("dp", "ep"), None),
            P(),
            P("ep", None),
            P("ep", None),
            P(),
            P("ep", None),
            P("ep", None),
            P(),
            P("ep", None, "dp"),
            P("ep", "dp", None),
        ),
        check_vma=False,
    )
```

```python
import functools

import jax
import jax.numpy as jnp
from jax import lax
from jax.experimental import pallas as pl
from jax.experimental.pallas import tpu as pltpu
from jax.sharding import PartitionSpec as P

HEAD = 64
SHORT_SEQS = 4
PAIR = 2 * HEAD
NEG = -1e30
ROOT = 0.7978845608028654
CUBE = 0.044715
F32 = jnp.float32
BF16 = jnp.bfloat16


def dot_nn(a, b):
    return lax.dot_general(a, b, (((1,), (0,)), ((), ())), preferred_element_type=F32)


def dot_nt(a, b):
    return lax.dot_general(a, b, (((1,), (1,)), ((), ())), preferred_element_type=F32)


def dot_tn(a, b):
    return lax.dot_general(a, b, (((0,), (0,)), ((), ())), preferred_element_type=F32)


def gelu_pair(v):
    sq = v * v
    t = jnp.tanh(v * (ROOT + (ROOT * CUBE) * sq))
    half = 0.5 * (1.0 + t)
    slope = half + (0.5 * v) * (1.0 - t * t) * (ROOT + (3.0 * ROOT * CUBE) * sq)
    return v * half, slope


def params(vmem_mib):
    return pltpu.CompilerParams(vmem_limit_bytes=vmem_mib << 20)


def cost(flops, nbytes):
    return pl.CostEstimate(flops=int(flops), bytes_accessed=int(nbytes), transcendentals=0)


def allowed_block(flag, row0, rows, cols, short):
    r = row0 + lax.broadcasted_iota(jnp.int32, (rows, cols), 0)
    c = lax.broadcasted_iota(jnp.int32, (rows, cols), 1)
    shift = short.bit_length() - 1
    same = jnp.logical_or(flag == 1, lax.shift_right_logical(r, shift) == lax.shift_right_logical(c, shift))
    return jnp.logical_and(c <= r, same)


def attn_fwd_kernel(tile, flag_ref, q_ref, k_ref, v_ref, o_ref, lse_ref):
    length = q_ref.shape[0]
    flag = flag_ref[0]
    lane = lax.broadcasted_iota(jnp.int32, (1, PAIR), 1)
    first = lane < HEAD
    scale = HEAD ** (-0.5)
    for row0 in range(0, length, tile):
        cols = row0 + tile
        ok = allowed_block(flag, row0, tile, cols, length // SHORT_SEQS)
        q = q_ref[row0 : row0 + tile, :]
        k = k_ref[0:cols, :]
        v = v_ref[0:cols, :]
        outs, lses = [], []
        for h in range(2):
            qh = jnp.where(first if h == 0 else jnp.logical_not(first), q, jnp.zeros_like(q))
            s = jnp.where(ok, dot_nt(qh, k) * scale, NEG)
            peak = jnp.max(s, axis=-1, keepdims=True)
            p = jnp.exp(s - peak)
            total = jnp.sum(p, axis=-1, keepdims=True)
            outs.append(dot_nn((p * (1.0 / total)).astype(BF16), v))
            lses.append(peak + jnp.log(total))
        o_ref[row0 : row0 + tile, :] = jnp.where(first, outs[0], outs[1]).astype(BF16)
        lse_ref[row0 : row0 + tile, :] = jnp.where(first, lses[0], lses[1])


def attention_forward(qkv, flag, tile=256):
    length, width = qkv.shape[0], qkv.shape[1] // 3
    pairs = width // PAIR
    spec = lambda off: pl.BlockSpec((length, PAIR), lambda j: (0, off + j))
    return pl.pallas_call(
        functools.partial(attn_fwd_kernel, tile),
        grid=(pairs,),
        in_specs=[pl.BlockSpec(memory_space=pltpu.SMEM), spec(0), spec(pairs), spec(2 * pairs)],
        out_specs=[spec(0), spec(0)],
        out_shape=[jax.ShapeDtypeStruct((length, width), BF16), jax.ShapeDtypeStruct((length, width), F32)],
        compiler_params=params(32),
        cost_estimate=cost(8 * length * length * width, 10 * length * width),
        name="attn_fwd",
    )(flag, qkv, qkv, qkv)


def attn_bwd_kernel(tile, flag_ref, q_ref, k_ref, v_ref, g_ref, lse_ref, o_ref):
    length = q_ref.shape[0]
    width = o_ref.shape[1] // 3
    flag = flag_ref[0]
    lane = lax.broadcasted_iota(jnp.int32, (1, PAIR), 1)
    first = lane < HEAD
    scale = HEAD ** (-0.5)
    starts = list(range(0, length, tile))
    dk = [None] * len(starts)
    dv = [None] * len(starts)
    col = pl.multiple_of(pl.program_id(0) * PAIR, PAIR)
    for i, row0 in enumerate(starts):
        cols = row0 + tile
        ok = allowed_block(flag, row0, tile, cols, length // SHORT_SEQS)
        q = q_ref[row0 : row0 + tile, :]
        g = g_ref[row0 : row0 + tile, :]
        lse = lse_ref[row0 : row0 + tile, :]
        k = k_ref[0:cols, :]
        v = v_ref[0:cols, :]
        dqs, dks, dvs = [], [], []
        for h in range(2):
            mine = first if h == 0 else jnp.logical_not(first)
            qh = jnp.where(mine, q, jnp.zeros_like(q))
            gh = jnp.where(mine, g, jnp.zeros_like(g))
            s = jnp.where(ok, dot_nt(qh, k) * scale, NEG)
            p = jnp.exp(s - lse[:, h * HEAD : h * HEAD + 1])
            dp = dot_nt(gh, v)
            centre = jnp.sum(p * dp, axis=-1, keepdims=True)
            ds = (p * (dp - centre)).astype(BF16)
            dqs.append(dot_nn(ds, k))
            dks.append(dot_tn(ds, qh))
            dvs.append(dot_tn(p.astype(BF16), gh))
        o_ref[row0 : row0 + tile, pl.ds(col, PAIR)] = (
            jnp.where(first, dqs[0], dqs[1]) * scale
        ).astype(BF16)
        dk_all = dks[0] + dks[1]
        dv_all = dvs[0] + dvs[1]
        for j in range(i + 1):
            part_k = dk_all[j * tile : (j + 1) * tile]
            part_v = dv_all[j * tile : (j + 1) * tile]
            dk[j] = part_k if dk[j] is None else dk[j] + part_k
            dv[j] = part_v if dv[j] is None else dv[j] + part_v
    for j, row0 in enumerate(starts):
        o_ref[row0 : row0 + tile, pl.ds(width + col, PAIR)] = (dk[j] * scale).astype(BF16)
        o_ref[row0 : row0 + tile, pl.ds(2 * width + col, PAIR)] = dv[j].astype(BF16)


def attention_backward(qkv, flag, grad, lse, tile=256):
    length, width = qkv.shape[0], qkv.shape[1] // 3
    pairs = width // PAIR
    spec = lambda off: pl.BlockSpec((length, PAIR), lambda j: (0, off + j))
    return pl.pallas_call(
        functools.partial(attn_bwd_kernel, tile),
        grid=(pairs,),
        in_specs=[
            pl.BlockSpec(memory_space=pltpu.SMEM),
            spec(0),
            spec(pairs),
            spec(2 * pairs),
            spec(0),
            spec(0),
        ],
        out_specs=pl.BlockSpec((length, 3 * width), lambda j: (0, 0)),
        out_shape=jax.ShapeDtypeStruct((length, 3 * width), BF16),
        compiler_params=params(40),
        cost_estimate=cost(20 * length * length * width, 20 * length * width),
        name="attn_bwd",
    )(flag, qkv, qkv, qkv, grad, lse)


def dense_kernel(mid_ref, dg_ref, up_ref, down_ref, out_ref, mg_ref, wu_ref, wd_ref):
    mid = mid_ref[...]
    dg = dg_ref[...]
    up = up_ref[...]
    down = down_ref[...]
    act, slope = gelu_pair(dot_nn(mid, up))
    act = act.astype(BF16)
    pg = (dot_nt(dg, down) * slope).astype(BF16)
    out = dot_nn(act, down)
    mg = dot_nt(pg, up)
    wu_ref[...] = dot_tn(mid, pg).astype(BF16)
    wd_ref[...] = dot_tn(act, dg).astype(BF16)

    @pl.when(pl.program_id(0) == 0)
    def _():
        out_ref[...] = out
        mg_ref[...] = mg

    @pl.when(pl.program_id(0) > 0)
    def _():
        out_ref[...] += out
        mg_ref[...] += mg


def dense_branch(mid, dg, up, down, tile=512):
    length, width = mid.shape
    ff = up.shape[1]
    whole = pl.BlockSpec((length, width), lambda j: (0, 0))
    cols = pl.BlockSpec((width, tile), lambda j: (0, j))
    rows = pl.BlockSpec((tile, width), lambda j: (j, 0))
    return pl.pallas_call(
        dense_kernel,
        grid=(ff // tile,),
        in_specs=[whole, whole, cols, rows],
        out_specs=[whole, whole, cols, rows],
        out_shape=[
            jax.ShapeDtypeStruct((length, width), F32),
            jax.ShapeDtypeStruct((length, width), F32),
            jax.ShapeDtypeStruct((width, ff), BF16),
            jax.ShapeDtypeStruct((ff, width), BF16),
        ],
        compiler_params=params(48),
        cost_estimate=cost(12 * length * width * ff, 8 * width * ff + 12 * length * width),
        name="dense_branch",
    )(mid, dg, up, down)


def expert_kernel(mid_ref, g_ref, mix_ref, up_ref, down_ref, po_ref, pi_ref, act_ref, pg_ref, eg_ref, dot_ref):
    mid = mid_ref[...]
    g = g_ref[...].astype(F32)
    logits = dot_nn(mid, mix_ref[...])
    share = 1.0 / (1.0 + jnp.exp(logits[:, 0:1] - logits[:, 1:2]))
    eg = (share * g).astype(BF16)
    eg_ref[...] = eg
    act, slope = gelu_pair(dot_nn(mid, up_ref[...]))
    act = act.astype(BF16)
    act_ref[...] = act
    pg = (dot_nt(eg, down_ref[...]) * slope).astype(BF16)
    pg_ref[...] = pg
    pi_ref[...] = dot_nt(pg, up_ref[...]).astype(BF16)
    po = dot_nn(act, down_ref[...])
    po_ref[...] = po.astype(BF16)
    dot_ref[...] = jnp.sum(po * g, axis=-1, keepdims=True)


def expert_chunk(mid, g, mix_pad, up, down, tile=320):
    rows, width = mid.shape
    hidden = up.shape[1]
    block = pl.BlockSpec((tile, width), lambda i: (i, 0))
    hblock = pl.BlockSpec((tile, hidden), lambda i: (i, 0))
    full = lambda a: pl.BlockSpec(a.shape, lambda i: (0, 0))
    return pl.pallas_call(
        expert_kernel,
        grid=(rows // tile,),
        in_specs=[block, block, full(mix_pad), full(up), full(down)],
        out_specs=[block, block, hblock, hblock, block, pl.BlockSpec((tile, 1), lambda i: (i, 0))],
        out_shape=[
            jax.ShapeDtypeStruct((rows, width), BF16),
            jax.ShapeDtypeStruct((rows, width), BF16),
            jax.ShapeDtypeStruct((rows, hidden), BF16),
            jax.ShapeDtypeStruct((rows, hidden), BF16),
            jax.ShapeDtypeStruct((rows, width), BF16),
            jax.ShapeDtypeStruct((rows, 1), F32),
        ],
        compiler_params=params(48),
        cost_estimate=cost(8 * rows * width * hidden, 14 * rows * width + 4 * width * hidden),
        name="expert_chunk",
    )(mid, g, mix_pad, up, down)


def expert_grad_kernel(count, *refs):
    mids, pgs, acts, egs = (refs[i * count : (i + 1) * count] for i in range(4))
    du_ref, dd_ref = refs[4 * count :]
    up_sum = dot_tn(mids[0][...], pgs[0][...])
    down_sum = dot_tn(acts[0][...], egs[0][...])
    for i in range(1, count):
        up_sum += dot_tn(mids[i][...], pgs[i][...])
        down_sum += dot_tn(acts[i][...], egs[i][...])
    du_ref[...] = up_sum
    dd_ref[...] = down_sum


def expert_weight_grads(mids, pgs, acts, egs, tile=256):
    count = len(mids)
    rows, width = mids[0].shape
    hidden = pgs[0].shape[1]
    full = lambda a: pl.BlockSpec(a.shape, lambda j: (0, 0))
    cols = lambda a: pl.BlockSpec((a.shape[0], tile), lambda j: (0, j))
    return pl.pallas_call(
        functools.partial(expert_grad_kernel, count),
        grid=(hidden // tile,),
        in_specs=[full(a) for a in mids]
        + [cols(a) for a in pgs]
        + [cols(a) for a in acts]
        + [full(a) for a in egs],
        out_specs=[
            pl.BlockSpec((width, tile), lambda j: (0, j)),
            pl.BlockSpec((tile, width), lambda j: (j, 0)),
        ],
        out_shape=[jax.ShapeDtypeStruct((width, hidden), F32), jax.ShapeDtypeStruct((hidden, width), F32)],
        compiler_params=params(48),
        cost_estimate=cost(4 * count * rows * width * hidden, 8 * count * rows * width + 8 * width * hidden),
        name="expert_weight_grads",
    )(*mids, *pgs, *acts, *egs)


def normalise(values_in):
    centred = values_in - jnp.mean(values_in, axis=-1, keepdims=True)
    inverse = lax.rsqrt(jnp.mean(centred * centred, axis=-1, keepdims=True) + 1e-05)
    return centred * inverse, inverse


def norm_backward(grad, gain_vec, unit, inverse):
    m = grad * gain_vec
    return inverse * (
        m
        - jnp.mean(m, axis=-1, keepdims=True)
        - unit * jnp.mean(m * unit, axis=-1, keepdims=True)
    )


def hop(rows, step, stage):
    size = lax.axis_size("dp")
    if step > 0:
        pairs = [(i, i + 1) for i in range(stage - 1, size - 1)]
    else:
        pairs = [(i + 1, i) for i in range(0, size - stage)]
    return lax.ppermute(rows, "dp", pairs)


def both_hops(low, high, stage):
    return hop(low, 1, stage), hop(high, -1, stage)


def send_hop(rows, step, stage):
    size = lax.axis_size("dp")
    if step > 0:
        pairs = [(i, i + 1) for i in range(stage)]
    else:
        pairs = [(i, i - 1) for i in range(size - stage, size)]
    return lax.ppermute(rows, "dp", pairs)


def line_reduce(parts, work):
    size = lax.axis_size("dp")
    up = send_hop(parts[size - 1], 1, 1)
    down = send_hop(parts[1], -1, 1)
    for stage in range(2, size):
        if stage - 2 < len(work):
            up, down = after((up, down), work[stage - 2])
        up = send_hop(up + parts[size - stage], 1, stage)
        down = send_hop(down + parts[stage], -1, stage)
    return parts[0].astype(F32) + up.astype(F32) + down.astype(F32)


def shifted(rows, step):
    size = lax.axis_size("dp")
    return lax.ppermute(rows, "dp", [((i + step) % size, i) for i in range(size)])


def after(values, *earlier):
    many = isinstance(values, tuple)
    held = lax.optimization_barrier((*values, *earlier) if many else (values, *earlier))
    return held[: len(values)] if many else held[0]


def sum_layers(rows):
    size, here = lax.axis_size("dp"), lax.axis_index("dp")
    pieces = rows.reshape(size, rows.shape[0] // size, rows.shape[1])
    piece = lambda k: lax.dynamic_index_in_dim(pieces, lax.rem(here + k, size), 0, keepdims=False)
    acc = piece(0).astype(F32)
    for k in range(1, size):
        acc = acc + shifted(piece(k), size - k).astype(F32)
    mine = acc.astype(BF16)
    ring = jnp.stack([mine] + [shifted(mine, k) for k in range(1, size)])
    ordered = lax.dynamic_slice_in_dim(jnp.concatenate([ring, ring]), size - here, size, 0)
    return ordered.reshape(rows.shape).astype(F32)


def sum_everywhere(values):
    for axis in ("dp", "ep"):
        size = lax.axis_size(axis)
        step = 1
        while step < size:
            values = values + lax.ppermute(values, axis, [(i, i ^ step) for i in range(size)])
            step *= 2
    return values


def on_device(
    tokens,
    bucket,
    expert_ids,
    ln1_gain,
    qkv_weight,
    out_weight,
    ln2_gain,
    up_weight,
    down_weight,
    mix_weight,
    expert_up,
    expert_down,
    cotangent,
):
    length, width = tokens.shape
    groups = lax.axis_size("ep")
    layers = lax.axis_size("dp")
    experts = groups * expert_up.shape[0]
    capacity = 5 * length // (4 * experts)
    slots = experts * capacity
    gather = lambda w: lax.all_gather(w, "ep", axis=0, tiled=True)
    exchange_out = lambda a: lax.all_to_all(a, "ep", split_axis=0, concat_axis=1, tiled=True)
    qkv_full, out_full, up_full, down_full = (
        gather(qkv_weight),
        gather(out_weight),
        gather(up_weight),
        gather(down_weight),
    )
    expert_up2 = expert_up[0]
    expert_down2 = expert_down[0]
    mix_pad = jnp.pad(mix_weight, ((0, 0), (0, 126)))

    chosen = expert_ids[:, 0]
    one_hot = chosen[:, None] == jnp.arange(experts, dtype=jnp.int32)[None, :]
    place = jnp.arange(length, dtype=jnp.int32)
    earlier = (place[None, :] < place[:, None]).astype(BF16)
    before = dot_nn(earlier, one_hot.astype(BF16))
    slot_index = jnp.sum(jnp.where(one_hot, before, 0.0), axis=1).astype(jnp.int32)
    target = jnp.where(slot_index < capacity, chosen * capacity + slot_index, -1)
    table = (target[:, None] == jnp.arange(slots, dtype=jnp.int32)[None, :]).astype(BF16)

    pick = lambda rows: dot_tn(table, rows).astype(BF16).reshape(experts, capacity, width)
    join = lambda lows, highs: [highs[k] + lows[layers - k] for k in range(1, layers)]

    token_rows = tokens.astype(F32)
    unit1, inverse1 = normalise(token_rows)
    normed_in = (unit1 * ln1_gain).astype(BF16)
    g_own = exchange_out(pick(cotangent)).reshape(slots, width)
    normed_in, g_own = lax.optimization_barrier((normed_in, g_own))
    g_low, g_high = [g_own], [g_own]
    mid_low_hops, mid_high_hops = [], []

    def step(lows, highs, *others):
        stage = len(lows)
        held = lax.optimization_barrier((lows[-1], highs[-1], *others))
        lows[-1], highs[-1] = held[:2]
        if stage < layers:
            low, high = both_hops(lows[-1], highs[-1], stage)
            lows.append(low)
            highs.append(high)
        return held[2:]

    step(g_low, g_high)
    qkv_rows = dot_nn(normed_in, qkv_full).astype(BF16)
    (qkv_rows,) = step(g_low, g_high, qkv_rows)
    attended, lse = attention_forward(qkv_rows, bucket)
    hidden_res = token_rows + dot_nn(attended, out_full)
    unit2, inverse2 = normalise(hidden_res)
    mid_low = (unit2 * ln2_gain).astype(BF16)
    mid_slots = pick(mid_low)
    (mid_slots,) = step(g_low, g_high, mid_slots)
    mid_own = exchange_out(mid_slots).reshape(slots, width)
    (mid_own,) = step(g_low, g_high, mid_own)
    gs = [g_own] + join(g_low, g_high)
    m_low, m_high = [mid_own], [mid_own]
    step(m_low, m_high)

    chunk = lambda mid, g: expert_chunk(mid, g, mix_pad, expert_up2, expert_down2)
    chunks = {0: chunk(mid_own, g_own)}
    step(m_low, m_high, chunks[0][0])

    grad_out = cotangent.astype(F32)
    logits = dot_nn(mid_low, mix_weight)
    mix1 = 1.0 / (1.0 + jnp.exp(logits[:, 0:1] - logits[:, 1:2]))
    mix0 = 1.0 / (1.0 + jnp.exp(logits[:, 1:2] - logits[:, 0:1]))
    dense_grad = (mix0 * grad_out).astype(BF16)
    while len(m_low) < layers:
        dense_grad, = step(m_low, m_high, dense_grad)
    mids = {0: mid_own}
    middle = layers // 2
    mids[middle] = m_high[middle] + m_low[layers - middle]
    chunks[middle] = chunk(mids[middle], gs[middle])
    for k in [layers - 1] + list(range(1, layers - 1)):
        if k != middle:
            mids[k] = m_high[k] + m_low[layers - k]
            chunks[k] = chunk(mids[k], gs[k])
    mids = [mids[k] for k in range(layers)]
    chunks = [chunks[k] for k in range(layers)]
    back = lambda k, a: shifted(a, layers - k) if k else a
    scatter = lambda a: lax.psum_scatter(a.astype(BF16), "ep", scatter_dimension=0, tiled=True)
    dense_out, mid_grad_dense, up_grad, down_grad = dense_branch(
        mid_low, after(dense_grad, chunks[1][0]), up_full, down_full
    )
    up_shard = scatter(up_grad)
    down_shard = scatter(after(down_grad, chunks[1][0]))
    expert_up_grad, expert_down_grad = expert_weight_grads(
        mids,
        [c[3] for c in chunks],
        [c[2] for c in chunks],
        [after(chunks[0][4], dense_out)] + [c[4] for c in chunks[1:]],
    )
    in_total = line_reduce([c[1] for c in chunks], [dense_out, expert_up_grad])
    dots = [back(k, chunks[k][5].reshape(groups, capacity)) for k in range(layers)]
    outs = [chunks[0][0]] + [back(k, after(chunks[k][0], in_total)) for k in range(1, layers)]
    def total(parts):
        acc = parts[0].astype(F32)
        for part in parts[1:]:
            acc = acc + part.astype(F32)
        return acc

    dot_sum = total(dots)
    dot_high = lax.reduce_precision(dot_sum, 8, 7)
    dot_low = dot_sum - dot_high
    extra = jnp.stack([dot_high, dot_low], axis=1)
    extra = jnp.pad(extra, ((0, 0), (0, 14), (0, width - capacity)))
    in_sum = in_total.reshape(groups, capacity, width)
    packed = jnp.concatenate([in_sum, extra], axis=1).astype(BF16)
    returned = lax.all_to_all(packed, "ep", split_axis=0, concat_axis=0, tiled=True)
    returned, up_shard = lax.optimization_barrier((returned, up_shard))
    in_rows = returned[:, :capacity].reshape(slots, width)
    dot_back = (
        returned[:, capacity, :capacity].astype(F32) + returned[:, capacity + 1, :capacity].astype(F32)
    ).reshape(1, slots)
    mix_dot1 = jnp.sum(table.astype(F32) * dot_back, axis=1, keepdims=True)
    mix_dot0 = jnp.sum(grad_out * dense_out, axis=-1, keepdims=True)
    mean_dot = mix0 * mix_dot0 + mix1 * mix_dot1
    logit_grad = jnp.concatenate(
        [mix0 * (mix_dot0 - mean_dot), mix1 * (mix_dot1 - mean_dot)], axis=1
    ).astype(BF16)
    mix_weight_grad = dot_tn(mid_low, logit_grad)
    mid_grad = mid_grad_dense + dot_nt(logit_grad, mix_weight) + dot_nn(table, in_rows)
    ln2_gain_grad = jnp.sum(mid_grad * unit2, axis=0)
    res_grad = grad_out + norm_backward(mid_grad, ln2_gain, unit2, inverse2)
    attn_out_grad = res_grad.astype(BF16)
    out_weight_grad = dot_tn(attended, attn_out_grad)
    attended_grad = dot_nt(attn_out_grad, out_full).astype(BF16)
    attended_grad, outs[1] = lax.optimization_barrier((attended_grad, outs[1]))
    qkv_grad = attention_backward(qkv_rows, bucket, attended_grad, lse)
    out_shard = scatter(after(out_weight_grad, up_shard))
    qkv_grad, outs[2], down_shard = lax.optimization_barrier((qkv_grad, outs[2], down_shard))
    qkv_weight_grad = dot_tn(normed_in, qkv_grad)
    normed_grad = dot_nt(qkv_grad, qkv_full)
    ln1_gain_grad = jnp.sum(normed_grad * unit1, axis=0)
    tokens_grad = res_grad + norm_backward(normed_grad, ln1_gain, unit1, inverse1)

    up_shard, down_shard, *outs = after((up_shard, down_shard, *outs), qkv_weight_grad)
    out_sum = total(outs).astype(BF16).reshape(groups, capacity, width)
    out_back = lax.all_to_all(out_sum, "ep", split_axis=0, concat_axis=0, tiled=True)
    expert_out = dot_nn(table, out_back.reshape(slots, width))
    result = (hidden_res + mix0 * dense_out + mix1 * expert_out).astype(BF16)

    up_final = sum_layers(up_shard)
    down_final = sum_layers(down_shard)
    out_final = sum_layers(after(out_shard, qkv_weight_grad))
    qkv_final = sum_layers(scatter(qkv_weight_grad))
    small_sums = sum_everywhere(
        jnp.concatenate([ln1_gain_grad[None], ln2_gain_grad[None], mix_weight_grad.T], axis=0)
    )
    return (
        result,
        tokens_grad,
        small_sums[0],
        qkv_final,
        out_final,
        small_sums[1],
        up_final,
        down_final,
        small_sums[2:].T,
        expert_up_grad[None],
        expert_down_grad[None],
    )


def solution(mesh):
    placed = (
        P(("dp", "ep"), None),
        P(("dp", "ep")),
        P(("dp", "ep"), None),
        P(),
        P("ep", None),
        P("ep", None),
        P(),
        P("ep", None),
        P("ep", None),
        P(),
        P("ep", None, "dp"),
        P("ep", "dp", None),
        P(("dp", "ep"), None),
    )
    return jax.shard_map(
        on_device,
        mesh=mesh,
        in_specs=placed,
        out_specs=(
            P(("dp", "ep"), None),
            P(("dp", "ep"), None),
            P(),
            P("ep", None),
            P("ep", None),
            P(),
            P("ep", None),
            P("ep", None),
            P(),
            P("ep", None, "dp"),
            P("ep", "dp", None),
        ),
        check_vma=False,
    )
```

```python
import functools

import jax
import jax.numpy as jnp
from jax import lax
from jax.experimental import pallas as pl
from jax.experimental.pallas import tpu as pltpu
from jax.sharding import PartitionSpec as P

HEAD = 64
SHORT_SEQS = 4
PAIR = 2 * HEAD
NEG = -1e30
ROOT = 0.7978845608028654
CUBE = 0.044715
F32 = jnp.float32
BF16 = jnp.bfloat16


def dot_nn(a, b):
    return lax.dot_general(a, b, (((1,), (0,)), ((), ())), preferred_element_type=F32)


def dot_nt(a, b):
    return lax.dot_general(a, b, (((1,), (1,)), ((), ())), preferred_element_type=F32)


def dot_tn(a, b):
    return lax.dot_general(a, b, (((0,), (0,)), ((), ())), preferred_element_type=F32)


def gelu_pair(v):
    sq = v * v
    t = jnp.tanh(v * (ROOT + (ROOT * CUBE) * sq))
    half = 0.5 * (1.0 + t)
    slope = half + (0.5 * v) * (1.0 - t * t) * (ROOT + (3.0 * ROOT * CUBE) * sq)
    return v * half, slope


def params(vmem_mib):
    return pltpu.CompilerParams(vmem_limit_bytes=vmem_mib << 20)


def cost(flops, nbytes):
    return pl.CostEstimate(flops=int(flops), bytes_accessed=int(nbytes), transcendentals=0)


def allowed_block(flag, row0, rows, cols, short):
    r = row0 + lax.broadcasted_iota(jnp.int32, (rows, cols), 0)
    c = lax.broadcasted_iota(jnp.int32, (rows, cols), 1)
    shift = short.bit_length() - 1
    same = jnp.logical_or(flag == 1, lax.shift_right_logical(r, shift) == lax.shift_right_logical(c, shift))
    return jnp.logical_and(c <= r, same)


def attn_fwd_kernel(tile, flag_ref, q_ref, k_ref, v_ref, o_ref, lse_ref):
    length = q_ref.shape[0]
    flag = flag_ref[0]
    lane = lax.broadcasted_iota(jnp.int32, (1, PAIR), 1)
    first = lane < HEAD
    scale = HEAD ** (-0.5)
    for row0 in range(0, length, tile):
        cols = row0 + tile
        ok = allowed_block(flag, row0, tile, cols, length // SHORT_SEQS)
        q = q_ref[row0 : row0 + tile, :]
        k = k_ref[0:cols, :]
        v = v_ref[0:cols, :]
        outs, lses = [], []
        for h in range(2):
            qh = jnp.where(first if h == 0 else jnp.logical_not(first), q, jnp.zeros_like(q))
            s = jnp.where(ok, dot_nt(qh, k) * scale, NEG)
            peak = jnp.max(s, axis=-1, keepdims=True)
            p = jnp.exp(s - peak)
            total = jnp.sum(p, axis=-1, keepdims=True)
            outs.append(dot_nn((p * (1.0 / total)).astype(BF16), v))
            lses.append(peak + jnp.log(total))
        o_ref[row0 : row0 + tile, :] = jnp.where(first, outs[0], outs[1]).astype(BF16)
        lse_ref[row0 : row0 + tile, :] = jnp.where(first, lses[0], lses[1])


def attention_forward(qkv, flag, tile=256):
    length, width = qkv.shape[0], qkv.shape[1] // 3
    pairs = width // PAIR
    spec = lambda off: pl.BlockSpec((length, PAIR), lambda j: (0, off + j))
    return pl.pallas_call(
        functools.partial(attn_fwd_kernel, tile),
        grid=(pairs,),
        in_specs=[pl.BlockSpec(memory_space=pltpu.SMEM), spec(0), spec(pairs), spec(2 * pairs)],
        out_specs=[spec(0), spec(0)],
        out_shape=[jax.ShapeDtypeStruct((length, width), BF16), jax.ShapeDtypeStruct((length, width), F32)],
        compiler_params=params(32),
        cost_estimate=cost(8 * length * length * width, 10 * length * width),
        name="attn_fwd",
    )(flag, qkv, qkv, qkv)


def attn_bwd_kernel(tile, flag_ref, q_ref, k_ref, v_ref, g_ref, lse_ref, o_ref):
    length = q_ref.shape[0]
    width = o_ref.shape[1] // 3
    flag = flag_ref[0]
    lane = lax.broadcasted_iota(jnp.int32, (1, PAIR), 1)
    first = lane < HEAD
    scale = HEAD ** (-0.5)
    starts = list(range(0, length, tile))
    dk = [None] * len(starts)
    dv = [None] * len(starts)
    col = pl.multiple_of(pl.program_id(0) * PAIR, PAIR)
    for i, row0 in enumerate(starts):
        cols = row0 + tile
        ok = allowed_block(flag, row0, tile, cols, length // SHORT_SEQS)
        q = q_ref[row0 : row0 + tile, :]
        g = g_ref[row0 : row0 + tile, :]
        lse = lse_ref[row0 : row0 + tile, :]
        k = k_ref[0:cols, :]
        v = v_ref[0:cols, :]
        dqs, dks, dvs = [], [], []
        for h in range(2):
            mine = first if h == 0 else jnp.logical_not(first)
            qh = jnp.where(mine, q, jnp.zeros_like(q))
            gh = jnp.where(mine, g, jnp.zeros_like(g))
            s = jnp.where(ok, dot_nt(qh, k) * scale, NEG)
            p = jnp.exp(s - lse[:, h * HEAD : h * HEAD + 1])
            dp = dot_nt(gh, v)
            centre = jnp.sum(p * dp, axis=-1, keepdims=True)
            ds = (p * (dp - centre)).astype(BF16)
            dqs.append(dot_nn(ds, k))
            dks.append(dot_tn(ds, qh))
            dvs.append(dot_tn(p.astype(BF16), gh))
        o_ref[row0 : row0 + tile, pl.ds(col, PAIR)] = (
            jnp.where(first, dqs[0], dqs[1]) * scale
        ).astype(BF16)
        dk_all = dks[0] + dks[1]
        dv_all = dvs[0] + dvs[1]
        for j in range(i + 1):
            part_k = dk_all[j * tile : (j + 1) * tile]
            part_v = dv_all[j * tile : (j + 1) * tile]
            dk[j] = part_k if dk[j] is None else dk[j] + part_k
            dv[j] = part_v if dv[j] is None else dv[j] + part_v
    for j, row0 in enumerate(starts):
        o_ref[row0 : row0 + tile, pl.ds(width + col, PAIR)] = (dk[j] * scale).astype(BF16)
        o_ref[row0 : row0 + tile, pl.ds(2 * width + col, PAIR)] = dv[j].astype(BF16)


def attention_backward(qkv, flag, grad, lse, tile=256):
    length, width = qkv.shape[0], qkv.shape[1] // 3
    pairs = width // PAIR
    spec = lambda off: pl.BlockSpec((length, PAIR), lambda j: (0, off + j))
    return pl.pallas_call(
        functools.partial(attn_bwd_kernel, tile),
        grid=(pairs,),
        in_specs=[
            pl.BlockSpec(memory_space=pltpu.SMEM),
            spec(0),
            spec(pairs),
            spec(2 * pairs),
            spec(0),
            spec(0),
        ],
        out_specs=pl.BlockSpec((length, 3 * width), lambda j: (0, 0)),
        out_shape=jax.ShapeDtypeStruct((length, 3 * width), BF16),
        compiler_params=params(40),
        cost_estimate=cost(20 * length * length * width, 20 * length * width),
        name="attn_bwd",
    )(flag, qkv, qkv, qkv, grad, lse)


def dense_kernel(mid_ref, dg_ref, up_ref, down_ref, out_ref, mg_ref, wu_ref, wd_ref):
    mid = mid_ref[...]
    dg = dg_ref[...]
    up = up_ref[...]
    down = down_ref[...]
    act, slope = gelu_pair(dot_nn(mid, up))
    act = act.astype(BF16)
    pg = (dot_nt(dg, down) * slope).astype(BF16)
    out = dot_nn(act, down)
    mg = dot_nt(pg, up)
    wu_ref[...] = dot_tn(mid, pg).astype(BF16)
    wd_ref[...] = dot_tn(act, dg).astype(BF16)

    @pl.when(pl.program_id(0) == 0)
    def _():
        out_ref[...] = out
        mg_ref[...] = mg

    @pl.when(pl.program_id(0) > 0)
    def _():
        out_ref[...] += out
        mg_ref[...] += mg


def dense_branch(mid, dg, up, down, tile=512):
    length, width = mid.shape
    ff = up.shape[1]
    whole = pl.BlockSpec((length, width), lambda j: (0, 0))
    cols = pl.BlockSpec((width, tile), lambda j: (0, j))
    rows = pl.BlockSpec((tile, width), lambda j: (j, 0))
    return pl.pallas_call(
        dense_kernel,
        grid=(ff // tile,),
        in_specs=[whole, whole, cols, rows],
        out_specs=[whole, whole, cols, rows],
        out_shape=[
            jax.ShapeDtypeStruct((length, width), F32),
            jax.ShapeDtypeStruct((length, width), F32),
            jax.ShapeDtypeStruct((width, ff), BF16),
            jax.ShapeDtypeStruct((ff, width), BF16),
        ],
        compiler_params=params(48),
        cost_estimate=cost(12 * length * width * ff, 8 * width * ff + 12 * length * width),
        name="dense_branch",
    )(mid, dg, up, down)


def expert_kernel(mid_ref, g_ref, mix_ref, up_ref, down_ref, po_ref, pi_ref, act_ref, pg_ref, eg_ref, dot_ref):
    mid = mid_ref[...]
    g = g_ref[...].astype(F32)
    logits = dot_nn(mid, mix_ref[...])
    share = 1.0 / (1.0 + jnp.exp(logits[:, 0:1] - logits[:, 1:2]))
    eg = (share * g).astype(BF16)
    eg_ref[...] = eg
    act, slope = gelu_pair(dot_nn(mid, up_ref[...]))
    act = act.astype(BF16)
    act_ref[...] = act
    pg = (dot_nt(eg, down_ref[...]) * slope).astype(BF16)
    pg_ref[...] = pg
    pi_ref[...] = dot_nt(pg, up_ref[...]).astype(BF16)
    po = dot_nn(act, down_ref[...])
    po_ref[...] = po.astype(BF16)
    dot_ref[...] = jnp.sum(po * g, axis=-1, keepdims=True)


def expert_chunk(mid, g, mix_pad, up, down, tile=320):
    rows, width = mid.shape
    hidden = up.shape[1]
    block = pl.BlockSpec((tile, width), lambda i: (i, 0))
    hblock = pl.BlockSpec((tile, hidden), lambda i: (i, 0))
    full = lambda a: pl.BlockSpec(a.shape, lambda i: (0, 0))
    return pl.pallas_call(
        expert_kernel,
        grid=(rows // tile,),
        in_specs=[block, block, full(mix_pad), full(up), full(down)],
        out_specs=[block, block, hblock, hblock, block, pl.BlockSpec((tile, 1), lambda i: (i, 0))],
        out_shape=[
            jax.ShapeDtypeStruct((rows, width), BF16),
            jax.ShapeDtypeStruct((rows, width), BF16),
            jax.ShapeDtypeStruct((rows, hidden), BF16),
            jax.ShapeDtypeStruct((rows, hidden), BF16),
            jax.ShapeDtypeStruct((rows, width), BF16),
            jax.ShapeDtypeStruct((rows, 1), F32),
        ],
        compiler_params=params(48),
        cost_estimate=cost(8 * rows * width * hidden, 14 * rows * width + 4 * width * hidden),
        name="expert_chunk",
    )(mid, g, mix_pad, up, down)


def expert_grad_kernel(count, *refs):
    mids, pgs, acts, egs = (refs[i * count : (i + 1) * count] for i in range(4))
    du_ref, dd_ref = refs[4 * count :]
    up_sum = dot_tn(mids[0][...], pgs[0][...])
    down_sum = dot_tn(acts[0][...], egs[0][...])
    for i in range(1, count):
        up_sum += dot_tn(mids[i][...], pgs[i][...])
        down_sum += dot_tn(acts[i][...], egs[i][...])
    du_ref[...] = up_sum
    dd_ref[...] = down_sum


def expert_weight_grads(mids, pgs, acts, egs, tile=256):
    count = len(mids)
    rows, width = mids[0].shape
    hidden = pgs[0].shape[1]
    full = lambda a: pl.BlockSpec(a.shape, lambda j: (0, 0))
    cols = lambda a: pl.BlockSpec((a.shape[0], tile), lambda j: (0, j))
    return pl.pallas_call(
        functools.partial(expert_grad_kernel, count),
        grid=(hidden // tile,),
        in_specs=[full(a) for a in mids]
        + [cols(a) for a in pgs]
        + [cols(a) for a in acts]
        + [full(a) for a in egs],
        out_specs=[
            pl.BlockSpec((width, tile), lambda j: (0, j)),
            pl.BlockSpec((tile, width), lambda j: (j, 0)),
        ],
        out_shape=[jax.ShapeDtypeStruct((width, hidden), F32), jax.ShapeDtypeStruct((hidden, width), F32)],
        compiler_params=params(48),
        cost_estimate=cost(4 * count * rows * width * hidden, 8 * count * rows * width + 8 * width * hidden),
        name="expert_weight_grads",
    )(*mids, *pgs, *acts, *egs)


def exchange_kernel(
    waves, layers, groups, slots_ref, *refs
):
    g_refs = refs[:layers]
    mix_ref, up_ref, down_ref, back_ref, slab_ref = refs[layers : layers + 5]
    po_refs = refs[layers + 5 : 2 * layers + 5]
    (
        du_ref, dd_ref, buf, part, got, act_s, pg_s, eg_s, home, home_slab,
        a_send, a_recv, z_send, z_recv, r_send, r_recv, b_send, b_recv,
    ) = refs[2 * layers + 5 :]
    each = groups // waves
    capacity, width = slots_ref.shape[1:]
    rows = each * capacity
    last = layers - 1
    here, me = lax.axis_index("dp"), lax.axis_index("ep")
    up_id, down_id = lax.rem(here + 1, layers), lax.rem(here + last, layers)
    peer = lambda j: lax.rem(me + j, groups)
    source = lambda j: lax.rem(me + groups - j, groups)
    mesh_id = pl.DeviceIdType.MESH

    def a_copy(j):
        return pltpu.make_async_remote_copy(
            slots_ref.at[peer(j)], buf.at[j // each, 0, lax.rem(j, each)],
            a_send.at[j], a_recv.at[j], device_id={"ep": peer(j)}, device_id_type=mesh_id,
        )

    def z_copy(w, way, s):
        src, dst = ((layers - s + 1) % layers, layers - s) if way == 0 else (s - 1, s)
        return pltpu.make_async_remote_copy(
            buf.at[w, src], buf.at[w, dst], z_send.at[w, way, s - 1], z_recv.at[w, way, s - 1],
            device_id={"dp": up_id if way == 0 else down_id}, device_id_type=mesh_id,
        )

    def r_copy(w, way, s):
        return pltpu.make_async_remote_copy(
            part.at[w, layers - s if way == 0 else s], got.at[w, way, s - 1],
            r_send.at[w, way, s - 1], r_recv.at[w, way, s - 1],
            device_id={"dp": up_id if way == 0 else down_id}, device_id_type=mesh_id,
        )

    def b_copies(j):
        w, i = j // each, lax.rem(j, each)
        start = pl.multiple_of(i * capacity, 16)
        return [
            pltpu.make_async_remote_copy(
                src, dst, b_send.at[j, n], b_recv.at[j, n],
                device_id={"ep": source(j)}, device_id_type=mesh_id,
            )
            for n, (src, dst) in enumerate(
                (
                    (part.at[w, 0, pl.ds(start, capacity)], home.at[j]),
                    (part.at[w, 0, pl.ds(rows, 16)], home_slab.at[j]),
                )
            )
        ]

    def z_sends(way, s):
        if way == 0:
            return jnp.logical_and(here <= last - 1, here >= s - 1)
        return jnp.logical_and(here >= 1, here <= layers - s)

    def z_gets(way, s):
        return here >= s if way == 0 else here <= last - s

    def r_sends(way, s):
        return here <= s - 1 if way == 0 else here >= layers - s

    def r_gets(way, s):
        if way == 0:
            return jnp.logical_and(here >= 1, here <= s)
        return jnp.logical_and(here >= last - s, here <= last - 1)

    part[...] = jnp.zeros_like(part)
    got[:, :, last - 1] = jnp.zeros_like(got[:, :, last - 1])
    du_ref[...] = jnp.zeros_like(du_ref)
    dd_ref[...] = jnp.zeros_like(dd_ref)

    barrier = pltpu.get_barrier_semaphore()

    def greet(j, carry):
        pl.semaphore_signal(barrier, inc=1, device_id={"ep": peer(j)}, device_id_type=mesh_id)
        return carry

    lax.fori_loop(1, groups, greet, 0)

    @pl.when(here < last)
    def _():
        pl.semaphore_signal(barrier, inc=1, device_id={"dp": up_id}, device_id_type=mesh_id)

    @pl.when(here > 0)
    def _():
        pl.semaphore_signal(barrier, inc=1, device_id={"dp": down_id}, device_id_type=mesh_id)

    pl.semaphore_wait(barrier, groups - 1 + jnp.where(here < last, 1, 0) + jnp.where(here > 0, 1, 0))

    def over(first, count, act):
        lax.fori_loop(first, count, lambda j, c: (act(j), c)[1], 0)

    over(1, groups, lambda j: a_copy(j).start())
    buf[0, 0, 0] = slots_ref[me]

    def slab_of(row):
        high = row.astype(BF16).astype(F32)
        line = lax.broadcasted_iota(jnp.int32, (16, rows), 0)
        return jnp.where(line == 0, high, jnp.where(line == 1, row - high, 0.0)).astype(BF16)

    def piece(w, ks):
        mid = jnp.concatenate([buf[w, k].reshape(rows, width) for k in ks], axis=0)
        g = jnp.concatenate(
            [g_refs[k][source(w * each + i)] for k in ks for i in range(each)], axis=0
        ).astype(F32)
        logits = dot_nn(mid, mix_ref[...])
        share = 1.0 / (1.0 + jnp.exp(logits[:, 0:1] - logits[:, 1:2]))
        eg = (share * g).astype(BF16)
        act, slope = gelu_pair(dot_nn(mid, up_ref[...]))
        act = act.astype(BF16)
        pg = (dot_nt(eg, down_ref[...]) * slope).astype(BF16)
        pi = dot_nt(pg, up_ref[...]).astype(BF16)
        po = dot_nn(act, down_ref[...])
        sums = jnp.sum(po * g, axis=-1, keepdims=True)
        po = po.astype(BF16)
        diag = lax.broadcasted_iota(jnp.int32, (rows, rows), 0) == lax.broadcasted_iota(
            jnp.int32, (rows, rows), 1
        )
        for n, k in enumerate(ks):
            mine = slice(n * rows, (n + 1) * rows)
            spot = slice(k * rows, (k + 1) * rows)
            eg_s[spot] = eg[mine]
            act_s[spot] = act[mine]
            pg_s[spot] = pg[mine]
            part[w, k, 0:rows] = pi[mine]
            line = jnp.sum(jnp.where(diag, sums[mine], 0.0), axis=0, keepdims=True)
            part[w, k, rows : rows + 16, 0:rows] = slab_of(line)
            for i in range(each):
                at = n * rows + i * capacity
                po_refs[k][source(w * each + i)] = po[at : at + capacity]

    def weight_grads(w):
        mid = buf[w].reshape(layers * rows, width)
        du_ref[...] += dot_tn(mid, pg_s[...])
        dd_ref[...] += dot_tn(act_s[...], eg_s[...])

    def add_to(w, k, pieces):
        total = part[w, k, 0:rows].astype(F32)
        extra = part[w, k, rows : rows + 16, 0:rows].astype(F32)
        for way, s in pieces:
            total = total + got[w, way, s - 1, 0:rows].astype(F32)
            extra = extra + got[w, way, s - 1, rows : rows + 16, 0:rows].astype(F32)
        part[w, k, 0:rows] = total.astype(BF16)
        part[w, k, rows : rows + 16, 0:rows] = slab_of(jnp.sum(extra, axis=0, keepdims=True))

    def start_hop(copy, sends, w, s):
        for way in range(2):
            pl.when(sends(way, s))(lambda way=way: copy(w, way, s).start())

    def get_hop(copy, gets, w, s):
        for way in range(2):
            pl.when(gets(way, s))(lambda way=way: copy(w, way, s).wait_recv())

    def pass_on(w, s):
        for way in range(2):

            @pl.when(r_gets(way, s))
            def _():
                r_copy(w, way, s).wait_recv()
                add_to(w, layers - s - 1 if way == 0 else s + 1, [(way, s)])

        start_hop(r_copy, r_sends, w, s + 1)

    def finish(w):
        get_hop(r_copy, r_gets, w, last)
        add_to(w, 0, [(0, last), (1, last)])
        for i in range(each):
            j = w * each + i
            start = i * capacity

            @pl.when(j > 0)
            def _():
                for copy in b_copies(j):
                    copy.start()

            @pl.when(j == 0)
            def _():
                home[0] = part[0, 0, start : start + capacity]
                home_slab[0] = part[0, 0, rows : rows + 16]

    far = [1, last]
    near = [k for k in range(layers) if k not in far]

    def body(i, carry):
        w = i - 1
        gathers = i < waves
        works = jnp.logical_and(i >= 1, i <= waves)

        @pl.when(gathers)
        def _():
            for n in range(each):
                pl.when(i * each + n > 0)(lambda n=n: a_copy(i * each + n).wait_recv())
            start_hop(z_copy, z_sends, i, 1)

        @pl.when(works)
        def _():
            piece(w, far)
            start_hop(r_copy, r_sends, w, 1)

        @pl.when(i >= 2)
        def _():
            finish(i - 2)

        for s in range(1, last):

            @pl.when(gathers)
            def _():
                get_hop(z_copy, z_gets, i, s)
                start_hop(z_copy, z_sends, i, s + 1)

            @pl.when(works)
            def _():
                if s == 1:
                    piece(w, near)
                if s == last - 1:
                    weight_grads(w)
                pass_on(w, s)

        @pl.when(gathers)
        def _():
            get_hop(z_copy, z_gets, i, last)

        return carry

    lax.fori_loop(0, waves + 2, body, 0)

    def land(j, carry):
        for copy in b_copies(j):
            copy.wait_recv()
            copy.wait_send()
        a_copy(j).wait_send()
        return carry

    lax.fori_loop(1, groups, land, 0)

    def sent(w, carry):
        for way in range(2):
            for s in range(1, layers):
                pl.when(z_sends(way, s))(lambda: z_copy(w, way, s).wait_send())
                pl.when(r_sends(way, s))(lambda: r_copy(w, way, s).wait_send())
        return carry

    lax.fori_loop(0, waves, sent, 0)

    def arrange(j, carry):
        back_ref[peer(j)] = home[j]
        slab_ref[peer(j)] = home_slab[j]
        return carry

    lax.fori_loop(0, groups, arrange, 0)


def exchange_waves(groups):
    return 4 if groups % 4 == 0 else 1


def expert_exchange(slots, gs, mix_pad, up, down):
    layers, groups = lax.axis_size("dp"), lax.axis_size("ep")
    waves = exchange_waves(groups)
    each = groups // waves
    _, capacity, width = slots.shape
    hidden = up.shape[1]
    rows = each * capacity
    sem = pltpu.SemaphoreType.DMA
    block = jax.ShapeDtypeStruct((groups, capacity, width), BF16)
    vmem = pl.BlockSpec(memory_space=pltpu.VMEM)
    total_rows = layers * groups * capacity
    outs = pl.pallas_call(
        functools.partial(exchange_kernel, waves, layers, groups),
        in_specs=[vmem] * (4 + layers),
        out_specs=[vmem] * (4 + layers),
        out_shape=[block, jax.ShapeDtypeStruct((groups, 16, width), BF16)]
        + [block] * layers
        + [jax.ShapeDtypeStruct((width, hidden), F32), jax.ShapeDtypeStruct((hidden, width), F32)],
        scratch_shapes=[
            pltpu.VMEM((waves, layers, each, capacity, width), BF16),
            pltpu.VMEM((waves, layers, rows + 16, width), BF16),
            pltpu.VMEM((waves, 2, layers - 1, rows + 16, width), BF16),
            pltpu.VMEM((layers * rows, hidden), BF16),
            pltpu.VMEM((layers * rows, hidden), BF16),
            pltpu.VMEM((layers * rows, width), BF16),
            pltpu.VMEM((groups, capacity, width), BF16),
            pltpu.VMEM((groups, 16, width), BF16),
            sem((groups,)),
            sem((groups,)),
            sem((waves, 2, layers - 1)),
            sem((waves, 2, layers - 1)),
            sem((waves, 2, layers - 1)),
            sem((waves, 2, layers - 1)),
            sem((groups, 2)),
            sem((groups, 2)),
        ],
        compiler_params=pltpu.CompilerParams(
            collective_id=0, has_side_effects=True, vmem_limit_bytes=62 << 20
        ),
        cost_estimate=cost(12 * total_rows * width * hidden, 20 * total_rows * width),
        name="expert_exchange",
    )(slots, *gs, mix_pad, up, down)
    return outs[0], outs[1], outs[2 : 2 + layers], outs[2 + layers], outs[3 + layers]


def normalise(values_in):
    centred = values_in - jnp.mean(values_in, axis=-1, keepdims=True)
    inverse = lax.rsqrt(jnp.mean(centred * centred, axis=-1, keepdims=True) + 1e-05)
    return centred * inverse, inverse


def norm_backward(grad, gain_vec, unit, inverse):
    m = grad * gain_vec
    return inverse * (
        m
        - jnp.mean(m, axis=-1, keepdims=True)
        - unit * jnp.mean(m * unit, axis=-1, keepdims=True)
    )


def hop(rows, step, stage):
    size = lax.axis_size("dp")
    if step > 0:
        pairs = [(i, i + 1) for i in range(stage - 1, size - 1)]
    else:
        pairs = [(i + 1, i) for i in range(0, size - stage)]
    return lax.ppermute(rows, "dp", pairs)


def both_hops(low, high, stage):
    return hop(low, 1, stage), hop(high, -1, stage)


def send_hop(rows, step, stage):
    size = lax.axis_size("dp")
    if step > 0:
        pairs = [(i, i + 1) for i in range(stage)]
    else:
        pairs = [(i, i - 1) for i in range(size - stage, size)]
    return lax.ppermute(rows, "dp", pairs)


def line_reduce(parts):
    size = lax.axis_size("dp")
    up = send_hop(parts[size - 1], 1, 1)
    down = send_hop(parts[1], -1, 1)
    for stage in range(2, size):
        up = send_hop(up + parts[size - stage], 1, stage)
        down = send_hop(down + parts[stage], -1, stage)
    return parts[0].astype(F32) + up.astype(F32) + down.astype(F32)


def shifted(rows, step):
    size = lax.axis_size("dp")
    return lax.ppermute(rows, "dp", [((i + step) % size, i) for i in range(size)])


def after(values, *earlier):
    many = isinstance(values, tuple)
    held = lax.optimization_barrier((*values, *earlier) if many else (values, *earlier))
    return held[: len(values)] if many else held[0]


def sum_layers(rows):
    size, here = lax.axis_size("dp"), lax.axis_index("dp")
    pieces = rows.reshape(size, rows.shape[0] // size, rows.shape[1])
    piece = lambda k: lax.dynamic_index_in_dim(pieces, lax.rem(here + k, size), 0, keepdims=False)
    acc = piece(0).astype(F32)
    for k in range(1, size):
        acc = acc + shifted(piece(k), size - k).astype(F32)
    mine = acc.astype(BF16)
    ring = jnp.stack([mine] + [shifted(mine, k) for k in range(1, size)])
    ordered = lax.dynamic_slice_in_dim(jnp.concatenate([ring, ring]), size - here, size, 0)
    return ordered.reshape(rows.shape).astype(F32)


def sum_everywhere(values):
    for axis in ("dp", "ep"):
        size = lax.axis_size(axis)
        step = 1
        while step < size:
            values = values + lax.ppermute(values, axis, [(i, i ^ step) for i in range(size)])
            step *= 2
    return values


def on_device(
    tokens,
    bucket,
    expert_ids,
    ln1_gain,
    qkv_weight,
    out_weight,
    ln2_gain,
    up_weight,
    down_weight,
    mix_weight,
    expert_up,
    expert_down,
    cotangent,
):
    length, width = tokens.shape
    groups = lax.axis_size("ep")
    layers = lax.axis_size("dp")
    experts = groups * expert_up.shape[0]
    capacity = 5 * length // (4 * experts)
    slots = experts * capacity
    gather = lambda w: lax.all_gather(w, "ep", axis=0, tiled=True)
    exchange_out = lambda a: lax.all_to_all(a, "ep", split_axis=0, concat_axis=1, tiled=True)
    expert_up2 = expert_up[0]
    expert_down2 = expert_down[0]
    mix_pad = jnp.pad(mix_weight, ((0, 0), (0, 126)))

    chosen = expert_ids[:, 0]
    one_hot = chosen[:, None] == jnp.arange(experts, dtype=jnp.int32)[None, :]
    place = jnp.arange(length, dtype=jnp.int32)
    earlier = (place[None, :] < place[:, None]).astype(BF16)
    before = dot_nn(earlier, one_hot.astype(BF16))
    slot_index = jnp.sum(jnp.where(one_hot, before, 0.0), axis=1).astype(jnp.int32)
    target = jnp.where(slot_index < capacity, chosen * capacity + slot_index, -1)
    table = (target[:, None] == jnp.arange(slots, dtype=jnp.int32)[None, :]).astype(BF16)

    pick = lambda rows: dot_tn(table, rows).astype(BF16).reshape(experts, capacity, width)
    join = lambda lows, highs: [highs[k] + lows[layers - k] for k in range(1, layers)]

    token_rows = tokens.astype(F32)
    unit1, inverse1 = normalise(token_rows)
    normed_in = (unit1 * ln1_gain).astype(BF16)
    g_own = exchange_out(pick(cotangent)).reshape(slots, width)
    normed_in, g_own, qkv_weight = lax.optimization_barrier((normed_in, g_own, qkv_weight))
    qkv_full, out_full, up_full, down_full = (
        gather(qkv_weight),
        gather(out_weight),
        gather(up_weight),
        gather(down_weight),
    )
    g_low, g_high = [g_own], [g_own]

    def step(lows, highs, *others):
        stage = len(lows)
        held = lax.optimization_barrier((lows[-1], highs[-1], *others))
        lows[-1], highs[-1] = held[:2]
        if stage < layers:
            low, high = both_hops(lows[-1], highs[-1], stage)
            lows.append(low)
            highs.append(high)
        return held[2:]

    step(g_low, g_high)
    qkv_rows = dot_nn(normed_in, qkv_full).astype(BF16)
    (qkv_rows,) = step(g_low, g_high, qkv_rows)
    attended, lse = attention_forward(qkv_rows, bucket)
    hidden_res = token_rows + dot_nn(attended, out_full)
    unit2, inverse2 = normalise(hidden_res)
    mid_low = (unit2 * ln2_gain).astype(BF16)
    mid_slots = pick(mid_low)
    (mid_slots,) = step(g_low, g_high, mid_slots)
    step(g_low, g_high)
    gs = [g_own] + join(g_low, g_high)

    grad_out = cotangent.astype(F32)
    logits = dot_nn(mid_low, mix_weight)
    mix1 = 1.0 / (1.0 + jnp.exp(logits[:, 0:1] - logits[:, 1:2]))
    mix0 = 1.0 / (1.0 + jnp.exp(logits[:, 1:2] - logits[:, 0:1]))
    dense_grad = (mix0 * grad_out).astype(BF16)
    scatter = lambda a: lax.psum_scatter(a.astype(BF16), "ep", scatter_dimension=0, tiled=True)
    back = lambda k, a: shifted(a, layers - k) if k else a

    def total(parts):
        acc = parts[0].astype(F32)
        for part in parts[1:]:
            acc = acc + part.astype(F32)
        return acc

    if capacity % 16 == 0:
        blocks = [g.reshape(groups, capacity, width) for g in gs]
        returned, slab, partial_outs, expert_up_grad, expert_down_grad = expert_exchange(
            mid_slots, blocks, mix_pad, expert_up2, expert_down2
        )
        each = groups // exchange_waves(groups)
        offset = lax.rem(
            jnp.arange(groups, dtype=jnp.int32) + groups - lax.axis_index("ep"), groups
        )
        spot = lax.rem(offset, each)[:, None] == jnp.arange(each, dtype=jnp.int32)[None, :]
        lines = slab[:, 0, : each * capacity].astype(F32) + slab[:, 1, : each * capacity].astype(F32)
        dot_back = jnp.sum(
            jnp.where(spot[:, :, None], lines.reshape(groups, each, capacity), 0.0), axis=1
        ).reshape(1, slots)
        dense_grad, returned = lax.optimization_barrier((dense_grad, returned))
        outs = [a.reshape(slots, width) for a in partial_outs]
    else:
        mid_own = exchange_out(mid_slots).reshape(slots, width)
        mids = [mid_own] + [shifted(mid_own, k) for k in range(1, layers)]
        chunks = [expert_chunk(mids[k], gs[k], mix_pad, expert_up2, expert_down2) for k in range(layers)]
        in_total = line_reduce([c[1] for c in chunks])
        dot_sum = total([back(k, chunks[k][5].reshape(groups, capacity)) for k in range(layers)])
        dot_high = lax.reduce_precision(dot_sum, 8, 7)
        extra = jnp.stack([dot_high, dot_sum - dot_high], axis=1)
        extra = jnp.pad(extra, ((0, 0), (0, 14), (0, width - capacity)))
        packed = jnp.concatenate([in_total.reshape(groups, capacity, width), extra], axis=1)
        both = lax.all_to_all(packed.astype(BF16), "ep", split_axis=0, concat_axis=0, tiled=True)
        returned = both[:, :capacity]
        dot_back = (
            both[:, capacity, :capacity].astype(F32) + both[:, capacity + 1, :capacity].astype(F32)
        ).reshape(1, slots)
        outs = [c[0] for c in chunks]
        expert_up_grad, expert_down_grad = expert_weight_grads(
            mids, [c[3] for c in chunks], [c[2] for c in chunks], [c[4] for c in chunks]
        )

    dense_out, mid_grad_dense, up_grad, down_grad = dense_branch(mid_low, dense_grad, up_full, down_full)
    up_shard = scatter(up_grad)
    down_shard = scatter(after(down_grad, up_shard))
    outs = [back(k, outs[k]) for k in range(layers)]
    in_rows = returned.reshape(slots, width)
    mix_dot1 = jnp.sum(table.astype(F32) * dot_back, axis=1, keepdims=True)
    mix_dot0 = jnp.sum(grad_out * dense_out, axis=-1, keepdims=True)
    mean_dot = mix0 * mix_dot0 + mix1 * mix_dot1
    logit_grad = jnp.concatenate(
        [mix0 * (mix_dot0 - mean_dot), mix1 * (mix_dot1 - mean_dot)], axis=1
    ).astype(BF16)
    mix_weight_grad = dot_tn(mid_low, logit_grad)
    mid_grad = mid_grad_dense + dot_nt(logit_grad, mix_weight) + dot_nn(table, in_rows)
    ln2_gain_grad = jnp.sum(mid_grad * unit2, axis=0)
    res_grad = grad_out + norm_backward(mid_grad, ln2_gain, unit2, inverse2)
    attn_out_grad = res_grad.astype(BF16)
    out_weight_grad = dot_tn(attended, attn_out_grad)
    attended_grad = dot_nt(attn_out_grad, out_full).astype(BF16)
    qkv_grad = attention_backward(qkv_rows, bucket, attended_grad, lse)
    out_shard = scatter(after(out_weight_grad, down_shard))
    qkv_grad, up_shard, outs[1] = lax.optimization_barrier((qkv_grad, up_shard, outs[1]))
    qkv_weight_grad = dot_tn(normed_in, qkv_grad)
    normed_grad = dot_nt(qkv_grad, qkv_full)
    ln1_gain_grad = jnp.sum(normed_grad * unit1, axis=0)
    tokens_grad = res_grad + norm_backward(normed_grad, ln1_gain, unit1, inverse1)

    up_shard, down_shard, out_shard, *outs = after(
        (up_shard, down_shard, out_shard, *outs), normed_grad
    )
    out_sum = total(outs).astype(BF16).reshape(groups, capacity, width)
    out_back = lax.all_to_all(out_sum, "ep", split_axis=0, concat_axis=0, tiled=True)
    expert_out = dot_nn(table, out_back.reshape(slots, width))
    result = (hidden_res + mix0 * dense_out + mix1 * expert_out).astype(BF16)

    up_final = sum_layers(up_shard)
    down_final = sum_layers(down_shard)
    out_final = sum_layers(out_shard)
    qkv_final = sum_layers(scatter(after(qkv_weight_grad, out_shard)))
    small_sums = sum_everywhere(
        jnp.concatenate([ln1_gain_grad[None], ln2_gain_grad[None], mix_weight_grad.T], axis=0)
    )
    return (
        result,
        tokens_grad,
        small_sums[0],
        qkv_final,
        out_final,
        small_sums[1],
        up_final,
        down_final,
        small_sums[2:].T,
        expert_up_grad[None],
        expert_down_grad[None],
    )


def solution(mesh):
    placed = (
        P(("dp", "ep"), None),
        P(("dp", "ep")),
        P(("dp", "ep"), None),
        P(),
        P("ep", None),
        P("ep", None),
        P(),
        P("ep", None),
        P("ep", None),
        P(),
        P("ep", None, "dp"),
        P("ep", "dp", None),
        P(("dp", "ep"), None),
    )
    return jax.shard_map(
        on_device,
        mesh=mesh,
        in_specs=placed,
        out_specs=(
            P(("dp", "ep"), None),
            P(("dp", "ep"), None),
            P(),
            P("ep", None),
            P("ep", None),
            P(),
            P("ep", None),
            P("ep", None),
            P(),
            P("ep", None, "dp"),
            P("ep", "dp", None),
        ),
        check_vma=False,
    )
```

```python
import functools

import jax
import jax.numpy as jnp
from jax import lax
from jax.experimental import pallas as pl
from jax.experimental.pallas import tpu as pltpu
from jax.sharding import PartitionSpec as P

HEAD = 64
SHORT_SEQS = 4
PAIR = 2 * HEAD
NEG = -1e30
ROOT = 0.7978845608028654
CUBE = 0.044715
F32 = jnp.float32
BF16 = jnp.bfloat16


def dot_nn(a, b):
    return lax.dot_general(a, b, (((1,), (0,)), ((), ())), preferred_element_type=F32)


def dot_nt(a, b):
    return lax.dot_general(a, b, (((1,), (1,)), ((), ())), preferred_element_type=F32)


def dot_tn(a, b):
    return lax.dot_general(a, b, (((0,), (0,)), ((), ())), preferred_element_type=F32)


def gelu_pair(v):
    sq = v * v
    t = jnp.tanh(v * (ROOT + (ROOT * CUBE) * sq))
    half = 0.5 * (1.0 + t)
    slope = half + (0.5 * v) * (1.0 - t * t) * (ROOT + (3.0 * ROOT * CUBE) * sq)
    return v * half, slope


def params(vmem_mib):
    return pltpu.CompilerParams(vmem_limit_bytes=vmem_mib << 20)


def cost(flops, nbytes):
    return pl.CostEstimate(flops=int(flops), bytes_accessed=int(nbytes), transcendentals=0)


def allowed_block(flag, row0, rows, cols, short):
    r = row0 + lax.broadcasted_iota(jnp.int32, (rows, cols), 0)
    c = lax.broadcasted_iota(jnp.int32, (rows, cols), 1)
    shift = short.bit_length() - 1
    same = jnp.logical_or(flag == 1, lax.shift_right_logical(r, shift) == lax.shift_right_logical(c, shift))
    return jnp.logical_and(c <= r, same)


def attn_fwd_kernel(tile, flag_ref, q_ref, k_ref, v_ref, o_ref, lse_ref):
    length = q_ref.shape[0]
    flag = flag_ref[0]
    lane = lax.broadcasted_iota(jnp.int32, (1, PAIR), 1)
    first = lane < HEAD
    scale = HEAD ** (-0.5)
    for row0 in range(0, length, tile):
        cols = row0 + tile
        ok = allowed_block(flag, row0, tile, cols, length // SHORT_SEQS)
        q = q_ref[row0 : row0 + tile, :]
        k = k_ref[0:cols, :]
        v = v_ref[0:cols, :]
        outs, lses = [], []
        for h in range(2):
            qh = jnp.where(first if h == 0 else jnp.logical_not(first), q, jnp.zeros_like(q))
            s = jnp.where(ok, dot_nt(qh, k) * scale, NEG)
            peak = jnp.max(s, axis=-1, keepdims=True)
            p = jnp.exp(s - peak)
            total = jnp.sum(p, axis=-1, keepdims=True)
            outs.append(dot_nn((p * (1.0 / total)).astype(BF16), v))
            lses.append(peak + jnp.log(total))
        o_ref[row0 : row0 + tile, :] = jnp.where(first, outs[0], outs[1]).astype(BF16)
        lse_ref[row0 : row0 + tile, :] = jnp.where(first, lses[0], lses[1])


def attention_forward(qkv, flag, tile=256):
    length, width = qkv.shape[0], qkv.shape[1] // 3
    pairs = width // PAIR
    spec = lambda off: pl.BlockSpec((length, PAIR), lambda j: (0, off + j))
    return pl.pallas_call(
        functools.partial(attn_fwd_kernel, tile),
        grid=(pairs,),
        in_specs=[pl.BlockSpec(memory_space=pltpu.SMEM), spec(0), spec(pairs), spec(2 * pairs)],
        out_specs=[spec(0), spec(0)],
        out_shape=[jax.ShapeDtypeStruct((length, width), BF16), jax.ShapeDtypeStruct((length, width), F32)],
        compiler_params=params(32),
        cost_estimate=cost(8 * length * length * width, 10 * length * width),
        name="attn_fwd",
    )(flag, qkv, qkv, qkv)


def attn_bwd_kernel(tile, flag_ref, q_ref, k_ref, v_ref, g_ref, lse_ref, o_ref):
    length = q_ref.shape[0]
    width = o_ref.shape[1] // 3
    flag = flag_ref[0]
    lane = lax.broadcasted_iota(jnp.int32, (1, PAIR), 1)
    first = lane < HEAD
    scale = HEAD ** (-0.5)
    starts = list(range(0, length, tile))
    dk = [None] * len(starts)
    dv = [None] * len(starts)
    col = pl.multiple_of(pl.program_id(0) * PAIR, PAIR)
    for i, row0 in enumerate(starts):
        cols = row0 + tile
        ok = allowed_block(flag, row0, tile, cols, length // SHORT_SEQS)
        q = q_ref[row0 : row0 + tile, :]
        g = g_ref[row0 : row0 + tile, :]
        lse = lse_ref[row0 : row0 + tile, :]
        k = k_ref[0:cols, :]
        v = v_ref[0:cols, :]
        dqs, dks, dvs = [], [], []
        for h in range(2):
            mine = first if h == 0 else jnp.logical_not(first)
            qh = jnp.where(mine, q, jnp.zeros_like(q))
            gh = jnp.where(mine, g, jnp.zeros_like(g))
            s = jnp.where(ok, dot_nt(qh, k) * scale, NEG)
            p = jnp.exp(s - lse[:, h * HEAD : h * HEAD + 1])
            dp = dot_nt(gh, v)
            centre = jnp.sum(p * dp, axis=-1, keepdims=True)
            ds = (p * (dp - centre)).astype(BF16)
            dqs.append(dot_nn(ds, k))
            dks.append(dot_tn(ds, qh))
            dvs.append(dot_tn(p.astype(BF16), gh))
        o_ref[row0 : row0 + tile, pl.ds(col, PAIR)] = (
            jnp.where(first, dqs[0], dqs[1]) * scale
        ).astype(BF16)
        dk_all = dks[0] + dks[1]
        dv_all = dvs[0] + dvs[1]
        for j in range(i + 1):
            part_k = dk_all[j * tile : (j + 1) * tile]
            part_v = dv_all[j * tile : (j + 1) * tile]
            dk[j] = part_k if dk[j] is None else dk[j] + part_k
            dv[j] = part_v if dv[j] is None else dv[j] + part_v
    for j, row0 in enumerate(starts):
        o_ref[row0 : row0 + tile, pl.ds(width + col, PAIR)] = (dk[j] * scale).astype(BF16)
        o_ref[row0 : row0 + tile, pl.ds(2 * width + col, PAIR)] = dv[j].astype(BF16)


def attention_backward(qkv, flag, grad, lse, tile=256):
    length, width = qkv.shape[0], qkv.shape[1] // 3
    pairs = width // PAIR
    spec = lambda off: pl.BlockSpec((length, PAIR), lambda j: (0, off + j))
    return pl.pallas_call(
        functools.partial(attn_bwd_kernel, tile),
        grid=(pairs,),
        in_specs=[
            pl.BlockSpec(memory_space=pltpu.SMEM),
            spec(0),
            spec(pairs),
            spec(2 * pairs),
            spec(0),
            spec(0),
        ],
        out_specs=pl.BlockSpec((length, 3 * width), lambda j: (0, 0)),
        out_shape=jax.ShapeDtypeStruct((length, 3 * width), BF16),
        compiler_params=params(40),
        cost_estimate=cost(20 * length * length * width, 20 * length * width),
        name="attn_bwd",
    )(flag, qkv, qkv, qkv, grad, lse)


def dense_kernel(mid_ref, dg_ref, up_ref, down_ref, out_ref, mg_ref, wu_ref, wd_ref):
    mid = mid_ref[...]
    dg = dg_ref[...]
    up = up_ref[...]
    down = down_ref[...]
    act, slope = gelu_pair(dot_nn(mid, up))
    act = act.astype(BF16)
    pg = (dot_nt(dg, down) * slope).astype(BF16)
    out = dot_nn(act, down)
    mg = dot_nt(pg, up)
    wu_ref[...] = dot_tn(mid, pg).astype(BF16)
    wd_ref[...] = dot_tn(act, dg).astype(BF16)

    @pl.when(pl.program_id(0) == 0)
    def _():
        out_ref[...] = out
        mg_ref[...] = mg

    @pl.when(pl.program_id(0) > 0)
    def _():
        out_ref[...] += out
        mg_ref[...] += mg


def dense_branch(mid, dg, up, down, tile=512):
    length, width = mid.shape
    ff = up.shape[1]
    whole = pl.BlockSpec((length, width), lambda j: (0, 0))
    cols = pl.BlockSpec((width, tile), lambda j: (0, j))
    rows = pl.BlockSpec((tile, width), lambda j: (j, 0))
    return pl.pallas_call(
        dense_kernel,
        grid=(ff // tile,),
        in_specs=[whole, whole, cols, rows],
        out_specs=[whole, whole, cols, rows],
        out_shape=[
            jax.ShapeDtypeStruct((length, width), F32),
            jax.ShapeDtypeStruct((length, width), F32),
            jax.ShapeDtypeStruct((width, ff), BF16),
            jax.ShapeDtypeStruct((ff, width), BF16),
        ],
        compiler_params=params(48),
        cost_estimate=cost(length, length),
        name="dense_branch",
    )(mid, dg, up, down)


def expert_kernel(mid_ref, g_ref, mix_ref, up_ref, down_ref, po_ref, pi_ref, act_ref, pg_ref, eg_ref, dot_ref):
    mid = mid_ref[...]
    g = g_ref[...].astype(F32)
    logits = dot_nn(mid, mix_ref[...])
    share = 1.0 / (1.0 + jnp.exp(logits[:, 0:1] - logits[:, 1:2]))
    eg = (share * g).astype(BF16)
    eg_ref[...] = eg
    act, slope = gelu_pair(dot_nn(mid, up_ref[...]))
    act = act.astype(BF16)
    act_ref[...] = act
    pg = (dot_nt(eg, down_ref[...]) * slope).astype(BF16)
    pg_ref[...] = pg
    pi_ref[...] = dot_nt(pg, up_ref[...]).astype(BF16)
    po = dot_nn(act, down_ref[...])
    po_ref[...] = po.astype(BF16)
    dot_ref[...] = jnp.sum(po * g, axis=-1, keepdims=True)


def expert_chunk(mid, g, mix_pad, up, down, tile=320):
    rows, width = mid.shape
    hidden = up.shape[1]
    block = pl.BlockSpec((tile, width), lambda i: (i, 0))
    hblock = pl.BlockSpec((tile, hidden), lambda i: (i, 0))
    full = lambda a: pl.BlockSpec(a.shape, lambda i: (0, 0))
    return pl.pallas_call(
        expert_kernel,
        grid=(rows // tile,),
        in_specs=[block, block, full(mix_pad), full(up), full(down)],
        out_specs=[block, block, hblock, hblock, block, pl.BlockSpec((tile, 1), lambda i: (i, 0))],
        out_shape=[
            jax.ShapeDtypeStruct((rows, width), BF16),
            jax.ShapeDtypeStruct((rows, width), BF16),
            jax.ShapeDtypeStruct((rows, hidden), BF16),
            jax.ShapeDtypeStruct((rows, hidden), BF16),
            jax.ShapeDtypeStruct((rows, width), BF16),
            jax.ShapeDtypeStruct((rows, 1), F32),
        ],
        compiler_params=params(48),
        cost_estimate=cost(8 * rows * width * hidden, 14 * rows * width + 4 * width * hidden),
        name="expert_chunk",
    )(mid, g, mix_pad, up, down)


def expert_grad_kernel(count, *refs):
    mids, pgs, acts, egs = (refs[i * count : (i + 1) * count] for i in range(4))
    du_ref, dd_ref = refs[4 * count :]
    up_sum = dot_tn(mids[0][...], pgs[0][...])
    down_sum = dot_tn(acts[0][...], egs[0][...])
    for i in range(1, count):
        up_sum += dot_tn(mids[i][...], pgs[i][...])
        down_sum += dot_tn(acts[i][...], egs[i][...])
    du_ref[...] = up_sum
    dd_ref[...] = down_sum


def expert_weight_grads(mids, pgs, acts, egs, tile=256):
    count = len(mids)
    rows, width = mids[0].shape
    hidden = pgs[0].shape[1]
    full = lambda a: pl.BlockSpec(a.shape, lambda j: (0, 0))
    cols = lambda a: pl.BlockSpec((a.shape[0], tile), lambda j: (0, j))
    return pl.pallas_call(
        functools.partial(expert_grad_kernel, count),
        grid=(hidden // tile,),
        in_specs=[full(a) for a in mids]
        + [cols(a) for a in pgs]
        + [cols(a) for a in acts]
        + [full(a) for a in egs],
        out_specs=[
            pl.BlockSpec((width, tile), lambda j: (0, j)),
            pl.BlockSpec((tile, width), lambda j: (j, 0)),
        ],
        out_shape=[jax.ShapeDtypeStruct((width, hidden), F32), jax.ShapeDtypeStruct((hidden, width), F32)],
        compiler_params=params(48),
        cost_estimate=cost(4 * count * rows * width * hidden, 8 * count * rows * width + 8 * width * hidden),
        name="expert_weight_grads",
    )(*mids, *pgs, *acts, *egs)


def exchange_kernel(
    waves, layers, groups, slots_ref, *refs
):
    gathered = 2 * layers - 1
    g_low = [refs[0], *refs[1:layers]]
    g_high = [refs[0], *refs[layers:gathered]]
    mix_ref, up_ref, down_ref, back_ref, slab_ref = refs[gathered : gathered + 5]
    po_refs = refs[gathered + 5 : gathered + layers + 5]
    (
        du_ref, dd_ref, g_refs, buf, part, got, act_s, pg_s, eg_s, home, home_slab,
        g_sem, a_send, a_recv, z_send, z_recv, r_send, r_recv, b_send, b_recv,
    ) = refs[gathered + layers + 5 :]
    each = groups // waves
    capacity, width = slots_ref.shape[1:]
    rows = each * capacity
    last = layers - 1
    here, me = lax.axis_index("dp"), lax.axis_index("ep")
    up_id, down_id = lax.rem(here + 1, layers), lax.rem(here + last, layers)
    peer = lambda j: lax.rem(me + j, groups)
    source = lambda j: lax.rem(me + groups - j, groups)
    mesh_id = pl.DeviceIdType.MESH

    def a_copy(j):
        return pltpu.make_async_remote_copy(
            slots_ref.at[peer(j)], buf.at[j // each, 0, lax.rem(j, each)],
            a_send.at[j], a_recv.at[j], device_id={"ep": peer(j)}, device_id_type=mesh_id,
        )

    def z_copy(w, way, s):
        src, dst = ((layers - s + 1) % layers, layers - s) if way == 0 else (s - 1, s)
        return pltpu.make_async_remote_copy(
            buf.at[w, src], buf.at[w, dst], z_send.at[w, way, s - 1], z_recv.at[w, way, s - 1],
            device_id={"dp": up_id if way == 0 else down_id}, device_id_type=mesh_id,
        )

    def r_copy(w, way, s):
        return pltpu.make_async_remote_copy(
            part.at[w, layers - s if way == 0 else s], got.at[w, way, s - 1],
            r_send.at[w, way, s - 1], r_recv.at[w, way, s - 1],
            device_id={"dp": up_id if way == 0 else down_id}, device_id_type=mesh_id,
        )

    def b_copies(j):
        w, i = j // each, lax.rem(j, each)
        start = pl.multiple_of(i * capacity, 16)
        return [
            pltpu.make_async_remote_copy(
                src, dst, b_send.at[j, n], b_recv.at[j, n],
                device_id={"ep": source(j)}, device_id_type=mesh_id,
            )
            for n, (src, dst) in enumerate(
                (
                    (part.at[w, 0, pl.ds(start, capacity)], home.at[j]),
                    (part.at[w, 0, pl.ds(rows, 16)], home_slab.at[j]),
                )
            )
        ]

    def z_sends(way, s):
        if way == 0:
            return jnp.logical_and(here <= last - 1, here >= s - 1)
        return jnp.logical_and(here >= 1, here <= layers - s)

    def z_gets(way, s):
        return here >= s if way == 0 else here <= last - s

    def r_sends(way, s):
        return here <= s - 1 if way == 0 else here >= layers - s

    def r_gets(way, s):
        if way == 0:
            return jnp.logical_and(here >= 1, here <= s)
        return jnp.logical_and(here >= last - s, here <= last - 1)

    def g_copy(ref, k):
        return pltpu.make_async_copy(ref, g_refs.at[k], g_sem.at[k])

    for k in range(layers):
        pl.when(here + k <= last)(lambda k=k: g_copy(g_high[k], k).start())
        if k:
            pl.when(here + k > last)(lambda k=k: g_copy(g_low[layers - k], k).start())

    part[...] = jnp.zeros_like(part)
    got[:, :, last - 1] = jnp.zeros_like(got[:, :, last - 1])
    du_ref[...] = jnp.zeros_like(du_ref)
    dd_ref[...] = jnp.zeros_like(dd_ref)

    barrier = pltpu.get_barrier_semaphore()

    def greet(j, carry):
        pl.semaphore_signal(barrier, inc=1, device_id={"ep": peer(j)}, device_id_type=mesh_id)
        return carry

    lax.fori_loop(1, groups, greet, 0)

    @pl.when(here < last)
    def _():
        pl.semaphore_signal(barrier, inc=1, device_id={"dp": up_id}, device_id_type=mesh_id)

    @pl.when(here > 0)
    def _():
        pl.semaphore_signal(barrier, inc=1, device_id={"dp": down_id}, device_id_type=mesh_id)

    pl.semaphore_wait(barrier, groups - 1 + jnp.where(here < last, 1, 0) + jnp.where(here > 0, 1, 0))

    def over(first, count, act):
        lax.fori_loop(first, count, lambda j, c: (act(j), c)[1], 0)

    over(1, groups, lambda j: a_copy(j).start())
    buf[0, 0, 0] = slots_ref[me]
    for k in range(layers):
        g_copy(g_high[k], k).wait()

    def slab_of(row):
        high = row.astype(BF16).astype(F32)
        line = lax.broadcasted_iota(jnp.int32, (16, rows), 0)
        return jnp.where(line == 0, high, jnp.where(line == 1, row - high, 0.0)).astype(BF16)

    def piece(w, ks):
        mid = jnp.concatenate([buf[w, k].reshape(rows, width) for k in ks], axis=0)
        g = jnp.concatenate(
            [g_refs[k, source(w * each + i)] for k in ks for i in range(each)], axis=0
        ).astype(F32)
        logits = dot_nn(mid, mix_ref[...])
        share = 1.0 / (1.0 + jnp.exp(logits[:, 0:1] - logits[:, 1:2]))
        eg = (share * g).astype(BF16)
        act, slope = gelu_pair(dot_nn(mid, up_ref[...]))
        act = act.astype(BF16)
        pg = (dot_nt(eg, down_ref[...]) * slope).astype(BF16)
        pi = dot_nt(pg, up_ref[...]).astype(BF16)
        po = dot_nn(act, down_ref[...])
        sums = jnp.sum(po * g, axis=-1, keepdims=True)
        po = po.astype(BF16)
        diag = lax.broadcasted_iota(jnp.int32, (rows, rows), 0) == lax.broadcasted_iota(
            jnp.int32, (rows, rows), 1
        )
        for n, k in enumerate(ks):
            mine = slice(n * rows, (n + 1) * rows)
            spot = slice(k * rows, (k + 1) * rows)
            eg_s[spot] = eg[mine]
            act_s[spot] = act[mine]
            pg_s[spot] = pg[mine]
            part[w, k, 0:rows] = pi[mine]
            line = jnp.sum(jnp.where(diag, sums[mine], 0.0), axis=0, keepdims=True)
            part[w, k, rows : rows + 16, 0:rows] = slab_of(line)
            for i in range(each):
                at = n * rows + i * capacity
                po_refs[k][source(w * each + i)] = po[at : at + capacity]

    def weight_grads(w):
        mid = buf[w].reshape(layers * rows, width)
        du_ref[...] += dot_tn(mid, pg_s[...])
        dd_ref[...] += dot_tn(act_s[...], eg_s[...])

    def add_to(w, k, pieces):
        total = part[w, k, 0:rows].astype(F32)
        extra = part[w, k, rows : rows + 16, 0:rows].astype(F32)
        for way, s in pieces:
            total = total + got[w, way, s - 1, 0:rows].astype(F32)
            extra = extra + got[w, way, s - 1, rows : rows + 16, 0:rows].astype(F32)
        part[w, k, 0:rows] = total.astype(BF16)
        part[w, k, rows : rows + 16, 0:rows] = slab_of(jnp.sum(extra, axis=0, keepdims=True))

    def start_hop(copy, sends, w, s):
        for way in range(2):
            pl.when(sends(way, s))(lambda way=way: copy(w, way, s).start())

    def get_hop(copy, gets, w, s):
        for way in range(2):
            pl.when(gets(way, s))(lambda way=way: copy(w, way, s).wait_recv())

    def pass_on(w, s):
        for way in range(2):

            @pl.when(r_gets(way, s))
            def _():
                r_copy(w, way, s).wait_recv()
                add_to(w, layers - s - 1 if way == 0 else s + 1, [(way, s)])

        start_hop(r_copy, r_sends, w, s + 1)

    def finish(w):
        get_hop(r_copy, r_gets, w, last)
        add_to(w, 0, [(0, last), (1, last)])
        for i in range(each):
            j = w * each + i
            start = i * capacity

            @pl.when(j > 0)
            def _():
                for copy in b_copies(j):
                    copy.start()

            @pl.when(j == 0)
            def _():
                home[0] = part[0, 0, start : start + capacity]
                home_slab[0] = part[0, 0, rows : rows + 16]

    far = [1, last]
    near = [k for k in range(layers) if k not in far]

    def body(i, carry):
        w = i - 1
        gathers = i < waves
        works = jnp.logical_and(i >= 1, i <= waves)

        @pl.when(gathers)
        def _():
            for n in range(each):
                pl.when(i * each + n > 0)(lambda n=n: a_copy(i * each + n).wait_recv())
            start_hop(z_copy, z_sends, i, 1)

        @pl.when(works)
        def _():
            piece(w, far)
            start_hop(r_copy, r_sends, w, 1)

        @pl.when(i >= 2)
        def _():
            finish(i - 2)

        for s in range(1, last):

            @pl.when(gathers)
            def _():
                get_hop(z_copy, z_gets, i, s)
                start_hop(z_copy, z_sends, i, s + 1)

            @pl.when(works)
            def _():
                if s == 1:
                    piece(w, near)
                if s == last - 1:
                    weight_grads(w)
                pass_on(w, s)

        @pl.when(gathers)
        def _():
            get_hop(z_copy, z_gets, i, last)

        return carry

    lax.fori_loop(0, waves + 2, body, 0)

    def land(j, carry):
        for copy in b_copies(j):
            copy.wait_recv()
            copy.wait_send()
        a_copy(j).wait_send()
        return carry

    lax.fori_loop(1, groups, land, 0)

    def sent(w, carry):
        for way in range(2):
            for s in range(1, layers):
                pl.when(z_sends(way, s))(lambda: z_copy(w, way, s).wait_send())
                pl.when(r_sends(way, s))(lambda: r_copy(w, way, s).wait_send())
        return carry

    lax.fori_loop(0, waves, sent, 0)

    def arrange(j, carry):
        back_ref[peer(j)] = home[j]
        slab_ref[peer(j)] = home_slab[j]
        return carry

    lax.fori_loop(0, groups, arrange, 0)


def exchange_waves(groups):
    return 4 if groups % 4 == 0 else 1


def expert_exchange(slots, g_low, g_high, mix_pad, up, down):
    layers, groups = lax.axis_size("dp"), lax.axis_size("ep")
    waves = exchange_waves(groups)
    each = groups // waves
    _, capacity, width = slots.shape
    hidden = up.shape[1]
    rows = each * capacity
    sem = pltpu.SemaphoreType.DMA
    block = jax.ShapeDtypeStruct((groups, capacity, width), BF16)
    vmem = pl.BlockSpec(memory_space=pltpu.VMEM)
    total_rows = layers * groups * capacity
    outs = pl.pallas_call(
        functools.partial(exchange_kernel, waves, layers, groups),
        in_specs=[vmem] + [pl.BlockSpec(memory_space=pl.ANY)] * (2 * layers - 1) + [vmem] * 3,
        out_specs=[vmem] * (4 + layers),
        out_shape=[block, jax.ShapeDtypeStruct((groups, 16, width), BF16)]
        + [block] * layers
        + [jax.ShapeDtypeStruct((width, hidden), F32), jax.ShapeDtypeStruct((hidden, width), F32)],
        scratch_shapes=[
            pltpu.VMEM((layers, groups, capacity, width), BF16),
            pltpu.VMEM((waves, layers, each, capacity, width), BF16),
            pltpu.VMEM((waves, layers, rows + 16, width), BF16),
            pltpu.VMEM((waves, 2, layers - 1, rows + 16, width), BF16),
            pltpu.VMEM((layers * rows, hidden), BF16),
            pltpu.VMEM((layers * rows, hidden), BF16),
            pltpu.VMEM((layers * rows, width), BF16),
            pltpu.VMEM((groups, capacity, width), BF16),
            pltpu.VMEM((groups, 16, width), BF16),
            sem((layers,)),
            sem((groups,)),
            sem((groups,)),
            sem((waves, 2, layers - 1)),
            sem((waves, 2, layers - 1)),
            sem((waves, 2, layers - 1)),
            sem((waves, 2, layers - 1)),
            sem((groups, 2)),
            sem((groups, 2)),
        ],
        compiler_params=pltpu.CompilerParams(
            collective_id=0, has_side_effects=True, vmem_limit_bytes=62 << 20
        ),
        cost_estimate=cost(12 * total_rows * width * hidden, 20 * total_rows * width),
        name="expert_exchange",
    )(slots, *g_low, *g_high[1:], mix_pad, up, down)
    return outs[0], outs[1], outs[2 : 2 + layers], outs[2 + layers], outs[3 + layers]


def sums_kernel(plan, layers, groups, small_ref, *refs):
    count = len(plan)
    mats, outs = refs[:count], refs[count : 2 * count]
    (
        small_out, own, sib, got, held, inner, final, wide, small_two, small_chip, small_layer,
        own_sem, s_send, s_recv, x_send, x_recv, z_send, z_recv, t_send, t_recv, o_sem,
    ) = refs[2 * count :]
    chips = groups // 2
    width = held.shape[-1]
    total = held.shape[0]
    last = layers - 1
    here, me = lax.axis_index("dp"), lax.axis_index("ep")
    core, chip = lax.rem(me, 2), me // 2
    sibling = me + 1 - 2 * core
    mesh_id = pl.DeviceIdType.MESH
    chip_at = lambda j: lax.rem(chip + j, chips)
    pieces = [(m, i) for m in range(count) for i in range(plan[m])]
    at_end = jnp.logical_or(here == 0, here == last)
    inside = jnp.logical_and(here > 0, here < last)
    inward = 1 + (here // last) * (last - 2)
    outward = lax.rem((here - 1) * last + layers * last, layers)
    across = last - here

    def source(m, i, half):
        if len(mats[m].shape) == 5:
            return mats[m].at[:, half, i]
        return mats[m].at[:, half, :, pl.ds(i * width, width)]

    def remote(src, dst, send, recv, where):
        return pltpu.make_async_remote_copy(
            src, dst, send, recv, device_id=where, device_id_type=mesh_id
        )

    def s_copy(c):
        return remote(source(*pieces[c], 1 - core), sib.at[c], s_send.at[c], s_recv.at[c], {"ep": sibling})

    def x_copy(c, j):
        return remote(
            own.at[c, chip_at(j)], got.at[c, j - 1], x_send.at[c, j - 1], x_recv.at[c, j - 1],
            {"ep": 2 * chip_at(j) + core},
        )

    def z_copy(c, n):
        src = (held, held, inner)[n]
        dst = (inner, final, final)[n]
        where = (inward, across, outward)[n]
        return remote(src.at[c], dst.at[c], z_send.at[c, n], z_recv.at[c, n], {"dp": where})

    def t_copy(n, j):
        if n == 0:
            return remote(small_ref, small_two, t_send.at[0, 0], t_recv.at[0, 0], {"ep": sibling})
        if n == 1:
            spot = small_chip.at[chip]
            return remote(spot, spot, t_send.at[1, j], t_recv.at[1, j], {"ep": 2 * chip_at(j) + core})
        spot = small_layer.at[here]
        return remote(
            spot, spot, t_send.at[2, j], t_recv.at[2, j], {"dp": lax.rem(here + j, layers)}
        )

    for c in range(total):
        pltpu.make_async_copy(source(*pieces[c], core), own.at[c], own_sem.at[c]).start()

    barrier = pltpu.get_barrier_semaphore()
    pl.semaphore_signal(barrier, inc=1, device_id={"ep": sibling}, device_id_type=mesh_id)

    def over(first, end, act):
        def step(j, carry):
            act(j)
            return carry

        lax.fori_loop(first, end, step, 0)

    over(
        1,
        chips,
        lambda j: pl.semaphore_signal(
            barrier, inc=1, device_id={"ep": 2 * chip_at(j) + core}, device_id_type=mesh_id
        ),
    )
    over(
        1,
        layers,
        lambda j: pl.semaphore_signal(
            barrier, inc=1, device_id={"dp": lax.rem(here + j, layers)}, device_id_type=mesh_id
        ),
    )
    pl.semaphore_wait(barrier, chips + last)

    t_copy(0, 0).start()
    for c in range(total):
        s_copy(c).start()

    def body(t, carry):
        @pl.when(t < total)
        def _():
            pltpu.make_async_copy(sib.at[t], own.at[t], own_sem.at[t]).wait()
            remote(own.at[t], sib.at[t], s_send.at[t], s_recv.at[t], {"ep": sibling}).wait_recv()

            def add(p):
                own[t, p] = own[t, p] + sib[t, p]

            over(0, chips, add)
            over(1, chips, lambda j: x_copy(t, j).start())

        @pl.when(jnp.logical_and(t >= 1, t <= total))
        def _():
            c = t - 1
            over(1, chips, lambda j: x_copy(c, j).wait_recv())
            wide[c] = own[c, chip].astype(F32)

            def add(j):
                wide[c] += got[c, j - 1].astype(F32)

            over(1, chips, add)
            held[c] = wide[c].astype(BF16)
            pl.when(at_end)(lambda: z_copy(c, 0).start())

        @pl.when(jnp.logical_and(inside, jnp.logical_and(t >= 2, t <= total + 1)))
        def _():
            c = t - 2
            z_copy(c, 0).wait_recv()
            held[c] = held[c] + inner[c]
            z_copy(c, 1).start()

        @pl.when(jnp.logical_and(inside, jnp.logical_and(t >= 3, t <= total + 2)))
        def _():
            c = t - 3
            z_copy(c, 1).wait_recv()
            both = held[c] + final[c]
            inner[c] = both
            wide[c] = both.astype(F32)
            z_copy(c, 2).start()

        @pl.when(jnp.logical_and(at_end, t >= 4))
        def _():
            c = t - 4
            z_copy(c, 2).wait_recv()
            wide[c] = final[c].astype(F32)

        @pl.when(t == 1)
        def _():
            t_copy(0, 0).wait_recv()
            small_chip[chip] = small_ref[...] + small_two[...]
            over(1, chips, lambda j: t_copy(1, j).start())

        @pl.when(t == 3)
        def _():
            over(1, chips, lambda j: t_copy(1, j).wait_recv())
            acc = small_chip[0]
            for n in range(1, chips):
                acc = acc + small_chip[n]
            small_layer[here] = acc
            over(1, layers, lambda j: t_copy(2, j).start())

        return carry

    lax.fori_loop(0, total + 4, body, 0)

    copies = []
    for c, (m, i) in enumerate(pieces):
        spot = outs[m].at[i] if len(outs[m].shape) == 3 else outs[m].at[:, pl.ds(i * width, width)]
        copies.append(pltpu.make_async_copy(wide.at[c], spot, o_sem.at[c]))
        copies[-1].start()

    over(1, layers, lambda j: t_copy(2, j).wait_recv())
    acc = small_layer[0]
    for n in range(1, layers):
        acc = acc + small_layer[n]
    small_out[...] = acc

    t_copy(0, 0).wait_send()
    over(1, chips, lambda j: t_copy(1, j).wait_send())
    over(1, layers, lambda j: t_copy(2, j).wait_send())

    def sent(c):
        remote(own.at[c], sib.at[c], s_send.at[c], s_recv.at[c], {"ep": sibling}).wait_send()
        over(1, chips, lambda j: x_copy(c, j).wait_send())
        pl.when(at_end)(lambda: z_copy(c, 0).wait_send())

        @pl.when(inside)
        def _():
            z_copy(c, 1).wait_send()
            z_copy(c, 2).wait_send()

    over(0, total, sent)
    for copy in copies:
        copy.wait()


def gradient_sums(small, columns, rows_split):
    layers, groups = lax.axis_size("dp"), lax.axis_size("ep")
    chips = groups // 2
    width = small.shape[1]
    plan = [a.shape[1] // width for a in columns] + [a.shape[0] // width for a in rows_split]
    high = columns[0].shape[0] // groups
    total = sum(plan)
    views = [a.reshape(chips, 2, high, a.shape[1]) for a in columns] + [
        a.reshape(chips, 2, n, high, width) for a, n in zip(rows_split, plan[len(columns) :])
    ]
    shapes = [jax.ShapeDtypeStruct((high, a.shape[1]), F32) for a in columns] + [
        jax.ShapeDtypeStruct((n, high, width), F32) for n in plan[len(columns) :]
    ]
    sem = pltpu.SemaphoreType.DMA
    vmem = pl.BlockSpec(memory_space=pltpu.VMEM)
    anywhere = pl.BlockSpec(memory_space=pl.ANY)
    buffers = lambda *lead: pltpu.VMEM((total, *lead, high, width), BF16)
    outs = pl.pallas_call(
        functools.partial(sums_kernel, plan, layers, groups),
        in_specs=[vmem] + [anywhere] * len(views),
        out_specs=[anywhere] * len(views) + [vmem],
        out_shape=shapes + [jax.ShapeDtypeStruct(small.shape, F32)],
        scratch_shapes=[
            buffers(chips),
            buffers(chips),
            buffers(chips - 1),
            buffers(),
            buffers(),
            buffers(),
            pltpu.VMEM((total, high, width), F32),
            pltpu.VMEM(small.shape, F32),
            pltpu.VMEM((chips, *small.shape), F32),
            pltpu.VMEM((layers, *small.shape), F32),
            sem((total,)),
            sem((total,)),
            sem((total,)),
            sem((total, chips - 1)),
            sem((total, chips - 1)),
            sem((total, 3)),
            sem((total, 3)),
            sem((3, max(chips, layers))),
            sem((3, max(chips, layers))),
            sem((total,)),
        ],
        compiler_params=pltpu.CompilerParams(
            collective_id=1, has_side_effects=True, vmem_limit_bytes=62 << 20
        ),
        cost_estimate=cost(10 * total * chips * high * width, 8 * total * chips * high * width),
        name="gradient_sums",
    )(small, *views)
    rows_out = [a.reshape(-1, width) for a in outs[len(columns) : -1]]
    return (*outs[: len(columns)], *rows_out, outs[-1])


def normalise(values_in):
    centred = values_in - jnp.mean(values_in, axis=-1, keepdims=True)
    inverse = lax.rsqrt(jnp.mean(centred * centred, axis=-1, keepdims=True) + 1e-05)
    return centred * inverse, inverse


def norm_backward(grad, gain_vec, unit, inverse):
    m = grad * gain_vec
    return inverse * (
        m
        - jnp.mean(m, axis=-1, keepdims=True)
        - unit * jnp.mean(m * unit, axis=-1, keepdims=True)
    )


def hop(rows, step, stage):
    size = lax.axis_size("dp")
    if step > 0:
        pairs = [(i, i + 1) for i in range(stage - 1, size - 1)]
    else:
        pairs = [(i + 1, i) for i in range(0, size - stage)]
    return lax.ppermute(rows, "dp", pairs)


def both_hops(low, high, stage):
    return hop(low, 1, stage), hop(high, -1, stage)


def send_hop(rows, step, stage):
    size = lax.axis_size("dp")
    if step > 0:
        pairs = [(i, i + 1) for i in range(stage)]
    else:
        pairs = [(i, i - 1) for i in range(size - stage, size)]
    return lax.ppermute(rows, "dp", pairs)


def line_reduce(parts):
    size = lax.axis_size("dp")
    up = send_hop(parts[size - 1], 1, 1)
    down = send_hop(parts[1], -1, 1)
    for stage in range(2, size):
        up = send_hop(up + parts[size - stage], 1, stage)
        down = send_hop(down + parts[stage], -1, stage)
    return parts[0].astype(F32) + up.astype(F32) + down.astype(F32)


def shifted(rows, step):
    size = lax.axis_size("dp")
    return lax.ppermute(rows, "dp", [((i + step) % size, i) for i in range(size)])


def after(values, *earlier):
    many = isinstance(values, tuple)
    held = lax.optimization_barrier((*values, *earlier) if many else (values, *earlier))
    return held[: len(values)] if many else held[0]


def sum_layers(rows):
    size, here = lax.axis_size("dp"), lax.axis_index("dp")
    pieces = rows.reshape(size, rows.shape[0] // size, rows.shape[1])
    piece = lambda k: lax.dynamic_index_in_dim(pieces, lax.rem(here + k, size), 0, keepdims=False)
    acc = piece(0).astype(F32)
    for k in range(1, size):
        acc = acc + shifted(piece(k), size - k).astype(F32)
    mine = acc.astype(BF16)
    ring = jnp.stack([mine] + [shifted(mine, k) for k in range(1, size)])
    ordered = lax.dynamic_slice_in_dim(jnp.concatenate([ring, ring]), size - here, size, 0)
    return ordered.reshape(rows.shape).astype(F32)


def sum_everywhere(values):
    for axis in ("dp", "ep"):
        size = lax.axis_size(axis)
        step = 1
        while step < size:
            values = values + lax.ppermute(values, axis, [(i, i ^ step) for i in range(size)])
            step *= 2
    return values


def on_device(
    tokens,
    bucket,
    expert_ids,
    ln1_gain,
    qkv_weight,
    out_weight,
    ln2_gain,
    up_weight,
    down_weight,
    mix_weight,
    expert_up,
    expert_down,
    cotangent,
):
    length, width = tokens.shape
    groups = lax.axis_size("ep")
    layers = lax.axis_size("dp")
    experts = groups * expert_up.shape[0]
    capacity = 5 * length // (4 * experts)
    slots = experts * capacity
    gather = lambda w: lax.all_gather(w, "ep", axis=0, tiled=True)
    exchange_out = lambda a: lax.all_to_all(a, "ep", split_axis=0, concat_axis=1, tiled=True)
    expert_up2 = expert_up[0]
    expert_down2 = expert_down[0]
    mix_pad = jnp.pad(mix_weight, ((0, 0), (0, 126)))

    chosen = expert_ids[:, 0]
    one_hot = chosen[:, None] == jnp.arange(experts, dtype=jnp.int32)[None, :]
    place = jnp.arange(length, dtype=jnp.int32)
    earlier = (place[None, :] < place[:, None]).astype(BF16)
    before = dot_nn(earlier, one_hot.astype(BF16))
    slot_index = jnp.sum(jnp.where(one_hot, before, 0.0), axis=1).astype(jnp.int32)
    target = jnp.where(slot_index < capacity, chosen * capacity + slot_index, -1)
    table = (target[:, None] == jnp.arange(slots, dtype=jnp.int32)[None, :]).astype(BF16)

    pick = lambda rows: dot_tn(table, rows).astype(BF16).reshape(experts, capacity, width)
    join = lambda lows, highs: [highs[k] + lows[layers - k] for k in range(1, layers)]

    token_rows = tokens.astype(F32)
    unit1, inverse1 = normalise(token_rows)
    normed_in = (unit1 * ln1_gain).astype(BF16)
    g_own = exchange_out(pick(cotangent)).reshape(slots, width)
    normed_in, g_own, qkv_weight = lax.optimization_barrier((normed_in, g_own, qkv_weight))
    qkv_full, out_full, up_full, down_full = (
        gather(qkv_weight),
        gather(out_weight),
        gather(up_weight),
        gather(down_weight),
    )
    g_low, g_high = [g_own], [g_own]

    def step(lows, highs, *others):
        stage = len(lows)
        held = lax.optimization_barrier((lows[-1], highs[-1], *others))
        lows[-1], highs[-1] = held[:2]
        if stage < layers:
            low, high = both_hops(lows[-1], highs[-1], stage)
            lows.append(low)
            highs.append(high)
        return held[2:]

    step(g_low, g_high)
    (normed_in,) = step(g_low, g_high, normed_in)
    qkv_rows = dot_nn(normed_in, qkv_full).astype(BF16)
    (qkv_rows,) = step(g_low, g_high, qkv_rows)
    attended, lse = attention_forward(qkv_rows, bucket)
    hidden_res = token_rows + dot_nn(attended, out_full)
    unit2, inverse2 = normalise(hidden_res)
    mid_low = (unit2 * ln2_gain).astype(BF16)
    mid_slots = pick(mid_low)
    (mid_slots,) = step(g_low, g_high, mid_slots)

    grad_out = cotangent.astype(F32)
    logits = dot_nn(mid_low, mix_weight)
    mix1 = 1.0 / (1.0 + jnp.exp(logits[:, 0:1] - logits[:, 1:2]))
    mix0 = 1.0 / (1.0 + jnp.exp(logits[:, 1:2] - logits[:, 0:1]))
    dense_grad = (mix0 * grad_out).astype(BF16)
    scatter = lambda a: lax.psum_scatter(a.astype(BF16), "ep", scatter_dimension=0, tiled=True)
    back = lambda k, a: shifted(a, layers - k) if k else a

    def total(parts):
        acc = parts[0].astype(F32)
        for part in parts[1:]:
            acc = acc + part.astype(F32)
        return acc

    if capacity % 16 == 0:
        blocks = lambda many: [g.reshape(groups, capacity, width) for g in many]
        returned, slab, partial_outs, expert_up_grad, expert_down_grad = expert_exchange(
            mid_slots, blocks(g_low), blocks(g_high), mix_pad, expert_up2, expert_down2
        )
        each = groups // exchange_waves(groups)
        offset = lax.rem(
            jnp.arange(groups, dtype=jnp.int32) + groups - lax.axis_index("ep"), groups
        )
        spot = lax.rem(offset, each)[:, None] == jnp.arange(each, dtype=jnp.int32)[None, :]
        lines = slab[:, 0, : each * capacity].astype(F32) + slab[:, 1, : each * capacity].astype(F32)
        dot_back = jnp.sum(
            jnp.where(spot[:, :, None], lines.reshape(groups, each, capacity), 0.0), axis=1
        ).reshape(1, slots)
        dense_grad, returned = lax.optimization_barrier((dense_grad, returned))
        outs = [a.reshape(slots, width) for a in partial_outs]
    else:
        gs = [g_own] + join(g_low, g_high)
        mid_own = exchange_out(mid_slots).reshape(slots, width)
        mids = [mid_own] + [shifted(mid_own, k) for k in range(1, layers)]
        chunks = [expert_chunk(mids[k], gs[k], mix_pad, expert_up2, expert_down2) for k in range(layers)]
        in_total = line_reduce([c[1] for c in chunks])
        dot_sum = total([back(k, chunks[k][5].reshape(groups, capacity)) for k in range(layers)])
        dot_high = lax.reduce_precision(dot_sum, 8, 7)
        extra = jnp.stack([dot_high, dot_sum - dot_high], axis=1)
        extra = jnp.pad(extra, ((0, 0), (0, 14), (0, width - capacity)))
        packed = jnp.concatenate([in_total.reshape(groups, capacity, width), extra], axis=1)
        both = lax.all_to_all(packed.astype(BF16), "ep", split_axis=0, concat_axis=0, tiled=True)
        returned = both[:, :capacity]
        dot_back = (
            both[:, capacity, :capacity].astype(F32) + both[:, capacity + 1, :capacity].astype(F32)
        ).reshape(1, slots)
        outs = [c[0] for c in chunks]
        expert_up_grad, expert_down_grad = expert_weight_grads(
            mids, [c[3] for c in chunks], [c[2] for c in chunks], [c[4] for c in chunks]
        )

    last = layers - 1
    out_up, out_down = send_hop(outs[last], 1, 1), send_hop(outs[1], -1, 1)
    dense_out, mid_grad_dense, up_grad, down_grad = dense_branch(mid_low, dense_grad, up_full, down_full)

    def out_step(stage, *others):
        held = lax.optimization_barrier((out_up, out_down, *others))
        return (
            send_hop(held[0] + outs[layers - stage], 1, stage),
            send_hop(held[1] + outs[stage], -1, stage),
            *held[2:],
        )

    out_up, out_down, dense_out = out_step(2, dense_out)
    in_rows = returned.reshape(slots, width)
    mix_dot1 = jnp.sum(table.astype(F32) * dot_back, axis=1, keepdims=True)
    mix_dot0 = jnp.sum(grad_out * dense_out, axis=-1, keepdims=True)
    mean_dot = mix0 * mix_dot0 + mix1 * mix_dot1
    logit_grad = jnp.concatenate(
        [mix0 * (mix_dot0 - mean_dot), mix1 * (mix_dot1 - mean_dot)], axis=1
    ).astype(BF16)
    mix_weight_grad = dot_tn(mid_low, logit_grad)
    mid_grad = mid_grad_dense + dot_nt(logit_grad, mix_weight) + dot_nn(table, in_rows)
    ln2_gain_grad = jnp.sum(mid_grad * unit2, axis=0)
    res_grad = grad_out + norm_backward(mid_grad, ln2_gain, unit2, inverse2)
    attn_out_grad = res_grad.astype(BF16)
    out_weight_grad = dot_tn(attended, attn_out_grad)
    attended_grad = dot_nt(attn_out_grad, out_full).astype(BF16)
    for stage in range(3, layers):
        out_up, out_down, attended_grad = out_step(stage, attended_grad)
    qkv_grad = attention_backward(qkv_rows, bucket, attended_grad, lse)
    out_up, out_down, qkv_grad = lax.optimization_barrier((out_up, out_down, qkv_grad))
    qkv_weight_grad = dot_tn(normed_in, qkv_grad)
    normed_grad = dot_nt(qkv_grad, qkv_full)
    ln1_gain_grad = jnp.sum(normed_grad * unit1, axis=0)
    tokens_grad = res_grad + norm_backward(normed_grad, ln1_gain, unit1, inverse1)

    out_sum = total([outs[0], out_up, out_down]).astype(BF16).reshape(groups, capacity, width)
    out_back = lax.all_to_all(out_sum, "ep", split_axis=0, concat_axis=0, tiled=True)
    expert_out = dot_nn(table, out_back.reshape(slots, width))
    result = (hidden_res + mix0 * dense_out + mix1 * expert_out).astype(BF16)

    ln1_gain_grad, result = lax.optimization_barrier((ln1_gain_grad, result))
    small = jnp.concatenate([ln1_gain_grad[None], ln2_gain_grad[None], mix_weight_grad.T], axis=0)
    small = jnp.pad(small, ((0, 4), (0, 0)))
    if layers == 4 and length // groups >= 16:
        qkv_final, out_final, up_final, down_final, small_sums = gradient_sums(
            small,
            [a.astype(BF16) for a in (qkv_weight_grad, out_weight_grad, up_grad)],
            [down_grad],
        )
    else:
        sums = [sum_layers(scatter(a)) for a in (qkv_weight_grad, out_weight_grad, up_grad, down_grad)]
        qkv_final, out_final, up_final, down_final = sums
        small_sums = sum_everywhere(small)
    return (
        result,
        tokens_grad,
        small_sums[0],
        qkv_final,
        out_final,
        small_sums[1],
        up_final,
        down_final,
        small_sums[2:4].T,
        expert_up_grad[None],
        expert_down_grad[None],
    )


def solution(mesh):
    placed = (
        P(("dp", "ep"), None),
        P(("dp", "ep")),
        P(("dp", "ep"), None),
        P(),
        P("ep", None),
        P("ep", None),
        P(),
        P("ep", None),
        P("ep", None),
        P(),
        P("ep", None, "dp"),
        P("ep", "dp", None),
        P(("dp", "ep"), None),
    )
    return jax.shard_map(
        on_device,
        mesh=mesh,
        in_specs=placed,
        out_specs=(
            P(("dp", "ep"), None),
            P(("dp", "ep"), None),
            P(),
            P("ep", None),
            P("ep", None),
            P(),
            P("ep", None),
            P("ep", None),
            P(),
            P("ep", None, "dp"),
            P("ep", "dp", None),
        ),
        check_vma=False,
    )
```

```python
import functools

import jax
import jax.numpy as jnp
from jax import lax
from jax.experimental import pallas as pl
from jax.experimental.pallas import tpu as pltpu
from jax.sharding import PartitionSpec as P

HEAD = 64
SHORT_SEQS = 4
PAIR = 2 * HEAD
NEG = -1e30
SPLIT = 2
LAG = 2
ROOT = 0.7978845608028654
CUBE = 0.044715
F32 = jnp.float32
BF16 = jnp.bfloat16


def dot_nn(a, b):
    return lax.dot_general(a, b, (((1,), (0,)), ((), ())), preferred_element_type=F32)


def dot_nt(a, b):
    return lax.dot_general(a, b, (((1,), (1,)), ((), ())), preferred_element_type=F32)


def dot_tn(a, b):
    return lax.dot_general(a, b, (((0,), (0,)), ((), ())), preferred_element_type=F32)


def gelu_pair(v):
    sq = v * v
    t = jnp.tanh(v * (ROOT + (ROOT * CUBE) * sq))
    half = 0.5 * (1.0 + t)
    slope = half + (0.5 * v) * (1.0 - t * t) * (ROOT + (3.0 * ROOT * CUBE) * sq)
    return v * half, slope


def params(vmem_mib):
    return pltpu.CompilerParams(vmem_limit_bytes=vmem_mib << 20)


def cost(flops, nbytes):
    return pl.CostEstimate(flops=int(flops), bytes_accessed=int(nbytes), transcendentals=0)


def allowed_block(flag, row0, rows, cols, short):
    r = row0 + lax.broadcasted_iota(jnp.int32, (rows, cols), 0)
    c = lax.broadcasted_iota(jnp.int32, (rows, cols), 1)
    shift = short.bit_length() - 1
    same = jnp.logical_or(flag == 1, lax.shift_right_logical(r, shift) == lax.shift_right_logical(c, shift))
    return jnp.logical_and(c <= r, same)


def attn_fwd_kernel(tile, flag_ref, q_ref, k_ref, v_ref, o_ref, lse_ref):
    length = q_ref.shape[0]
    flag = flag_ref[0]
    lane = lax.broadcasted_iota(jnp.int32, (1, PAIR), 1)
    first = lane < HEAD
    scale = HEAD ** (-0.5)
    for row0 in range(0, length, tile):
        cols = row0 + tile
        ok = allowed_block(flag, row0, tile, cols, length // SHORT_SEQS)
        q = q_ref[row0 : row0 + tile, :]
        k = k_ref[0:cols, :]
        v = v_ref[0:cols, :]
        outs, lses = [], []
        for h in range(2):
            qh = jnp.where(first if h == 0 else jnp.logical_not(first), q, jnp.zeros_like(q))
            s = jnp.where(ok, dot_nt(qh, k) * scale, NEG)
            peak = jnp.max(s, axis=-1, keepdims=True)
            p = jnp.exp(s - peak)
            total = jnp.sum(p, axis=-1, keepdims=True)
            outs.append(dot_nn((p * (1.0 / total)).astype(BF16), v))
            lses.append(peak + jnp.log(total))
        o_ref[row0 : row0 + tile, :] = jnp.where(first, outs[0], outs[1]).astype(BF16)
        lse_ref[row0 : row0 + tile, :] = jnp.where(first, lses[0], lses[1])


def attention_forward(qkv, flag, tile=256):
    length, width = qkv.shape[0], qkv.shape[1] // 3
    pairs = width // PAIR
    spec = lambda off: pl.BlockSpec((length, PAIR), lambda j: (0, off + j))
    return pl.pallas_call(
        functools.partial(attn_fwd_kernel, tile),
        grid=(pairs,),
        in_specs=[pl.BlockSpec(memory_space=pltpu.SMEM), spec(0), spec(pairs), spec(2 * pairs)],
        out_specs=[spec(0), spec(0)],
        out_shape=[jax.ShapeDtypeStruct((length, width), BF16), jax.ShapeDtypeStruct((length, width), F32)],
        compiler_params=params(32),
        cost_estimate=cost(8 * length * length * width, 10 * length * width),
        name="attn_fwd",
    )(flag, qkv, qkv, qkv)


def attn_bwd_kernel(tile, flag_ref, q_ref, k_ref, v_ref, g_ref, lse_ref, o_ref):
    length = q_ref.shape[0]
    width = o_ref.shape[1] // 3
    flag = flag_ref[0]
    lane = lax.broadcasted_iota(jnp.int32, (1, PAIR), 1)
    first = lane < HEAD
    scale = HEAD ** (-0.5)
    starts = list(range(0, length, tile))
    dk = [None] * len(starts)
    dv = [None] * len(starts)
    col = pl.multiple_of(pl.program_id(0) * PAIR, PAIR)
    for i, row0 in enumerate(starts):
        cols = row0 + tile
        ok = allowed_block(flag, row0, tile, cols, length // SHORT_SEQS)
        q = q_ref[row0 : row0 + tile, :]
        g = g_ref[row0 : row0 + tile, :]
        lse = lse_ref[row0 : row0 + tile, :]
        k = k_ref[0:cols, :]
        v = v_ref[0:cols, :]
        dqs, dks, dvs = [], [], []
        for h in range(2):
            mine = first if h == 0 else jnp.logical_not(first)
            qh = jnp.where(mine, q, jnp.zeros_like(q))
            gh = jnp.where(mine, g, jnp.zeros_like(g))
            s = jnp.where(ok, dot_nt(qh, k) * scale, NEG)
            p = jnp.exp(s - lse[:, h * HEAD : h * HEAD + 1])
            dp = dot_nt(gh, v)
            centre = jnp.sum(p * dp, axis=-1, keepdims=True)
            ds = (p * (dp - centre)).astype(BF16)
            dqs.append(dot_nn(ds, k))
            dks.append(dot_tn(ds, qh))
            dvs.append(dot_tn(p.astype(BF16), gh))
        o_ref[row0 : row0 + tile, pl.ds(col, PAIR)] = (
            jnp.where(first, dqs[0], dqs[1]) * scale
        ).astype(BF16)
        dk_all = dks[0] + dks[1]
        dv_all = dvs[0] + dvs[1]
        for j in range(i + 1):
            part_k = dk_all[j * tile : (j + 1) * tile]
            part_v = dv_all[j * tile : (j + 1) * tile]
            dk[j] = part_k if dk[j] is None else dk[j] + part_k
            dv[j] = part_v if dv[j] is None else dv[j] + part_v
    for j, row0 in enumerate(starts):
        o_ref[row0 : row0 + tile, pl.ds(width + col, PAIR)] = (dk[j] * scale).astype(BF16)
        o_ref[row0 : row0 + tile, pl.ds(2 * width + col, PAIR)] = dv[j].astype(BF16)


def attention_backward(qkv, flag, grad, lse, tile=256):
    length, width = qkv.shape[0], qkv.shape[1] // 3
    pairs = width // PAIR
    spec = lambda off: pl.BlockSpec((length, PAIR), lambda j: (0, off + j))
    return pl.pallas_call(
        functools.partial(attn_bwd_kernel, tile),
        grid=(pairs,),
        in_specs=[
            pl.BlockSpec(memory_space=pltpu.SMEM),
            spec(0),
            spec(pairs),
            spec(2 * pairs),
            spec(0),
            spec(0),
        ],
        out_specs=pl.BlockSpec((length, 3 * width), lambda j: (0, 0)),
        out_shape=jax.ShapeDtypeStruct((length, 3 * width), BF16),
        compiler_params=params(40),
        cost_estimate=cost(length, length),
        name="attn_bwd",
    )(flag, qkv, qkv, qkv, grad, lse)


def dense_kernel(mid_ref, dg_ref, up_ref, down_ref, out_ref, mg_ref, wu_ref, wd_ref):
    mid = mid_ref[...]
    dg = dg_ref[...]
    up = up_ref[...]
    down = down_ref[...]
    act, slope = gelu_pair(dot_nn(mid, up))
    act = act.astype(BF16)
    pg = (dot_nt(dg, down) * slope).astype(BF16)
    out = dot_nn(act, down)
    mg = dot_nt(pg, up)
    wu_ref[...] = dot_tn(mid, pg).astype(BF16)
    wd_ref[...] = dot_tn(act, dg).astype(BF16)

    @pl.when(pl.program_id(0) == 0)
    def _():
        out_ref[...] = out
        mg_ref[...] = mg

    @pl.when(pl.program_id(0) > 0)
    def _():
        out_ref[...] += out
        mg_ref[...] += mg


def dense_branch(mid, dg, up, down, tile=512):
    length, width = mid.shape
    ff = up.shape[1]
    whole = pl.BlockSpec((length, width), lambda j: (0, 0))
    cols = pl.BlockSpec((width, tile), lambda j: (0, j))
    rows = pl.BlockSpec((tile, width), lambda j: (j, 0))
    return pl.pallas_call(
        dense_kernel,
        grid=(ff // tile,),
        in_specs=[whole, whole, cols, rows],
        out_specs=[whole, whole, cols, rows],
        out_shape=[
            jax.ShapeDtypeStruct((length, width), F32),
            jax.ShapeDtypeStruct((length, width), F32),
            jax.ShapeDtypeStruct((width, ff), BF16),
            jax.ShapeDtypeStruct((ff, width), BF16),
        ],
        compiler_params=params(48),
        cost_estimate=cost(length, length),
        name="dense_branch",
    )(mid, dg, up, down)


def expert_kernel(mid_ref, g_ref, mix_ref, up_ref, down_ref, po_ref, pi_ref, act_ref, pg_ref, eg_ref, dot_ref):
    mid = mid_ref[...]
    g = g_ref[...].astype(F32)
    logits = dot_nn(mid, mix_ref[...])
    share = 1.0 / (1.0 + jnp.exp(logits[:, 0:1] - logits[:, 1:2]))
    eg = (share * g).astype(BF16)
    eg_ref[...] = eg
    act, slope = gelu_pair(dot_nn(mid, up_ref[...]))
    act = act.astype(BF16)
    act_ref[...] = act
    pg = (dot_nt(eg, down_ref[...]) * slope).astype(BF16)
    pg_ref[...] = pg
    pi_ref[...] = dot_nt(pg, up_ref[...]).astype(BF16)
    po = dot_nn(act, down_ref[...])
    po_ref[...] = po.astype(BF16)
    dot_ref[...] = jnp.sum(po * g, axis=-1, keepdims=True)


def expert_chunk(mid, g, mix_pad, up, down, tile=320):
    rows, width = mid.shape
    hidden = up.shape[1]
    block = pl.BlockSpec((tile, width), lambda i: (i, 0))
    hblock = pl.BlockSpec((tile, hidden), lambda i: (i, 0))
    full = lambda a: pl.BlockSpec(a.shape, lambda i: (0, 0))
    return pl.pallas_call(
        expert_kernel,
        grid=(rows // tile,),
        in_specs=[block, block, full(mix_pad), full(up), full(down)],
        out_specs=[block, block, hblock, hblock, block, pl.BlockSpec((tile, 1), lambda i: (i, 0))],
        out_shape=[
            jax.ShapeDtypeStruct((rows, width), BF16),
            jax.ShapeDtypeStruct((rows, width), BF16),
            jax.ShapeDtypeStruct((rows, hidden), BF16),
            jax.ShapeDtypeStruct((rows, hidden), BF16),
            jax.ShapeDtypeStruct((rows, width), BF16),
            jax.ShapeDtypeStruct((rows, 1), F32),
        ],
        compiler_params=params(48),
        cost_estimate=cost(8 * rows * width * hidden, 14 * rows * width + 4 * width * hidden),
        name="expert_chunk",
    )(mid, g, mix_pad, up, down)


def expert_grad_kernel(count, *refs):
    mids, pgs, acts, egs = (refs[i * count : (i + 1) * count] for i in range(4))
    du_ref, dd_ref = refs[4 * count :]
    up_sum = dot_tn(mids[0][...], pgs[0][...])
    down_sum = dot_tn(acts[0][...], egs[0][...])
    for i in range(1, count):
        up_sum += dot_tn(mids[i][...], pgs[i][...])
        down_sum += dot_tn(acts[i][...], egs[i][...])
    du_ref[...] = up_sum
    dd_ref[...] = down_sum


def expert_weight_grads(mids, pgs, acts, egs, tile=256):
    count = len(mids)
    rows, width = mids[0].shape
    hidden = pgs[0].shape[1]
    full = lambda a: pl.BlockSpec(a.shape, lambda j: (0, 0))
    cols = lambda a: pl.BlockSpec((a.shape[0], tile), lambda j: (0, j))
    return pl.pallas_call(
        functools.partial(expert_grad_kernel, count),
        grid=(hidden // tile,),
        in_specs=[full(a) for a in mids]
        + [cols(a) for a in pgs]
        + [cols(a) for a in acts]
        + [full(a) for a in egs],
        out_specs=[
            pl.BlockSpec((width, tile), lambda j: (0, j)),
            pl.BlockSpec((tile, width), lambda j: (j, 0)),
        ],
        out_shape=[jax.ShapeDtypeStruct((width, hidden), F32), jax.ShapeDtypeStruct((hidden, width), F32)],
        compiler_params=params(48),
        cost_estimate=cost(4 * count * rows * width * hidden, 8 * count * rows * width + 8 * width * hidden),
        name="expert_weight_grads",
    )(*mids, *pgs, *acts, *egs)


def exchange_kernel(
    waves, layers, groups, slots_ref, *refs
):
    gathered = 2 * layers - 1
    g_low = [refs[0], *refs[1:layers]]
    g_high = [refs[0], *refs[layers:gathered]]
    mix_ref, up_ref, down_ref, back_ref, slab_ref = refs[gathered : gathered + 5]
    po_refs = refs[gathered + 5 : gathered + layers + 5]
    (
        du_ref, dd_ref, g_refs, buf, part, got, act_s, pg_s, eg_s, home, home_slab,
        g_sem, a_send, a_recv, z_send, z_recv, r_send, r_recv, b_send, b_recv,
    ) = refs[gathered + layers + 5 :]
    each = groups // waves
    capacity, width = slots_ref.shape[1:]
    rows = each * capacity
    last = layers - 1
    here, me = lax.axis_index("dp"), lax.axis_index("ep")
    up_id, down_id = lax.rem(here + 1, layers), lax.rem(here + last, layers)
    peer = lambda j: lax.rem(me + j, groups)
    source = lambda j: lax.rem(me + groups - j, groups)
    mesh_id = pl.DeviceIdType.MESH

    def a_copy(j):
        return pltpu.make_async_remote_copy(
            slots_ref.at[peer(j)], buf.at[j // each, 0, lax.rem(j, each)],
            a_send.at[j], a_recv.at[j], device_id={"ep": peer(j)}, device_id_type=mesh_id,
        )

    def z_copy(w, way, s):
        src, dst = ((layers - s + 1) % layers, layers - s) if way == 0 else (s - 1, s)
        return pltpu.make_async_remote_copy(
            buf.at[w, src], buf.at[w, dst], z_send.at[w, way, s - 1], z_recv.at[w, way, s - 1],
            device_id={"dp": up_id if way == 0 else down_id}, device_id_type=mesh_id,
        )

    def r_copy(w, way, s):
        return pltpu.make_async_remote_copy(
            part.at[w, layers - s if way == 0 else s], got.at[w, way, s - 1],
            r_send.at[w, way, s - 1], r_recv.at[w, way, s - 1],
            device_id={"dp": up_id if way == 0 else down_id}, device_id_type=mesh_id,
        )

    def b_copies(j):
        w, i = j // each, lax.rem(j, each)
        start = pl.multiple_of(i * capacity, 16)
        return [
            pltpu.make_async_remote_copy(
                src, dst, b_send.at[j, n], b_recv.at[j, n],
                device_id={"ep": source(j)}, device_id_type=mesh_id,
            )
            for n, (src, dst) in enumerate(
                (
                    (part.at[w, 0, pl.ds(start, capacity)], home.at[j]),
                    (part.at[w, 0, pl.ds(rows, 16)], home_slab.at[j]),
                )
            )
        ]

    def z_sends(way, s):
        if way == 0:
            return jnp.logical_and(here <= last - 1, here >= s - 1)
        return jnp.logical_and(here >= 1, here <= layers - s)

    def z_gets(way, s):
        return here >= s if way == 0 else here <= last - s

    def r_sends(way, s):
        return here <= s - 1 if way == 0 else here >= layers - s

    def r_gets(way, s):
        if way == 0:
            return jnp.logical_and(here >= 1, here <= s)
        return jnp.logical_and(here >= last - s, here <= last - 1)

    def g_copy(ref, k):
        return pltpu.make_async_copy(ref, g_refs.at[k], g_sem.at[k])

    for k in range(layers):
        pl.when(here + k <= last)(lambda k=k: g_copy(g_high[k], k).start())
        if k:
            pl.when(here + k > last)(lambda k=k: g_copy(g_low[layers - k], k).start())

    part[...] = jnp.zeros_like(part)
    got[:, :, last - 1] = jnp.zeros_like(got[:, :, last - 1])
    du_ref[...] = jnp.zeros_like(du_ref)
    dd_ref[...] = jnp.zeros_like(dd_ref)

    barrier = pltpu.get_barrier_semaphore()

    def greet(j, carry):
        pl.semaphore_signal(barrier, inc=1, device_id={"ep": peer(j)}, device_id_type=mesh_id)
        return carry

    lax.fori_loop(1, groups, greet, 0)

    @pl.when(here < last)
    def _():
        pl.semaphore_signal(barrier, inc=1, device_id={"dp": up_id}, device_id_type=mesh_id)

    @pl.when(here > 0)
    def _():
        pl.semaphore_signal(barrier, inc=1, device_id={"dp": down_id}, device_id_type=mesh_id)

    pl.semaphore_wait(barrier, groups - 1 + jnp.where(here < last, 1, 0) + jnp.where(here > 0, 1, 0))

    def over(first, count, act):
        lax.fori_loop(first, count, lambda j, c: (act(j), c)[1], 0)

    over(1, groups, lambda j: a_copy(j).start())
    buf[0, 0, 0] = slots_ref[me]
    for k in range(layers):
        g_copy(g_high[k], k).wait()

    def slab_of(row):
        high = row.astype(BF16).astype(F32)
        line = lax.broadcasted_iota(jnp.int32, (16, rows), 0)
        return jnp.where(line == 0, high, jnp.where(line == 1, row - high, 0.0)).astype(BF16)

    def piece(w, ks):
        mid = jnp.concatenate([buf[w, k].reshape(rows, width) for k in ks], axis=0)
        g = jnp.concatenate(
            [g_refs[k, source(w * each + i)] for k in ks for i in range(each)], axis=0
        ).astype(F32)
        logits = dot_nn(mid, mix_ref[...])
        share = 1.0 / (1.0 + jnp.exp(logits[:, 0:1] - logits[:, 1:2]))
        eg = (share * g).astype(BF16)
        act, slope = gelu_pair(dot_nn(mid, up_ref[...]))
        act = act.astype(BF16)
        pg = (dot_nt(eg, down_ref[...]) * slope).astype(BF16)
        pi = dot_nt(pg, up_ref[...]).astype(BF16)
        po = dot_nn(act, down_ref[...])
        sums = jnp.sum(po * g, axis=-1, keepdims=True)
        po = po.astype(BF16)
        diag = lax.broadcasted_iota(jnp.int32, (rows, rows), 0) == lax.broadcasted_iota(
            jnp.int32, (rows, rows), 1
        )
        for n, k in enumerate(ks):
            mine = slice(n * rows, (n + 1) * rows)
            spot = slice(k * rows, (k + 1) * rows)
            eg_s[spot] = eg[mine]
            act_s[spot] = act[mine]
            pg_s[spot] = pg[mine]
            part[w, k, 0:rows] = pi[mine]
            line = jnp.sum(jnp.where(diag, sums[mine], 0.0), axis=0, keepdims=True)
            part[w, k, rows : rows + 16, 0:rows] = slab_of(line)
            for i in range(each):
                at = n * rows + i * capacity
                po_refs[k][source(w * each + i)] = po[at : at + capacity]

    def weight_grads(w):
        mid = buf[w].reshape(layers * rows, width)
        du_ref[...] += dot_tn(mid, pg_s[...])
        dd_ref[...] += dot_tn(act_s[...], eg_s[...])

    def add_to(w, k, pieces):
        total = part[w, k, 0:rows].astype(F32)
        extra = part[w, k, rows : rows + 16, 0:rows].astype(F32)
        for way, s in pieces:
            total = total + got[w, way, s - 1, 0:rows].astype(F32)
            extra = extra + got[w, way, s - 1, rows : rows + 16, 0:rows].astype(F32)
        part[w, k, 0:rows] = total.astype(BF16)
        part[w, k, rows : rows + 16, 0:rows] = slab_of(jnp.sum(extra, axis=0, keepdims=True))

    def start_hop(copy, sends, w, s):
        for way in range(2):
            pl.when(sends(way, s))(lambda way=way: copy(w, way, s).start())

    def get_hop(copy, gets, w, s):
        for way in range(2):
            pl.when(gets(way, s))(lambda way=way: copy(w, way, s).wait_recv())

    def pass_on(w, s):
        for way in range(2):

            @pl.when(r_gets(way, s))
            def _():
                r_copy(w, way, s).wait_recv()
                add_to(w, layers - s - 1 if way == 0 else s + 1, [(way, s)])

        start_hop(r_copy, r_sends, w, s + 1)

    def finish(w):
        get_hop(r_copy, r_gets, w, last)
        add_to(w, 0, [(0, last), (1, last)])
        for i in range(each):
            j = w * each + i
            start = i * capacity

            @pl.when(j > 0)
            def _():
                for copy in b_copies(j):
                    copy.start()

            @pl.when(j == 0)
            def _():
                home[0] = part[0, 0, start : start + capacity]
                home_slab[0] = part[0, 0, rows : rows + 16]

    def first_hop(w):
        for n in range(each):
            pl.when(w * each + n > 0)(lambda n=n: a_copy(w * each + n).wait_recv())
        start_hop(z_copy, z_sends, w, 1)

    far = [1, last]
    near = [k for k in range(layers) if k not in far]

    def body(i, carry):
        w = i - 1
        gathers = i < waves
        works = jnp.logical_and(i >= 1, i <= waves)

        pl.when(i == 0)(lambda: first_hop(0))

        @pl.when(works)
        def _():
            piece(w, far)
            start_hop(r_copy, r_sends, w, 1)

        @pl.when(i >= 2)
        def _():
            finish(i - 2)

        for s in range(1, last):

            @pl.when(gathers)
            def _():
                get_hop(z_copy, z_gets, i, s)
                start_hop(z_copy, z_sends, i, s + 1)
                if s == last - 1:
                    pl.when(i + 1 < waves)(lambda: first_hop(i + 1))

            @pl.when(works)
            def _():
                if s == 1:
                    piece(w, near)
                if s == last - 1:
                    weight_grads(w)
                pass_on(w, s)

        @pl.when(gathers)
        def _():
            get_hop(z_copy, z_gets, i, last)

        return carry

    lax.fori_loop(0, waves + 2, body, 0)

    def land(j, carry):
        for copy in b_copies(j):
            copy.wait_recv()
            copy.wait_send()
        a_copy(j).wait_send()
        return carry

    lax.fori_loop(1, groups, land, 0)

    def sent(w, carry):
        for way in range(2):
            for s in range(1, layers):
                pl.when(z_sends(way, s))(lambda: z_copy(w, way, s).wait_send())
                pl.when(r_sends(way, s))(lambda: r_copy(w, way, s).wait_send())
        return carry

    lax.fori_loop(0, waves, sent, 0)

    def arrange(j, carry):
        back_ref[peer(j)] = home[j]
        slab_ref[peer(j)] = home_slab[j]
        return carry

    lax.fori_loop(0, groups, arrange, 0)


def exchange_waves(groups):
    return 4 if groups % 4 == 0 else 1


def expert_exchange(slots, g_low, g_high, mix_pad, up, down):
    layers, groups = lax.axis_size("dp"), lax.axis_size("ep")
    waves = exchange_waves(groups)
    each = groups // waves
    _, capacity, width = slots.shape
    hidden = up.shape[1]
    rows = each * capacity
    sem = pltpu.SemaphoreType.DMA
    block = jax.ShapeDtypeStruct((groups, capacity, width), BF16)
    vmem = pl.BlockSpec(memory_space=pltpu.VMEM)
    total_rows = layers * groups * capacity
    outs = pl.pallas_call(
        functools.partial(exchange_kernel, waves, layers, groups),
        in_specs=[vmem] + [pl.BlockSpec(memory_space=pl.ANY)] * (2 * layers - 1) + [vmem] * 3,
        out_specs=[vmem] * (4 + layers),
        out_shape=[block, jax.ShapeDtypeStruct((groups, 16, width), BF16)]
        + [block] * layers
        + [jax.ShapeDtypeStruct((width, hidden), F32), jax.ShapeDtypeStruct((hidden, width), F32)],
        scratch_shapes=[
            pltpu.VMEM((layers, groups, capacity, width), BF16),
            pltpu.VMEM((waves, layers, each, capacity, width), BF16),
            pltpu.VMEM((waves, layers, rows + 16, width), BF16),
            pltpu.VMEM((waves, 2, layers - 1, rows + 16, width), BF16),
            pltpu.VMEM((layers * rows, hidden), BF16),
            pltpu.VMEM((layers * rows, hidden), BF16),
            pltpu.VMEM((layers * rows, width), BF16),
            pltpu.VMEM((groups, capacity, width), BF16),
            pltpu.VMEM((groups, 16, width), BF16),
            sem((layers,)),
            sem((groups,)),
            sem((groups,)),
            sem((waves, 2, layers - 1)),
            sem((waves, 2, layers - 1)),
            sem((waves, 2, layers - 1)),
            sem((waves, 2, layers - 1)),
            sem((groups, 2)),
            sem((groups, 2)),
        ],
        compiler_params=pltpu.CompilerParams(
            collective_id=0, has_side_effects=True, vmem_limit_bytes=62 << 20
        ),
        cost_estimate=cost(12 * total_rows * width * hidden, 20 * total_rows * width),
        name="expert_exchange",
    )(slots, *g_low, *g_high[1:], mix_pad, up, down)
    return outs[0], outs[1], outs[2 : 2 + layers], outs[2 + layers], outs[3 + layers]


def sums_kernel(plan, split, layers, groups, small_ref, *refs):
    count = len(plan)
    mats, outs = refs[:count], refs[count : 2 * count]
    (
        small_out, own, sib, got, held, inner, final, wide, small_two, small_chip, small_layer,
        own_sem, s_send, s_recv, x_send, x_recv, z_send, z_recv, t_send, t_recv, o_sem,
    ) = refs[2 * count :]
    chips = groups // 2
    width = held.shape[-1]
    total = held.shape[0]
    last = layers - 1
    here, me = lax.axis_index("dp"), lax.axis_index("ep")
    core, chip = lax.rem(me, 2), me // 2
    sibling = me + 1 - 2 * core
    mesh_id = pl.DeviceIdType.MESH
    chip_at = lambda j: lax.rem(chip + j, chips)
    pieces = [(m, i, n) for m in range(count) for i in range(plan[m]) for n in range(split)]
    lines = held.shape[1]
    square = chips == 4
    by_one = chip + 1 - 2 * lax.rem(chip, 2)
    by_two = chip + 2 - 4 * (chip // 2)
    at_end = jnp.logical_or(here == 0, here == last)
    inside = jnp.logical_and(here > 0, here < last)
    inward = 1 + (here // last) * (last - 2)
    outward = lax.rem((here - 1) * last + layers * last, layers)
    across = last - here

    def source(m, i, n, half):
        span = pl.ds(n * lines, lines)
        if len(mats[m].shape) == 5:
            return mats[m].at[:, half, i, span]
        return mats[m].at[:, half, span, pl.ds(i * width, width)]

    def remote(src, dst, send, recv, where):
        return pltpu.make_async_remote_copy(
            src, dst, send, recv, device_id=where, device_id_type=mesh_id
        )

    def s_copy(c):
        return remote(source(*pieces[c], 1 - core), sib.at[c], s_send.at[c], s_recv.at[c], {"ep": sibling})

    def x_copy(c, j):
        return remote(
            own.at[c, chip_at(j)], got.at[c, j - 1], x_send.at[c, j - 1], x_recv.at[c, j - 1],
            {"ep": 2 * chip_at(j) + core},
        )

    def near_chip(c):
        return by_one + lax.rem(c, 2) * (by_two - by_one)

    def next_chip(c):
        return by_two + lax.rem(c, 2) * (by_one - by_two)

    def y_copy(c, n):
        block = (near_chip(c), 3 - chip, next_chip(c))[n]
        where = next_chip(c) if n == 2 else near_chip(c)
        return remote(
            own.at[c, block], got.at[c, n], x_send.at[c, n], x_recv.at[c, n], {"ep": 2 * where + core}
        )

    lags = [LAG * n for n in range(1, 6)] if square else [0] + [LAG * n for n in range(1, 5)]

    def due(t, n):
        return jnp.logical_and(t >= lags[n], t < total + lags[n])

    def z_copy(c, n):
        src = (held, held, inner)[n]
        dst = (inner, final, final)[n]
        where = (inward, across, outward)[n]
        return remote(src.at[c], dst.at[c], z_send.at[c, n], z_recv.at[c, n], {"dp": where})

    def t_copy(n, j):
        if n == 0:
            return remote(small_ref, small_two, t_send.at[0, 0], t_recv.at[0, 0], {"ep": sibling})
        if n == 1:
            spot = small_chip.at[chip]
            return remote(spot, spot, t_send.at[1, j], t_recv.at[1, j], {"ep": 2 * chip_at(j) + core})
        spot = small_layer.at[here]
        return remote(
            spot, spot, t_send.at[2, j], t_recv.at[2, j], {"dp": lax.rem(here + j, layers)}
        )

    for c in range(total):
        pltpu.make_async_copy(source(*pieces[c], core), own.at[c], own_sem.at[c]).start()

    barrier = pltpu.get_barrier_semaphore()
    pl.semaphore_signal(barrier, inc=1, device_id={"ep": sibling}, device_id_type=mesh_id)

    def over(first, end, act):
        def step(j, carry):
            act(j)
            return carry

        lax.fori_loop(first, end, step, 0)

    over(
        1,
        chips,
        lambda j: pl.semaphore_signal(
            barrier, inc=1, device_id={"ep": 2 * chip_at(j) + core}, device_id_type=mesh_id
        ),
    )
    over(
        1,
        layers,
        lambda j: pl.semaphore_signal(
            barrier, inc=1, device_id={"dp": lax.rem(here + j, layers)}, device_id_type=mesh_id
        ),
    )
    pl.semaphore_wait(barrier, chips + last)

    t_copy(0, 0).start()
    for c in range(total):
        s_copy(c).start()

    def body(t, carry):
        @pl.when(t < total)
        def _():
            pltpu.make_async_copy(sib.at[t], own.at[t], own_sem.at[t]).wait()
            remote(own.at[t], sib.at[t], s_send.at[t], s_recv.at[t], {"ep": sibling}).wait_recv()

            def add(p):
                own[t, p] = own[t, p] + sib[t, p]

            over(0, chips, add)
            if square:
                y_copy(t, 1).start()
                y_copy(t, 0).start()
            else:
                over(1, chips, lambda j: x_copy(t, j).start())

        if square:

            @pl.when(due(t, 0))
            def _():
                c = t - lags[0]
                y_copy(c, 1).wait_recv()
                own[c, next_chip(c)] = own[c, next_chip(c)] + got[c, 1]
                y_copy(c, 2).start()
                y_copy(c, 0).wait_recv()
                own[c, chip] = own[c, chip] + got[c, 0]

        @pl.when(due(t, 1))
        def _():
            c = t - lags[1]
            if square:
                y_copy(c, 2).wait_recv()
                held[c] = own[c, chip] + got[c, 2]
            else:
                over(1, chips, lambda j: x_copy(c, j).wait_recv())
                wide[c] = own[c, chip].astype(F32)

                def add(j):
                    wide[c] += got[c, j - 1].astype(F32)

                over(1, chips, add)
                held[c] = wide[c].astype(BF16)
            pl.when(at_end)(lambda: z_copy(c, 0).start())

        @pl.when(jnp.logical_and(inside, due(t, 2)))
        def _():
            c = t - lags[2]
            z_copy(c, 0).wait_recv()
            held[c] = held[c] + inner[c]
            z_copy(c, 1).start()

        @pl.when(jnp.logical_and(inside, due(t, 3)))
        def _():
            c = t - lags[3]
            z_copy(c, 1).wait_recv()
            both = held[c] + final[c]
            inner[c] = both
            wide[c] = both.astype(F32)
            z_copy(c, 2).start()

        @pl.when(jnp.logical_and(at_end, due(t, 4)))
        def _():
            c = t - lags[4]
            z_copy(c, 2).wait_recv()
            wide[c] = final[c].astype(F32)

        @pl.when(t == 1)
        def _():
            t_copy(0, 0).wait_recv()
            small_chip[chip] = small_ref[...] + small_two[...]
            over(1, chips, lambda j: t_copy(1, j).start())

        @pl.when(t == 3)
        def _():
            over(1, chips, lambda j: t_copy(1, j).wait_recv())
            acc = small_chip[0]
            for n in range(1, chips):
                acc = acc + small_chip[n]
            small_layer[here] = acc
            over(1, layers, lambda j: t_copy(2, j).start())

        return carry

    lax.fori_loop(0, total + lags[4], body, 0)

    copies = []
    for c, (m, i, n) in enumerate(pieces):
        span = pl.ds(n * lines, lines)
        if len(outs[m].shape) == 3:
            spot = outs[m].at[i, span]
        else:
            spot = outs[m].at[span, pl.ds(i * width, width)]
        copies.append(pltpu.make_async_copy(wide.at[c], spot, o_sem.at[c]))
        copies[-1].start()

    over(1, layers, lambda j: t_copy(2, j).wait_recv())
    acc = small_layer[0]
    for n in range(1, layers):
        acc = acc + small_layer[n]
    small_out[...] = acc

    t_copy(0, 0).wait_send()
    over(1, chips, lambda j: t_copy(1, j).wait_send())
    over(1, layers, lambda j: t_copy(2, j).wait_send())

    def sent(c):
        remote(own.at[c], sib.at[c], s_send.at[c], s_recv.at[c], {"ep": sibling}).wait_send()
        if square:
            for n in range(3):
                y_copy(c, n).wait_send()
        else:
            over(1, chips, lambda j: x_copy(c, j).wait_send())
        pl.when(at_end)(lambda: z_copy(c, 0).wait_send())

        @pl.when(inside)
        def _():
            z_copy(c, 1).wait_send()
            z_copy(c, 2).wait_send()

    over(0, total, sent)
    for copy in copies:
        copy.wait()


def gradient_sums(small, columns, rows_split):
    layers, groups = lax.axis_size("dp"), lax.axis_size("ep")
    chips = groups // 2
    width = small.shape[1]
    plan = [a.shape[1] // width for a in columns] + [a.shape[0] // width for a in rows_split]
    high = columns[0].shape[0] // groups
    split = SPLIT if high % (16 * SPLIT) == 0 else 1
    total, lines = sum(plan) * split, high // split
    views = [a.reshape(chips, 2, high, a.shape[1]) for a in columns] + [
        a.reshape(chips, 2, n, high, width) for a, n in zip(rows_split, plan[len(columns) :])
    ]
    shapes = [jax.ShapeDtypeStruct((high, a.shape[1]), F32) for a in columns] + [
        jax.ShapeDtypeStruct((n, high, width), F32) for n in plan[len(columns) :]
    ]
    sem = pltpu.SemaphoreType.DMA
    vmem = pl.BlockSpec(memory_space=pltpu.VMEM)
    anywhere = pl.BlockSpec(memory_space=pl.ANY)
    buffers = lambda *lead: pltpu.VMEM((total, *lead, lines, width), BF16)
    outs = pl.pallas_call(
        functools.partial(sums_kernel, plan, split, layers, groups),
        in_specs=[vmem] + [anywhere] * len(views),
        out_specs=[anywhere] * len(views) + [vmem],
        out_shape=shapes + [jax.ShapeDtypeStruct(small.shape, F32)],
        scratch_shapes=[
            buffers(chips),
            buffers(chips),
            buffers(chips - 1),
            buffers(),
            buffers(),
            buffers(),
            pltpu.VMEM((total, lines, width), F32),
            pltpu.VMEM(small.shape, F32),
            pltpu.VMEM((chips, *small.shape), F32),
            pltpu.VMEM((layers, *small.shape), F32),
            sem((total,)),
            sem((total,)),
            sem((total,)),
            sem((total, chips - 1)),
            sem((total, chips - 1)),
            sem((total, 3)),
            sem((total, 3)),
            sem((3, max(chips, layers))),
            sem((3, max(chips, layers))),
            sem((total,)),
        ],
        compiler_params=pltpu.CompilerParams(
            collective_id=1, has_side_effects=True, vmem_limit_bytes=62 << 20
        ),
        cost_estimate=cost(10 * total * chips * lines * width, 8 * total * chips * lines * width),
        name="gradient_sums",
    )(small, *views)
    rows_out = [a.reshape(-1, width) for a in outs[len(columns) : -1]]
    return (*outs[: len(columns)], *rows_out, outs[-1])


def normalise(values_in):
    centred = values_in - jnp.mean(values_in, axis=-1, keepdims=True)
    inverse = lax.rsqrt(jnp.mean(centred * centred, axis=-1, keepdims=True) + 1e-05)
    return centred * inverse, inverse


def norm_backward(grad, gain_vec, unit, inverse):
    m = grad * gain_vec
    return inverse * (
        m
        - jnp.mean(m, axis=-1, keepdims=True)
        - unit * jnp.mean(m * unit, axis=-1, keepdims=True)
    )


def hop(rows, step, stage):
    size = lax.axis_size("dp")
    if step > 0:
        pairs = [(i, i + 1) for i in range(stage - 1, size - 1)]
    else:
        pairs = [(i + 1, i) for i in range(0, size - stage)]
    return lax.ppermute(rows, "dp", pairs)


def both_hops(low, high, stage):
    return hop(low, 1, stage), hop(high, -1, stage)


def send_hop(rows, step, stage):
    size = lax.axis_size("dp")
    if step > 0:
        pairs = [(i, i + 1) for i in range(stage)]
    else:
        pairs = [(i, i - 1) for i in range(size - stage, size)]
    return lax.ppermute(rows, "dp", pairs)


def line_reduce(parts):
    size = lax.axis_size("dp")
    up = send_hop(parts[size - 1], 1, 1)
    down = send_hop(parts[1], -1, 1)
    for stage in range(2, size):
        up = send_hop(up + parts[size - stage], 1, stage)
        down = send_hop(down + parts[stage], -1, stage)
    return parts[0].astype(F32) + up.astype(F32) + down.astype(F32)


def shifted(rows, step):
    size = lax.axis_size("dp")
    return lax.ppermute(rows, "dp", [((i + step) % size, i) for i in range(size)])


def after(values, *earlier):
    many = isinstance(values, tuple)
    held = lax.optimization_barrier((*values, *earlier) if many else (values, *earlier))
    return held[: len(values)] if many else held[0]


def sum_layers(rows):
    size, here = lax.axis_size("dp"), lax.axis_index("dp")
    pieces = rows.reshape(size, rows.shape[0] // size, rows.shape[1])
    piece = lambda k: lax.dynamic_index_in_dim(pieces, lax.rem(here + k, size), 0, keepdims=False)
    acc = piece(0).astype(F32)
    for k in range(1, size):
        acc = acc + shifted(piece(k), size - k).astype(F32)
    mine = acc.astype(BF16)
    ring = jnp.stack([mine] + [shifted(mine, k) for k in range(1, size)])
    ordered = lax.dynamic_slice_in_dim(jnp.concatenate([ring, ring]), size - here, size, 0)
    return ordered.reshape(rows.shape).astype(F32)


def sum_everywhere(values):
    for axis in ("dp", "ep"):
        size = lax.axis_size(axis)
        step = 1
        while step < size:
            values = values + lax.ppermute(values, axis, [(i, i ^ step) for i in range(size)])
            step *= 2
    return values


def on_device(
    tokens,
    bucket,
    expert_ids,
    ln1_gain,
    qkv_weight,
    out_weight,
    ln2_gain,
    up_weight,
    down_weight,
    mix_weight,
    expert_up,
    expert_down,
    cotangent,
):
    length, width = tokens.shape
    groups = lax.axis_size("ep")
    layers = lax.axis_size("dp")
    experts = groups * expert_up.shape[0]
    capacity = 5 * length // (4 * experts)
    slots = experts * capacity
    gather = lambda w: lax.all_gather(w, "ep", axis=0, tiled=True)
    exchange_out = lambda a: lax.all_to_all(a, "ep", split_axis=0, concat_axis=1, tiled=True)
    expert_up2 = expert_up[0]
    expert_down2 = expert_down[0]
    mix_pad = jnp.pad(mix_weight, ((0, 0), (0, 126)))

    chosen = expert_ids[:, 0]
    one_hot = chosen[:, None] == jnp.arange(experts, dtype=jnp.int32)[None, :]
    place = jnp.arange(length, dtype=jnp.int32)
    earlier = (place[None, :] < place[:, None]).astype(BF16)
    before = dot_nn(earlier, one_hot.astype(BF16))
    slot_index = jnp.sum(jnp.where(one_hot, before, 0.0), axis=1).astype(jnp.int32)
    target = jnp.where(slot_index < capacity, chosen * capacity + slot_index, -1)
    table = (target[:, None] == jnp.arange(slots, dtype=jnp.int32)[None, :]).astype(BF16)

    pick = lambda rows: dot_tn(table, rows).astype(BF16).reshape(experts, capacity, width)
    join = lambda lows, highs: [highs[k] + lows[layers - k] for k in range(1, layers)]

    token_rows = tokens.astype(F32)
    unit1, inverse1 = normalise(token_rows)
    normed_in = (unit1 * ln1_gain).astype(BF16)
    g_own = exchange_out(pick(cotangent)).reshape(slots, width)
    normed_in, g_own, qkv_weight = lax.optimization_barrier((normed_in, g_own, qkv_weight))
    qkv_full, out_full, up_full, down_full = (
        gather(qkv_weight),
        gather(out_weight),
        gather(up_weight),
        gather(down_weight),
    )
    g_low, g_high = [g_own], [g_own]

    def step(lows, highs, *others):
        stage = len(lows)
        held = lax.optimization_barrier((lows[-1], highs[-1], *others))
        lows[-1], highs[-1] = held[:2]
        if stage < layers:
            low, high = both_hops(lows[-1], highs[-1], stage)
            lows.append(low)
            highs.append(high)
        return held[2:]

    step(g_low, g_high)
    (normed_in,) = step(g_low, g_high, normed_in)
    qkv_rows = dot_nn(normed_in, qkv_full).astype(BF16)
    (qkv_rows,) = step(g_low, g_high, qkv_rows)
    attended, lse = attention_forward(qkv_rows, bucket)
    hidden_res = token_rows + dot_nn(attended, out_full)
    unit2, inverse2 = normalise(hidden_res)
    mid_low = (unit2 * ln2_gain).astype(BF16)
    mid_slots = pick(mid_low)
    (mid_slots,) = step(g_low, g_high, mid_slots)

    grad_out = cotangent.astype(F32)
    logits = dot_nn(mid_low, mix_weight)
    mix1 = 1.0 / (1.0 + jnp.exp(logits[:, 0:1] - logits[:, 1:2]))
    mix0 = 1.0 / (1.0 + jnp.exp(logits[:, 1:2] - logits[:, 0:1]))
    dense_grad = (mix0 * grad_out).astype(BF16)
    scatter = lambda a: lax.psum_scatter(a.astype(BF16), "ep", scatter_dimension=0, tiled=True)
    back = lambda k, a: shifted(a, layers - k) if k else a

    def total(parts):
        acc = parts[0].astype(F32)
        for part in parts[1:]:
            acc = acc + part.astype(F32)
        return acc

    if capacity % 16 == 0:
        blocks = lambda many: [g.reshape(groups, capacity, width) for g in many]
        returned, slab, partial_outs, expert_up_grad, expert_down_grad = expert_exchange(
            mid_slots, blocks(g_low), blocks(g_high), mix_pad, expert_up2, expert_down2
        )
        each = groups // exchange_waves(groups)
        offset = lax.rem(
            jnp.arange(groups, dtype=jnp.int32) + groups - lax.axis_index("ep"), groups
        )
        spot = lax.rem(offset, each)[:, None] == jnp.arange(each, dtype=jnp.int32)[None, :]
        lines = slab[:, 0, : each * capacity].astype(F32) + slab[:, 1, : each * capacity].astype(F32)
        dot_back = jnp.sum(
            jnp.where(spot[:, :, None], lines.reshape(groups, each, capacity), 0.0), axis=1
        ).reshape(1, slots)
        dense_grad, returned = lax.optimization_barrier((dense_grad, returned))
        outs = [a.reshape(slots, width) for a in partial_outs]
    else:
        gs = [g_own] + join(g_low, g_high)
        mid_own = exchange_out(mid_slots).reshape(slots, width)
        mids = [mid_own] + [shifted(mid_own, k) for k in range(1, layers)]
        chunks = [expert_chunk(mids[k], gs[k], mix_pad, expert_up2, expert_down2) for k in range(layers)]
        in_total = line_reduce([c[1] for c in chunks])
        dot_sum = total([back(k, chunks[k][5].reshape(groups, capacity)) for k in range(layers)])
        dot_high = lax.reduce_precision(dot_sum, 8, 7)
        extra = jnp.stack([dot_high, dot_sum - dot_high], axis=1)
        extra = jnp.pad(extra, ((0, 0), (0, 14), (0, width - capacity)))
        packed = jnp.concatenate([in_total.reshape(groups, capacity, width), extra], axis=1)
        both = lax.all_to_all(packed.astype(BF16), "ep", split_axis=0, concat_axis=0, tiled=True)
        returned = both[:, :capacity]
        dot_back = (
            both[:, capacity, :capacity].astype(F32) + both[:, capacity + 1, :capacity].astype(F32)
        ).reshape(1, slots)
        outs = [c[0] for c in chunks]
        expert_up_grad, expert_down_grad = expert_weight_grads(
            mids, [c[3] for c in chunks], [c[2] for c in chunks], [c[4] for c in chunks]
        )

    outs = [back(k, outs[k]) for k in range(layers)]
    dense_out, mid_grad_dense, up_grad, down_grad = dense_branch(mid_low, dense_grad, up_full, down_full)
    in_rows = returned.reshape(slots, width)
    mix_dot1 = jnp.sum(table.astype(F32) * dot_back, axis=1, keepdims=True)
    mix_dot0 = jnp.sum(grad_out * dense_out, axis=-1, keepdims=True)
    mean_dot = mix0 * mix_dot0 + mix1 * mix_dot1
    logit_grad = jnp.concatenate(
        [mix0 * (mix_dot0 - mean_dot), mix1 * (mix_dot1 - mean_dot)], axis=1
    ).astype(BF16)
    mix_weight_grad = dot_tn(mid_low, logit_grad)
    mid_grad = mid_grad_dense + dot_nt(logit_grad, mix_weight) + dot_nn(table, in_rows)
    ln2_gain_grad = jnp.sum(mid_grad * unit2, axis=0)
    res_grad = grad_out + norm_backward(mid_grad, ln2_gain, unit2, inverse2)
    attn_out_grad = res_grad.astype(BF16)
    out_weight_grad = dot_tn(attended, attn_out_grad)
    attended_grad = dot_nt(attn_out_grad, out_full).astype(BF16)
    qkv_grad = attention_backward(qkv_rows, bucket, attended_grad, lse)
    qkv_weight_grad = dot_tn(normed_in, qkv_grad)
    normed_grad = dot_nt(qkv_grad, qkv_full)
    ln1_gain_grad = jnp.sum(normed_grad * unit1, axis=0)
    tokens_grad = res_grad + norm_backward(normed_grad, ln1_gain, unit1, inverse1)

    small = jnp.concatenate([ln1_gain_grad[None], ln2_gain_grad[None], mix_weight_grad.T], axis=0)
    small = jnp.pad(small, ((0, 4), (0, 0)))
    if layers == 4 and length // groups >= 16:
        qkv_final, out_final, up_final, down_final, small_sums = gradient_sums(
            small,
            [a.astype(BF16) for a in (qkv_weight_grad, out_weight_grad, up_grad)],
            [down_grad],
        )
    else:
        sums = [sum_layers(scatter(a)) for a in (qkv_weight_grad, out_weight_grad, up_grad, down_grad)]
        qkv_final, out_final, up_final, down_final = sums
        small_sums = sum_everywhere(small)
    outs = list(after(tuple(outs), small_sums))
    out_sum = total(outs).astype(BF16).reshape(groups, capacity, width)
    out_back = lax.all_to_all(out_sum, "ep", split_axis=0, concat_axis=0, tiled=True)
    expert_out = dot_nn(table, out_back.reshape(slots, width))
    result = (hidden_res + mix0 * dense_out + mix1 * expert_out).astype(BF16)

    return (
        result,
        tokens_grad,
        small_sums[0],
        qkv_final,
        out_final,
        small_sums[1],
        up_final,
        down_final,
        small_sums[2:4].T,
        expert_up_grad[None],
        expert_down_grad[None],
    )


def solution(mesh):
    placed = (
        P(("dp", "ep"), None),
        P(("dp", "ep")),
        P(("dp", "ep"), None),
        P(),
        P("ep", None),
        P("ep", None),
        P(),
        P("ep", None),
        P("ep", None),
        P(),
        P("ep", None, "dp"),
        P("ep", "dp", None),
        P(("dp", "ep"), None),
    )
    return jax.shard_map(
        on_device,
        mesh=mesh,
        in_specs=placed,
        out_specs=(
            P(("dp", "ep"), None),
            P(("dp", "ep"), None),
            P(),
            P("ep", None),
            P("ep", None),
            P(),
            P("ep", None),
            P("ep", None),
            P(),
            P("ep", None, "dp"),
            P("ep", "dp", None),
        ),
        check_vma=False,
    )
```

```python
import functools

import jax
import jax.numpy as jnp
from jax import lax
from jax.experimental import pallas as pl
from jax.experimental.pallas import tpu as pltpu
from jax.sharding import PartitionSpec as P

HEAD = 64
SHORT_SEQS = 4
PAIR = 2 * HEAD
NEG = -1e30
SPLIT = 2
LAG = 2
ROOT = 0.7978845608028654
CUBE = 0.044715
F32 = jnp.float32
BF16 = jnp.bfloat16


def dot_nn(a, b):
    return lax.dot_general(a, b, (((1,), (0,)), ((), ())), preferred_element_type=F32)


def dot_nt(a, b):
    return lax.dot_general(a, b, (((1,), (1,)), ((), ())), preferred_element_type=F32)


def dot_tn(a, b):
    return lax.dot_general(a, b, (((0,), (0,)), ((), ())), preferred_element_type=F32)


def gelu_pair(v):
    sq = v * v
    t = jnp.tanh(v * (ROOT + (ROOT * CUBE) * sq))
    half = 0.5 * (1.0 + t)
    slope = half + (0.5 * v) * (1.0 - t * t) * (ROOT + (3.0 * ROOT * CUBE) * sq)
    return v * half, slope


def params(vmem_mib):
    return pltpu.CompilerParams(vmem_limit_bytes=vmem_mib << 20)


def cost(flops, nbytes):
    return pl.CostEstimate(flops=int(flops), bytes_accessed=int(nbytes), transcendentals=0)


def allowed_block(flag, row0, rows, cols, short):
    r = row0 + lax.broadcasted_iota(jnp.int32, (rows, cols), 0)
    c = lax.broadcasted_iota(jnp.int32, (rows, cols), 1)
    shift = short.bit_length() - 1
    same = jnp.logical_or(flag == 1, lax.shift_right_logical(r, shift) == lax.shift_right_logical(c, shift))
    return jnp.logical_and(c <= r, same)


def attn_fwd_kernel(tile, flag_ref, q_ref, k_ref, v_ref, o_ref, lse_ref):
    length = q_ref.shape[0]
    flag = flag_ref[0]
    lane = lax.broadcasted_iota(jnp.int32, (1, PAIR), 1)
    first = lane < HEAD
    scale = HEAD ** (-0.5)
    for row0 in range(0, length, tile):
        cols = row0 + tile
        ok = allowed_block(flag, row0, tile, cols, length // SHORT_SEQS)
        q = q_ref[row0 : row0 + tile, :]
        k = k_ref[0:cols, :]
        v = v_ref[0:cols, :]
        outs, lses = [], []
        for h in range(2):
            qh = jnp.where(first if h == 0 else jnp.logical_not(first), q, jnp.zeros_like(q))
            s = jnp.where(ok, dot_nt(qh, k) * scale, NEG)
            peak = jnp.max(s, axis=-1, keepdims=True)
            p = jnp.exp(s - peak)
            total = jnp.sum(p, axis=-1, keepdims=True)
            outs.append(dot_nn((p * (1.0 / total)).astype(BF16), v))
            lses.append(peak + jnp.log(total))
        o_ref[row0 : row0 + tile, :] = jnp.where(first, outs[0], outs[1]).astype(BF16)
        lse_ref[row0 : row0 + tile, :] = jnp.where(first, lses[0], lses[1])


def attention_forward(qkv, flag, tile=256):
    length, width = qkv.shape[0], qkv.shape[1] // 3
    pairs = width // PAIR
    spec = lambda off: pl.BlockSpec((length, PAIR), lambda j: (0, off + j))
    return pl.pallas_call(
        functools.partial(attn_fwd_kernel, tile),
        grid=(pairs,),
        in_specs=[pl.BlockSpec(memory_space=pltpu.SMEM), spec(0), spec(pairs), spec(2 * pairs)],
        out_specs=[spec(0), spec(0)],
        out_shape=[jax.ShapeDtypeStruct((length, width), BF16), jax.ShapeDtypeStruct((length, width), F32)],
        compiler_params=params(32),
        cost_estimate=cost(8 * length * length * width, 10 * length * width),
        name="attn_fwd",
    )(flag, qkv, qkv, qkv)


def attn_bwd_kernel(tile, flag_ref, q_ref, k_ref, v_ref, g_ref, lse_ref, o_ref):
    length = q_ref.shape[0]
    width = o_ref.shape[1] // 3
    flag = flag_ref[0]
    lane = lax.broadcasted_iota(jnp.int32, (1, PAIR), 1)
    first = lane < HEAD
    scale = HEAD ** (-0.5)
    starts = list(range(0, length, tile))
    dk = [None] * len(starts)
    dv = [None] * len(starts)
    col = pl.multiple_of(pl.program_id(0) * PAIR, PAIR)
    for i, row0 in enumerate(starts):
        cols = row0 + tile
        ok = allowed_block(flag, row0, tile, cols, length // SHORT_SEQS)
        q = q_ref[row0 : row0 + tile, :]
        g = g_ref[row0 : row0 + tile, :]
        lse = lse_ref[row0 : row0 + tile, :]
        k = k_ref[0:cols, :]
        v = v_ref[0:cols, :]
        dqs, dks, dvs = [], [], []
        for h in range(2):
            mine = first if h == 0 else jnp.logical_not(first)
            qh = jnp.where(mine, q, jnp.zeros_like(q))
            gh = jnp.where(mine, g, jnp.zeros_like(g))
            s = jnp.where(ok, dot_nt(qh, k) * scale, NEG)
            p = jnp.exp(s - lse[:, h * HEAD : h * HEAD + 1])
            dp = dot_nt(gh, v)
            centre = jnp.sum(p * dp, axis=-1, keepdims=True)
            ds = (p * (dp - centre)).astype(BF16)
            dqs.append(dot_nn(ds, k))
            dks.append(dot_tn(ds, qh))
            dvs.append(dot_tn(p.astype(BF16), gh))
        o_ref[row0 : row0 + tile, pl.ds(col, PAIR)] = (
            jnp.where(first, dqs[0], dqs[1]) * scale
        ).astype(BF16)
        dk_all = dks[0] + dks[1]
        dv_all = dvs[0] + dvs[1]
        for j in range(i + 1):
            part_k = dk_all[j * tile : (j + 1) * tile]
            part_v = dv_all[j * tile : (j + 1) * tile]
            dk[j] = part_k if dk[j] is None else dk[j] + part_k
            dv[j] = part_v if dv[j] is None else dv[j] + part_v
    for j, row0 in enumerate(starts):
        o_ref[row0 : row0 + tile, pl.ds(width + col, PAIR)] = (dk[j] * scale).astype(BF16)
        o_ref[row0 : row0 + tile, pl.ds(2 * width + col, PAIR)] = dv[j].astype(BF16)


def attention_backward(qkv, flag, grad, lse, tile=256):
    length, width = qkv.shape[0], qkv.shape[1] // 3
    pairs = width // PAIR
    spec = lambda off: pl.BlockSpec((length, PAIR), lambda j: (0, off + j))
    return pl.pallas_call(
        functools.partial(attn_bwd_kernel, tile),
        grid=(pairs,),
        in_specs=[
            pl.BlockSpec(memory_space=pltpu.SMEM),
            spec(0),
            spec(pairs),
            spec(2 * pairs),
            spec(0),
            spec(0),
        ],
        out_specs=pl.BlockSpec((length, 3 * width), lambda j: (0, 0)),
        out_shape=jax.ShapeDtypeStruct((length, 3 * width), BF16),
        compiler_params=params(40),
        cost_estimate=cost(length, length),
        name="attn_bwd",
    )(flag, qkv, qkv, qkv, grad, lse)


def dense_kernel(mid_ref, dg_ref, up_ref, down_ref, out_ref, mg_ref, wu_ref, wd_ref):
    mid = mid_ref[...]
    dg = dg_ref[...]
    up = up_ref[...]
    down = down_ref[...]
    act, slope = gelu_pair(dot_nn(mid, up))
    act = act.astype(BF16)
    pg = (dot_nt(dg, down) * slope).astype(BF16)
    out = dot_nn(act, down)
    mg = dot_nt(pg, up)
    wu_ref[...] = dot_tn(mid, pg).astype(BF16)
    wd_ref[...] = dot_tn(act, dg).astype(BF16)

    @pl.when(pl.program_id(0) == 0)
    def _():
        out_ref[...] = out
        mg_ref[...] = mg

    @pl.when(pl.program_id(0) > 0)
    def _():
        out_ref[...] += out
        mg_ref[...] += mg


def dense_branch(mid, dg, up, down, tile=1024):
    length, width = mid.shape
    ff = up.shape[1]
    whole = pl.BlockSpec((length, width), lambda j: (0, 0))
    cols = pl.BlockSpec((width, tile), lambda j: (0, j))
    rows = pl.BlockSpec((tile, width), lambda j: (j, 0))
    return pl.pallas_call(
        dense_kernel,
        grid=(ff // tile,),
        in_specs=[whole, whole, cols, rows],
        out_specs=[whole, whole, cols, rows],
        out_shape=[
            jax.ShapeDtypeStruct((length, width), F32),
            jax.ShapeDtypeStruct((length, width), F32),
            jax.ShapeDtypeStruct((width, ff), BF16),
            jax.ShapeDtypeStruct((ff, width), BF16),
        ],
        compiler_params=params(48),
        cost_estimate=cost(length, length),
        name="dense_branch",
    )(mid, dg, up, down)


def expert_kernel(mid_ref, g_ref, mix_ref, up_ref, down_ref, po_ref, pi_ref, act_ref, pg_ref, eg_ref, dot_ref):
    mid = mid_ref[...]
    g = g_ref[...].astype(F32)
    logits = dot_nn(mid, mix_ref[...])
    share = 1.0 / (1.0 + jnp.exp(logits[:, 0:1] - logits[:, 1:2]))
    eg = (share * g).astype(BF16)
    eg_ref[...] = eg
    act, slope = gelu_pair(dot_nn(mid, up_ref[...]))
    act = act.astype(BF16)
    act_ref[...] = act
    pg = (dot_nt(eg, down_ref[...]) * slope).astype(BF16)
    pg_ref[...] = pg
    pi_ref[...] = dot_nt(pg, up_ref[...]).astype(BF16)
    po = dot_nn(act, down_ref[...])
    po_ref[...] = po.astype(BF16)
    dot_ref[...] = jnp.sum(po * g, axis=-1, keepdims=True)


def expert_chunk(mid, g, mix_pad, up, down, tile=320):
    rows, width = mid.shape
    hidden = up.shape[1]
    block = pl.BlockSpec((tile, width), lambda i: (i, 0))
    hblock = pl.BlockSpec((tile, hidden), lambda i: (i, 0))
    full = lambda a: pl.BlockSpec(a.shape, lambda i: (0, 0))
    return pl.pallas_call(
        expert_kernel,
        grid=(rows // tile,),
        in_specs=[block, block, full(mix_pad), full(up), full(down)],
        out_specs=[block, block, hblock, hblock, block, pl.BlockSpec((tile, 1), lambda i: (i, 0))],
        out_shape=[
            jax.ShapeDtypeStruct((rows, width), BF16),
            jax.ShapeDtypeStruct((rows, width), BF16),
            jax.ShapeDtypeStruct((rows, hidden), BF16),
            jax.ShapeDtypeStruct((rows, hidden), BF16),
            jax.ShapeDtypeStruct((rows, width), BF16),
            jax.ShapeDtypeStruct((rows, 1), F32),
        ],
        compiler_params=params(48),
        cost_estimate=cost(8 * rows * width * hidden, 14 * rows * width + 4 * width * hidden),
        name="expert_chunk",
    )(mid, g, mix_pad, up, down)


def expert_grad_kernel(count, *refs):
    mids, pgs, acts, egs = (refs[i * count : (i + 1) * count] for i in range(4))
    du_ref, dd_ref = refs[4 * count :]
    up_sum = dot_tn(mids[0][...], pgs[0][...])
    down_sum = dot_tn(acts[0][...], egs[0][...])
    for i in range(1, count):
        up_sum += dot_tn(mids[i][...], pgs[i][...])
        down_sum += dot_tn(acts[i][...], egs[i][...])
    du_ref[...] = up_sum
    dd_ref[...] = down_sum


def expert_weight_grads(mids, pgs, acts, egs, tile=256):
    count = len(mids)
    rows, width = mids[0].shape
    hidden = pgs[0].shape[1]
    full = lambda a: pl.BlockSpec(a.shape, lambda j: (0, 0))
    cols = lambda a: pl.BlockSpec((a.shape[0], tile), lambda j: (0, j))
    return pl.pallas_call(
        functools.partial(expert_grad_kernel, count),
        grid=(hidden // tile,),
        in_specs=[full(a) for a in mids]
        + [cols(a) for a in pgs]
        + [cols(a) for a in acts]
        + [full(a) for a in egs],
        out_specs=[
            pl.BlockSpec((width, tile), lambda j: (0, j)),
            pl.BlockSpec((tile, width), lambda j: (j, 0)),
        ],
        out_shape=[jax.ShapeDtypeStruct((width, hidden), F32), jax.ShapeDtypeStruct((hidden, width), F32)],
        compiler_params=params(48),
        cost_estimate=cost(4 * count * rows * width * hidden, 8 * count * rows * width + 8 * width * hidden),
        name="expert_weight_grads",
    )(*mids, *pgs, *acts, *egs)


def exchange_kernel(
    waves, layers, groups, slots_ref, *refs
):
    gathered = 2 * layers - 1
    g_low = [refs[0], *refs[1:layers]]
    g_high = [refs[0], *refs[layers:gathered]]
    mix_ref, up_ref, down_ref, back_ref, slab_ref = refs[gathered : gathered + 5]
    po_refs = refs[gathered + 5 : gathered + layers + 5]
    (
        du_ref, dd_ref, g_refs, buf, part, got, act_s, pg_s, eg_s, home, home_slab,
        g_sem, a_send, a_recv, z_send, z_recv, r_send, r_recv, b_send, b_recv,
    ) = refs[gathered + layers + 5 :]
    each = groups // waves
    capacity, width = slots_ref.shape[1:]
    rows = each * capacity
    last = layers - 1
    here, me = lax.axis_index("dp"), lax.axis_index("ep")
    up_id, down_id = lax.rem(here + 1, layers), lax.rem(here + last, layers)
    peer = lambda j: lax.rem(me + j, groups)
    source = lambda j: lax.rem(me + groups - j, groups)
    mesh_id = pl.DeviceIdType.MESH

    def a_copy(j):
        return pltpu.make_async_remote_copy(
            slots_ref.at[peer(j)], buf.at[j // each, 0, lax.rem(j, each)],
            a_send.at[j], a_recv.at[j], device_id={"ep": peer(j)}, device_id_type=mesh_id,
        )

    def z_copy(w, way, s):
        src, dst = ((layers - s + 1) % layers, layers - s) if way == 0 else (s - 1, s)
        return [
            pltpu.make_async_remote_copy(
                buf.at[w, src], buf.at[w, dst], z_send.at[w, way, s - 1], z_recv.at[w, way, s - 1],
                device_id={"dp": up_id if way == 0 else down_id}, device_id_type=mesh_id,
            )
        ]

    lanes = -(-rows // 128) * 128
    main, extra_rows = pl.ds(0, rows), pl.ds(rows, 16)

    def r_copy(w, way, s):
        k = layers - s if way == 0 else s
        return [
            pltpu.make_async_remote_copy(
                src, dst, r_send.at[w, way, s - 1, n], r_recv.at[w, way, s - 1, n],
                device_id={"dp": up_id if way == 0 else down_id}, device_id_type=mesh_id,
            )
            for n, (src, dst) in enumerate(
                (
                    (part.at[w, k, main], got.at[w, way, s - 1, main]),
                    (
                        part.at[w, k, extra_rows, pl.ds(0, lanes)],
                        got.at[w, way, s - 1, extra_rows, pl.ds(0, lanes)],
                    ),
                )
            )
        ]

    def b_copies(j):
        w, i = j // each, lax.rem(j, each)
        start = pl.multiple_of(i * capacity, 16)
        return [
            pltpu.make_async_remote_copy(
                src, dst, b_send.at[j, n], b_recv.at[j, n],
                device_id={"ep": source(j)}, device_id_type=mesh_id,
            )
            for n, (src, dst) in enumerate(
                (
                    (part.at[w, 0, pl.ds(start, capacity)], home.at[j]),
                    (part.at[w, 0, extra_rows, pl.ds(0, lanes)], home_slab.at[j]),
                )
            )
        ]

    def z_sends(way, s):
        if way == 0:
            return jnp.logical_and(here <= last - 1, here >= s - 1)
        return jnp.logical_and(here >= 1, here <= layers - s)

    def z_gets(way, s):
        return here >= s if way == 0 else here <= last - s

    def r_sends(way, s):
        return here <= s - 1 if way == 0 else here >= layers - s

    def r_gets(way, s):
        if way == 0:
            return jnp.logical_and(here >= 1, here <= s)
        return jnp.logical_and(here >= last - s, here <= last - 1)

    def g_copy(ref, k):
        return pltpu.make_async_copy(ref, g_refs.at[k], g_sem.at[k])

    for k in range(layers):
        pl.when(here + k <= last)(lambda k=k: g_copy(g_high[k], k).start())
        if k:
            pl.when(here + k > last)(lambda k=k: g_copy(g_low[layers - k], k).start())

    part[...] = jnp.zeros_like(part)
    got[:, :, last - 1] = jnp.zeros_like(got[:, :, last - 1])
    du_ref[...] = jnp.zeros_like(du_ref)
    dd_ref[...] = jnp.zeros_like(dd_ref)

    barrier = pltpu.get_barrier_semaphore()

    def greet(j, carry):
        pl.semaphore_signal(barrier, inc=1, device_id={"ep": peer(j)}, device_id_type=mesh_id)
        return carry

    lax.fori_loop(1, groups, greet, 0)

    @pl.when(here < last)
    def _():
        pl.semaphore_signal(barrier, inc=1, device_id={"dp": up_id}, device_id_type=mesh_id)

    @pl.when(here > 0)
    def _():
        pl.semaphore_signal(barrier, inc=1, device_id={"dp": down_id}, device_id_type=mesh_id)

    pl.semaphore_wait(barrier, groups - 1 + jnp.where(here < last, 1, 0) + jnp.where(here > 0, 1, 0))

    def over(first, count, act):
        lax.fori_loop(first, count, lambda j, c: (act(j), c)[1], 0)

    over(1, groups, lambda j: a_copy(j).start())
    buf[0, 0, 0] = slots_ref[me]
    for k in range(layers):
        g_copy(g_high[k], k).wait()

    def slab_of(row):
        high = row.astype(BF16).astype(F32)
        line = lax.broadcasted_iota(jnp.int32, (16, rows), 0)
        return jnp.where(line == 0, high, jnp.where(line == 1, row - high, 0.0)).astype(BF16)

    def piece(w, ks):
        mid = jnp.concatenate([buf[w, k].reshape(rows, width) for k in ks], axis=0)
        g = jnp.concatenate(
            [g_refs[k, source(w * each + i)] for k in ks for i in range(each)], axis=0
        ).astype(F32)
        logits = dot_nn(mid, mix_ref[...])
        share = 1.0 / (1.0 + jnp.exp(logits[:, 0:1] - logits[:, 1:2]))
        eg = (share * g).astype(BF16)
        act, slope = gelu_pair(dot_nn(mid, up_ref[...]))
        act = act.astype(BF16)
        pg = (dot_nt(eg, down_ref[...]) * slope).astype(BF16)
        pi = dot_nt(pg, up_ref[...]).astype(BF16)
        po = dot_nn(act, down_ref[...])
        sums = jnp.sum(po * g, axis=-1, keepdims=True)
        po = po.astype(BF16)
        diag = lax.broadcasted_iota(jnp.int32, (rows, rows), 0) == lax.broadcasted_iota(
            jnp.int32, (rows, rows), 1
        )
        for n, k in enumerate(ks):
            mine = slice(n * rows, (n + 1) * rows)
            spot = slice(k * rows, (k + 1) * rows)
            eg_s[spot] = eg[mine]
            act_s[spot] = act[mine]
            pg_s[spot] = pg[mine]
            part[w, k, 0:rows] = pi[mine]
            line = jnp.sum(jnp.where(diag, sums[mine], 0.0), axis=0, keepdims=True)
            part[w, k, rows : rows + 16, 0:rows] = slab_of(line)
            for i in range(each):
                at = n * rows + i * capacity
                po_refs[k][source(w * each + i)] = po[at : at + capacity]

    def weight_grads(w):
        mid = buf[w].reshape(layers * rows, width)
        du_ref[...] += dot_tn(mid, pg_s[...])
        dd_ref[...] += dot_tn(act_s[...], eg_s[...])

    def add_to(w, k, pieces):
        total = part[w, k, 0:rows].astype(F32)
        extra = part[w, k, rows : rows + 16, 0:rows].astype(F32)
        for way, s in pieces:
            total = total + got[w, way, s - 1, 0:rows].astype(F32)
            extra = extra + got[w, way, s - 1, rows : rows + 16, 0:rows].astype(F32)
        part[w, k, 0:rows] = total.astype(BF16)
        part[w, k, rows : rows + 16, 0:rows] = slab_of(jnp.sum(extra, axis=0, keepdims=True))

    def start_hop(copy, sends, w, s):
        for way in range(2):
            pl.when(sends(way, s))(lambda way=way: [c.start() for c in copy(w, way, s)][:0] or None)

    def get_hop(copy, gets, w, s):
        for way in range(2):
            pl.when(gets(way, s))(lambda way=way: [c.wait_recv() for c in copy(w, way, s)][:0] or None)

    def pass_on(w, s):
        for way in range(2):

            @pl.when(r_gets(way, s))
            def _():
                for copy in r_copy(w, way, s):
                    copy.wait_recv()
                add_to(w, layers - s - 1 if way == 0 else s + 1, [(way, s)])

        start_hop(r_copy, r_sends, w, s + 1)

    def finish(w):
        get_hop(r_copy, r_gets, w, last)
        add_to(w, 0, [(0, last), (1, last)])
        for i in range(each):
            j = w * each + i
            start = i * capacity

            @pl.when(j > 0)
            def _():
                for copy in b_copies(j):
                    copy.start()

            @pl.when(j == 0)
            def _():
                home[0] = part[0, 0, start : start + capacity]
                home_slab[0] = part[0, 0, rows : rows + 16, 0:lanes]

    def first_hop(w):
        for n in range(each):
            pl.when(w * each + n > 0)(lambda n=n: a_copy(w * each + n).wait_recv())
        start_hop(z_copy, z_sends, w, 1)

    far = [1, last]
    near = [k for k in range(layers) if k not in far]

    def valid(w):
        return jnp.logical_and(w >= 0, w < waves)

    def body(t, carry):
        for s in range(1, layers):
            pl.when(valid(t - s))(lambda s=s: get_hop(z_copy, z_gets, t - s, s))
        for s in range(2, layers):
            pl.when(valid(t + 1 - s))(lambda s=s: start_hop(z_copy, z_sends, t + 1 - s, s))
        pl.when(t + 1 < waves)(lambda: first_hop(t + 1))
        w = t - last

        @pl.when(valid(w))
        def _():
            piece(w, far)
            start_hop(r_copy, r_sends, w, 1)

        for s in range(1, last):
            pl.when(valid(w - s))(lambda s=s: pass_on(w - s, s))
        pl.when(valid(w - last))(lambda: finish(w - last))

        @pl.when(valid(w))
        def _():
            piece(w, near)
            weight_grads(w)

        return carry

    first_hop(0)
    lax.fori_loop(0, waves + 2 * last, body, 0)

    def land(j, carry):
        for copy in b_copies(j):
            copy.wait_recv()
            copy.wait_send()
        a_copy(j).wait_send()
        return carry

    lax.fori_loop(1, groups, land, 0)

    def sent(w, carry):
        for way in range(2):
            for s in range(1, layers):
                for copy, sends in ((z_copy, z_sends), (r_copy, r_sends)):

                    @pl.when(sends(way, s))
                    def _():
                        for one in copy(w, way, s):
                            one.wait_send()

        return carry

    lax.fori_loop(0, waves, sent, 0)

    def arrange(j, carry):
        back_ref[peer(j)] = home[j]
        slab_ref[peer(j)] = home_slab[j]
        return carry

    lax.fori_loop(0, groups, arrange, 0)


def exchange_waves(groups):
    return 8 if groups % 8 == 0 else 1


def expert_exchange(slots, g_low, g_high, mix_pad, up, down):
    layers, groups = lax.axis_size("dp"), lax.axis_size("ep")
    waves = exchange_waves(groups)
    each = groups // waves
    _, capacity, width = slots.shape
    hidden = up.shape[1]
    rows = each * capacity
    lanes = -(-rows // 128) * 128
    sem = pltpu.SemaphoreType.DMA
    block = jax.ShapeDtypeStruct((groups, capacity, width), BF16)
    vmem = pl.BlockSpec(memory_space=pltpu.VMEM)
    total_rows = layers * groups * capacity
    outs = pl.pallas_call(
        functools.partial(exchange_kernel, waves, layers, groups),
        in_specs=[vmem] + [pl.BlockSpec(memory_space=pl.ANY)] * (2 * layers - 1) + [vmem] * 3,
        out_specs=[vmem] * (4 + layers),
        out_shape=[block, jax.ShapeDtypeStruct((groups, 16, lanes), BF16)]
        + [block] * layers
        + [jax.ShapeDtypeStruct((width, hidden), F32), jax.ShapeDtypeStruct((hidden, width), F32)],
        scratch_shapes=[
            pltpu.VMEM((layers, groups, capacity, width), BF16),
            pltpu.VMEM((waves, layers, each, capacity, width), BF16),
            pltpu.VMEM((waves, layers, rows + 16, width), BF16),
            pltpu.VMEM((waves, 2, layers - 1, rows + 16, width), BF16),
            pltpu.VMEM((layers * rows, hidden), BF16),
            pltpu.VMEM((layers * rows, hidden), BF16),
            pltpu.VMEM((layers * rows, width), BF16),
            pltpu.VMEM((groups, capacity, width), BF16),
            pltpu.VMEM((groups, 16, lanes), BF16),
            sem((layers,)),
            sem((groups,)),
            sem((groups,)),
            sem((waves, 2, layers - 1)),
            sem((waves, 2, layers - 1)),
            sem((waves, 2, layers - 1, 2)),
            sem((waves, 2, layers - 1, 2)),
            sem((groups, 2)),
            sem((groups, 2)),
        ],
        compiler_params=pltpu.CompilerParams(
            collective_id=0, has_side_effects=True, vmem_limit_bytes=62 << 20
        ),
        cost_estimate=cost(12 * total_rows * width * hidden, 20 * total_rows * width),
        name="expert_exchange",
    )(slots, *g_low, *g_high[1:], mix_pad, up, down)
    return outs[0], outs[1], outs[2 : 2 + layers], outs[2 + layers], outs[3 + layers]


def sums_kernel(plan, split, layers, groups, small_ref, *refs):
    count = len(plan)
    mats, outs = refs[:count], refs[count : 2 * count]
    (
        small_out, own, sib, got, held, inner, final, small_two, small_chip, small_layer,
        own_sem, s_send, s_recv, x_send, x_recv, z_send, z_recv, t_send, t_recv, o_sem,
    ) = refs[2 * count :]
    chips = groups // 2
    width = held.shape[-1]
    total = held.shape[0]
    last = layers - 1
    here, me = lax.axis_index("dp"), lax.axis_index("ep")
    core, chip = lax.rem(me, 2), me // 2
    sibling = me + 1 - 2 * core
    mesh_id = pl.DeviceIdType.MESH
    chip_at = lambda j: lax.rem(chip + j, chips)
    pieces = [(m, i, n) for m in range(count) for i in range(plan[m]) for n in range(split)]
    lines = held.shape[1]
    square = chips == 4
    by_one = chip + 1 - 2 * lax.rem(chip, 2)
    by_two = chip + 2 - 4 * (chip // 2)
    at_end = jnp.logical_or(here == 0, here == last)
    inside = jnp.logical_and(here > 0, here < last)
    inward = 1 + (here // last) * (last - 2)
    outward = lax.rem((here - 1) * last + layers * last, layers)
    across = last - here

    def source(m, i, n, half):
        span = pl.ds(n * lines, lines)
        if len(mats[m].shape) == 5:
            return mats[m].at[:, half, i, span]
        return mats[m].at[:, half, span, pl.ds(i * width, width)]

    def remote(src, dst, send, recv, where):
        return pltpu.make_async_remote_copy(
            src, dst, send, recv, device_id=where, device_id_type=mesh_id
        )

    def s_copy(c):
        return remote(source(*pieces[c], 1 - core), sib.at[c], s_send.at[c], s_recv.at[c], {"ep": sibling})

    def x_copy(c, j):
        return remote(
            own.at[c, chip_at(j)], got.at[c, j - 1], x_send.at[c, j - 1], x_recv.at[c, j - 1],
            {"ep": 2 * chip_at(j) + core},
        )

    def near_chip(c):
        return by_one + lax.rem(c, 2) * (by_two - by_one)

    def next_chip(c):
        return by_two + lax.rem(c, 2) * (by_one - by_two)

    def y_copy(c, n):
        block = (near_chip(c), 3 - chip, next_chip(c))[n]
        where = next_chip(c) if n == 2 else near_chip(c)
        return remote(
            own.at[c, block], got.at[c, n], x_send.at[c, n], x_recv.at[c, n], {"ep": 2 * where + core}
        )

    lags = [LAG * n for n in range(1, 6)] if square else [0] + [LAG * n for n in range(1, 5)]

    def due(t, n):
        return jnp.logical_and(t >= lags[n], t < total + lags[n])

    def z_copy(c, n):
        src = (held, held, inner)[n]
        dst = (inner, final, final)[n]
        where = (inward, across, outward)[n]
        return remote(src.at[c], dst.at[c], z_send.at[c, n], z_recv.at[c, n], {"dp": where})

    def t_copy(n, j):
        if n == 0:
            return remote(small_ref, small_two, t_send.at[0, 0], t_recv.at[0, 0], {"ep": sibling})
        if n == 1:
            spot = small_chip.at[chip]
            return remote(spot, spot, t_send.at[1, j], t_recv.at[1, j], {"ep": 2 * chip_at(j) + core})
        spot = small_layer.at[here]
        return remote(
            spot, spot, t_send.at[2, j], t_recv.at[2, j], {"dp": lax.rem(here + j, layers)}
        )

    for c in range(total):
        pltpu.make_async_copy(source(*pieces[c], core), own.at[c], own_sem.at[c]).start()

    barrier = pltpu.get_barrier_semaphore()
    pl.semaphore_signal(barrier, inc=1, device_id={"ep": sibling}, device_id_type=mesh_id)

    def over(first, end, act):
        def step(j, carry):
            act(j)
            return carry

        lax.fori_loop(first, end, step, 0)

    over(
        1,
        chips,
        lambda j: pl.semaphore_signal(
            barrier, inc=1, device_id={"ep": 2 * chip_at(j) + core}, device_id_type=mesh_id
        ),
    )
    over(
        1,
        layers,
        lambda j: pl.semaphore_signal(
            barrier, inc=1, device_id={"dp": lax.rem(here + j, layers)}, device_id_type=mesh_id
        ),
    )
    pl.semaphore_wait(barrier, chips + last)

    t_copy(0, 0).start()
    for c in range(total):
        s_copy(c).start()

    def body(t, carry):
        @pl.when(t < total)
        def _():
            pltpu.make_async_copy(sib.at[t], own.at[t], own_sem.at[t]).wait()
            remote(own.at[t], sib.at[t], s_send.at[t], s_recv.at[t], {"ep": sibling}).wait_recv()

            def add(p):
                own[t, p] = own[t, p] + sib[t, p]

            over(0, chips, add)
            if square:
                y_copy(t, 1).start()
                y_copy(t, 0).start()
            else:
                over(1, chips, lambda j: x_copy(t, j).start())

        if square:

            @pl.when(due(t, 0))
            def _():
                c = t - lags[0]
                y_copy(c, 1).wait_recv()
                own[c, next_chip(c)] = own[c, next_chip(c)] + got[c, 1]
                y_copy(c, 2).start()
                y_copy(c, 0).wait_recv()
                own[c, chip] = own[c, chip] + got[c, 0]

        @pl.when(due(t, 1))
        def _():
            c = t - lags[1]
            if square:
                y_copy(c, 2).wait_recv()
                held[c] = own[c, chip] + got[c, 2]
            else:
                over(1, chips, lambda j: x_copy(c, j).wait_recv())
                held[c] = lax.fori_loop(
                    1, chips, lambda j, acc: acc + got[c, j - 1].astype(F32), own[c, chip].astype(F32)
                ).astype(BF16)
            pl.when(at_end)(lambda: z_copy(c, 0).start())

        @pl.when(jnp.logical_and(inside, due(t, 2)))
        def _():
            c = t - lags[2]
            z_copy(c, 0).wait_recv()
            held[c] = held[c] + inner[c]
            z_copy(c, 1).start()

        @pl.when(jnp.logical_and(inside, due(t, 3)))
        def _():
            c = t - lags[3]
            z_copy(c, 1).wait_recv()
            inner[c] = held[c] + final[c]
            z_copy(c, 2).start()

        @pl.when(jnp.logical_and(at_end, due(t, 4)))
        def _():
            c = t - lags[4]
            z_copy(c, 2).wait_recv()

        @pl.when(t == 1)
        def _():
            t_copy(0, 0).wait_recv()
            small_chip[chip] = small_ref[...] + small_two[...]
            over(1, chips, lambda j: t_copy(1, j).start())

        @pl.when(t == 3)
        def _():
            over(1, chips, lambda j: t_copy(1, j).wait_recv())
            acc = small_chip[0]
            for n in range(1, chips):
                acc = acc + small_chip[n]
            small_layer[here] = acc
            over(1, layers, lambda j: t_copy(2, j).start())

        return carry

    lax.fori_loop(0, total + lags[4], body, 0)

    def result(sums, c):
        m, i, n = pieces[c]
        span = pl.ds(n * lines, lines)
        if len(outs[m].shape) == 3:
            spot = outs[m].at[i, span]
        else:
            spot = outs[m].at[span, pl.ds(i * width, width)]
        return pltpu.make_async_copy(sums.at[c], spot, o_sem.at[c])

    @pl.when(inside)
    def _():
        for c in range(total):
            result(inner, c).start()

    @pl.when(at_end)
    def _():
        for c in range(total):
            result(final, c).start()

    over(1, layers, lambda j: t_copy(2, j).wait_recv())
    acc = small_layer[0]
    for n in range(1, layers):
        acc = acc + small_layer[n]
    small_out[...] = acc

    t_copy(0, 0).wait_send()
    over(1, chips, lambda j: t_copy(1, j).wait_send())
    over(1, layers, lambda j: t_copy(2, j).wait_send())

    def sent(c):
        remote(own.at[c], sib.at[c], s_send.at[c], s_recv.at[c], {"ep": sibling}).wait_send()
        if square:
            for n in range(3):
                y_copy(c, n).wait_send()
        else:
            over(1, chips, lambda j: x_copy(c, j).wait_send())
        pl.when(at_end)(lambda: z_copy(c, 0).wait_send())

        @pl.when(inside)
        def _():
            z_copy(c, 1).wait_send()
            z_copy(c, 2).wait_send()

    over(0, total, sent)
    for c in range(total):
        result(final, c).wait()


def gradient_sums(small, columns, rows_split):
    layers, groups = lax.axis_size("dp"), lax.axis_size("ep")
    chips = groups // 2
    width = small.shape[1]
    plan = [a.shape[1] // width for a in columns] + [a.shape[0] // width for a in rows_split]
    high = columns[0].shape[0] // groups
    split = SPLIT if high % (16 * SPLIT) == 0 else 1
    total, lines = sum(plan) * split, high // split
    views = [a.reshape(chips, 2, high, a.shape[1]) for a in columns] + [
        a.reshape(chips, 2, n, high, width) for a, n in zip(rows_split, plan[len(columns) :])
    ]
    shapes = [jax.ShapeDtypeStruct((high, a.shape[1]), BF16) for a in columns] + [
        jax.ShapeDtypeStruct((n, high, width), BF16) for n in plan[len(columns) :]
    ]
    sem = pltpu.SemaphoreType.DMA
    vmem = pl.BlockSpec(memory_space=pltpu.VMEM)
    anywhere = pl.BlockSpec(memory_space=pl.ANY)
    buffers = lambda *lead: pltpu.VMEM((total, *lead, lines, width), BF16)
    outs = pl.pallas_call(
        functools.partial(sums_kernel, plan, split, layers, groups),
        in_specs=[vmem] + [anywhere] * len(views),
        out_specs=[anywhere] * len(views) + [vmem],
        out_shape=shapes + [jax.ShapeDtypeStruct(small.shape, F32)],
        scratch_shapes=[
            buffers(chips),
            buffers(chips),
            buffers(chips - 1),
            buffers(),
            buffers(),
            buffers(),
            pltpu.VMEM(small.shape, F32),
            pltpu.VMEM((chips, *small.shape), F32),
            pltpu.VMEM((layers, *small.shape), F32),
            sem((total,)),
            sem((total,)),
            sem((total,)),
            sem((total, chips - 1)),
            sem((total, chips - 1)),
            sem((total, 3)),
            sem((total, 3)),
            sem((3, max(chips, layers))),
            sem((3, max(chips, layers))),
            sem((total,)),
        ],
        compiler_params=pltpu.CompilerParams(
            collective_id=1, has_side_effects=True, vmem_limit_bytes=62 << 20
        ),
        cost_estimate=cost(10 * total * chips * lines * width, 8 * total * chips * lines * width),
        name="gradient_sums",
    )(small, *views)
    rows_out = [a.reshape(-1, width) for a in outs[len(columns) : -1]]
    return (*outs[: len(columns)], *rows_out, outs[-1])


def normalise(values_in):
    centred = values_in - jnp.mean(values_in, axis=-1, keepdims=True)
    inverse = lax.rsqrt(jnp.mean(centred * centred, axis=-1, keepdims=True) + 1e-05)
    return centred * inverse, inverse


def norm_backward(grad, gain_vec, unit, inverse):
    m = grad * gain_vec
    return inverse * (
        m
        - jnp.mean(m, axis=-1, keepdims=True)
        - unit * jnp.mean(m * unit, axis=-1, keepdims=True)
    )


def hop(rows, step, stage):
    size = lax.axis_size("dp")
    if step > 0:
        pairs = [(i, i + 1) for i in range(stage - 1, size - 1)]
    else:
        pairs = [(i + 1, i) for i in range(0, size - stage)]
    return lax.ppermute(rows, "dp", pairs)


def both_hops(low, high, stage):
    return hop(low, 1, stage), hop(high, -1, stage)


def send_hop(rows, step, stage):
    size = lax.axis_size("dp")
    if step > 0:
        pairs = [(i, i + 1) for i in range(stage)]
    else:
        pairs = [(i, i - 1) for i in range(size - stage, size)]
    return lax.ppermute(rows, "dp", pairs)


def line_reduce(parts):
    size = lax.axis_size("dp")
    up = send_hop(parts[size - 1], 1, 1)
    down = send_hop(parts[1], -1, 1)
    for stage in range(2, size):
        up = send_hop(up + parts[size - stage], 1, stage)
        down = send_hop(down + parts[stage], -1, stage)
    return parts[0].astype(F32) + up.astype(F32) + down.astype(F32)


def shifted(rows, step):
    size = lax.axis_size("dp")
    return lax.ppermute(rows, "dp", [((i + step) % size, i) for i in range(size)])


def after(values, *earlier):
    many = isinstance(values, tuple)
    held = lax.optimization_barrier((*values, *earlier) if many else (values, *earlier))
    return held[: len(values)] if many else held[0]


def sum_layers(rows):
    size, here = lax.axis_size("dp"), lax.axis_index("dp")
    pieces = rows.reshape(size, rows.shape[0] // size, rows.shape[1])
    piece = lambda k: lax.dynamic_index_in_dim(pieces, lax.rem(here + k, size), 0, keepdims=False)
    acc = piece(0).astype(F32)
    for k in range(1, size):
        acc = acc + shifted(piece(k), size - k).astype(F32)
    mine = acc.astype(BF16)
    ring = jnp.stack([mine] + [shifted(mine, k) for k in range(1, size)])
    ordered = lax.dynamic_slice_in_dim(jnp.concatenate([ring, ring]), size - here, size, 0)
    return ordered.reshape(rows.shape).astype(F32)


def sum_everywhere(values):
    for axis in ("dp", "ep"):
        size = lax.axis_size(axis)
        step = 1
        while step < size:
            values = values + lax.ppermute(values, axis, [(i, i ^ step) for i in range(size)])
            step *= 2
    return values


def on_device(
    tokens,
    bucket,
    expert_ids,
    ln1_gain,
    qkv_weight,
    out_weight,
    ln2_gain,
    up_weight,
    down_weight,
    mix_weight,
    expert_up,
    expert_down,
    cotangent,
):
    length, width = tokens.shape
    groups = lax.axis_size("ep")
    layers = lax.axis_size("dp")
    experts = groups * expert_up.shape[0]
    capacity = 5 * length // (4 * experts)
    slots = experts * capacity
    gather = lambda w: lax.all_gather(w, "ep", axis=0, tiled=True)
    exchange_out = lambda a: lax.all_to_all(a, "ep", split_axis=0, concat_axis=1, tiled=True)
    expert_up2 = expert_up[0]
    expert_down2 = expert_down[0]
    mix_pad = jnp.pad(mix_weight, ((0, 0), (0, 126)))

    chosen = expert_ids[:, 0]
    one_hot = chosen[:, None] == jnp.arange(experts, dtype=jnp.int32)[None, :]
    place = jnp.arange(length, dtype=jnp.int32)
    earlier = (place[None, :] < place[:, None]).astype(BF16)
    before = dot_nn(earlier, one_hot.astype(BF16))
    slot_index = jnp.sum(jnp.where(one_hot, before, 0.0), axis=1).astype(jnp.int32)
    target = jnp.where(slot_index < capacity, chosen * capacity + slot_index, -1)
    table = (target[:, None] == jnp.arange(slots, dtype=jnp.int32)[None, :]).astype(BF16)

    pick = lambda rows: dot_tn(table, rows).astype(BF16).reshape(experts, capacity, width)
    join = lambda lows, highs: [highs[k] + lows[layers - k] for k in range(1, layers)]

    token_rows = tokens.astype(F32)
    unit1, inverse1 = normalise(token_rows)
    normed_in = (unit1 * ln1_gain).astype(BF16)
    g_own = exchange_out(pick(cotangent)).reshape(slots, width)
    normed_in, g_own, qkv_weight = lax.optimization_barrier((normed_in, g_own, qkv_weight))
    qkv_full, out_full, up_full, down_full = (
        gather(qkv_weight),
        gather(out_weight),
        gather(up_weight),
        gather(down_weight),
    )
    g_low, g_high = [g_own], [g_own]

    def step(lows, highs, *others):
        stage = len(lows)
        held = lax.optimization_barrier((lows[-1], highs[-1], *others))
        lows[-1], highs[-1] = held[:2]
        if stage < layers:
            low, high = both_hops(lows[-1], highs[-1], stage)
            lows.append(low)
            highs.append(high)
        return held[2:]

    step(g_low, g_high)
    (normed_in,) = step(g_low, g_high, normed_in)
    qkv_rows = dot_nn(normed_in, qkv_full).astype(BF16)
    (qkv_rows,) = step(g_low, g_high, qkv_rows)
    attended, lse = attention_forward(qkv_rows, bucket)
    hidden_res = token_rows + dot_nn(attended, out_full)
    unit2, inverse2 = normalise(hidden_res)
    mid_low = (unit2 * ln2_gain).astype(BF16)
    mid_slots = pick(mid_low)
    (mid_slots,) = step(g_low, g_high, mid_slots)

    grad_out = cotangent.astype(F32)
    logits = dot_nn(mid_low, mix_weight)
    mix1 = 1.0 / (1.0 + jnp.exp(logits[:, 0:1] - logits[:, 1:2]))
    mix0 = 1.0 / (1.0 + jnp.exp(logits[:, 1:2] - logits[:, 0:1]))
    dense_grad = (mix0 * grad_out).astype(BF16)
    scatter = lambda a: lax.psum_scatter(a.astype(BF16), "ep", scatter_dimension=0, tiled=True)
    back = lambda k, a: shifted(a, layers - k) if k else a

    def total(parts):
        acc = parts[0].astype(F32)
        for part in parts[1:]:
            acc = acc + part.astype(F32)
        return acc

    if capacity % 16 == 0:
        blocks = lambda many: [g.reshape(groups, capacity, width) for g in many]
        returned, slab, partial_outs, expert_up_grad, expert_down_grad = expert_exchange(
            mid_slots, blocks(g_low), blocks(g_high), mix_pad, expert_up2, expert_down2
        )
        each = groups // exchange_waves(groups)
        offset = lax.rem(
            jnp.arange(groups, dtype=jnp.int32) + groups - lax.axis_index("ep"), groups
        )
        spot = lax.rem(offset, each)[:, None] == jnp.arange(each, dtype=jnp.int32)[None, :]
        lines = slab[:, 0, : each * capacity].astype(F32) + slab[:, 1, : each * capacity].astype(F32)
        dot_back = jnp.sum(
            jnp.where(spot[:, :, None], lines.reshape(groups, each, capacity), 0.0), axis=1
        ).reshape(1, slots)
        dense_grad, returned = lax.optimization_barrier((dense_grad, returned))
        outs = [a.reshape(slots, width) for a in partial_outs]
    else:
        gs = [g_own] + join(g_low, g_high)
        mid_own = exchange_out(mid_slots).reshape(slots, width)
        mids = [mid_own] + [shifted(mid_own, k) for k in range(1, layers)]
        chunks = [expert_chunk(mids[k], gs[k], mix_pad, expert_up2, expert_down2) for k in range(layers)]
        in_total = line_reduce([c[1] for c in chunks])
        dot_sum = total([back(k, chunks[k][5].reshape(groups, capacity)) for k in range(layers)])
        dot_high = lax.reduce_precision(dot_sum, 8, 7)
        extra = jnp.stack([dot_high, dot_sum - dot_high], axis=1)
        extra = jnp.pad(extra, ((0, 0), (0, 14), (0, width - capacity)))
        packed = jnp.concatenate([in_total.reshape(groups, capacity, width), extra], axis=1)
        both = lax.all_to_all(packed.astype(BF16), "ep", split_axis=0, concat_axis=0, tiled=True)
        returned = both[:, :capacity]
        dot_back = (
            both[:, capacity, :capacity].astype(F32) + both[:, capacity + 1, :capacity].astype(F32)
        ).reshape(1, slots)
        outs = [c[0] for c in chunks]
        expert_up_grad, expert_down_grad = expert_weight_grads(
            mids, [c[3] for c in chunks], [c[2] for c in chunks], [c[4] for c in chunks]
        )

    outs = [back(k, outs[k]) for k in range(layers)]
    dense_out, mid_grad_dense, up_grad, down_grad = dense_branch(mid_low, dense_grad, up_full, down_full)
    in_rows = returned.reshape(slots, width)
    mix_dot1 = jnp.sum(table.astype(F32) * dot_back, axis=1, keepdims=True)
    mix_dot0 = jnp.sum(grad_out * dense_out, axis=-1, keepdims=True)
    mean_dot = mix0 * mix_dot0 + mix1 * mix_dot1
    logit_grad = jnp.concatenate(
        [mix0 * (mix_dot0 - mean_dot), mix1 * (mix_dot1 - mean_dot)], axis=1
    ).astype(BF16)
    mix_weight_grad = dot_tn(mid_low, logit_grad)
    mid_grad = mid_grad_dense + dot_nt(logit_grad, mix_weight) + dot_nn(table, in_rows)
    ln2_gain_grad = jnp.sum(mid_grad * unit2, axis=0)
    res_grad = grad_out + norm_backward(mid_grad, ln2_gain, unit2, inverse2)
    attn_out_grad = res_grad.astype(BF16)
    out_weight_grad = dot_tn(attended, attn_out_grad)
    attended_grad = dot_nt(attn_out_grad, out_full).astype(BF16)
    qkv_grad = attention_backward(qkv_rows, bucket, attended_grad, lse)
    qkv_weight_grad = dot_tn(normed_in, qkv_grad)
    normed_grad = dot_nt(qkv_grad, qkv_full)
    ln1_gain_grad = jnp.sum(normed_grad * unit1, axis=0)
    tokens_grad = res_grad + norm_backward(normed_grad, ln1_gain, unit1, inverse1)

    small = jnp.concatenate([ln1_gain_grad[None], ln2_gain_grad[None], mix_weight_grad.T], axis=0)
    small = jnp.pad(small, ((0, 4), (0, 0)))
    if layers == 4 and length // groups >= 16:
        qkv_final, out_final, up_final, down_final, small_sums = gradient_sums(
            small,
            [a.astype(BF16) for a in (qkv_weight_grad, out_weight_grad, up_grad)],
            [down_grad],
        )
    else:
        sums = [sum_layers(scatter(a)) for a in (qkv_weight_grad, out_weight_grad, up_grad, down_grad)]
        qkv_final, out_final, up_final, down_final = sums
        small_sums = sum_everywhere(small)
    outs = list(after(tuple(outs), small_sums))
    out_sum = total(outs).astype(BF16).reshape(groups, capacity, width)
    out_back = lax.all_to_all(out_sum, "ep", split_axis=0, concat_axis=0, tiled=True)
    bucket, qkv_final, out_final, up_final, down_final = after(
        (bucket, qkv_final, out_final, up_final, down_final), out_sum
    )
    unit = jnp.where(bucket[0] < 0, 0.0, 1.0)
    expert_up_grad, expert_down_grad, qkv_final, out_final, up_final, down_final, out_back = (
        lax.optimization_barrier(
            (
                expert_up_grad * unit,
                expert_down_grad * unit,
                *(a.astype(F32) for a in (qkv_final, out_final, up_final, down_final)),
                out_back,
            )
        )
    )
    expert_out = dot_nn(table, out_back.reshape(slots, width))
    result = (hidden_res + mix0 * dense_out + mix1 * expert_out).astype(BF16)
    return (
        result,
        tokens_grad,
        small_sums[0],
        qkv_final,
        out_final,
        small_sums[1],
        up_final,
        down_final,
        small_sums[2:4].T,
        expert_up_grad[None],
        expert_down_grad[None],
    )


def solution(mesh):
    placed = (
        P(("dp", "ep"), None),
        P(("dp", "ep")),
        P(("dp", "ep"), None),
        P(),
        P("ep", None),
        P("ep", None),
        P(),
        P("ep", None),
        P("ep", None),
        P(),
        P("ep", None, "dp"),
        P("ep", "dp", None),
        P(("dp", "ep"), None),
    )
    return jax.shard_map(
        on_device,
        mesh=mesh,
        in_specs=placed,
        out_specs=(
            P(("dp", "ep"), None),
            P(("dp", "ep"), None),
            P(),
            P("ep", None),
            P("ep", None),
            P(),
            P("ep", None),
            P("ep", None),
            P(),
            P("ep", None, "dp"),
            P("ep", "dp", None),
        ),
        check_vma=False,
    )
```

```python
import functools

import jax
import jax.numpy as jnp
from jax import lax
from jax.experimental import pallas as pl
from jax.experimental.pallas import tpu as pltpu
from jax.sharding import PartitionSpec as P

HEAD = 64
SHORT_SEQS = 4
PAIR = 2 * HEAD
NEG = -1e30
SPLIT = 2
LAG = 2
ROOT = 0.7978845608028654
CUBE = 0.044715
F32 = jnp.float32
BF16 = jnp.bfloat16


def dot_nn(a, b):
    return lax.dot_general(a, b, (((1,), (0,)), ((), ())), preferred_element_type=F32)


def dot_nt(a, b):
    return lax.dot_general(a, b, (((1,), (1,)), ((), ())), preferred_element_type=F32)


def dot_tn(a, b):
    return lax.dot_general(a, b, (((0,), (0,)), ((), ())), preferred_element_type=F32)


def gelu_pair(v):
    sq = v * v
    t = jnp.tanh(v * (ROOT + (ROOT * CUBE) * sq))
    half = 0.5 * (1.0 + t)
    slope = half + (0.5 * v) * (1.0 - t * t) * (ROOT + (3.0 * ROOT * CUBE) * sq)
    return v * half, slope


def params(vmem_mib):
    return pltpu.CompilerParams(vmem_limit_bytes=vmem_mib << 20)


def cost(flops, nbytes):
    return pl.CostEstimate(flops=int(flops), bytes_accessed=int(nbytes), transcendentals=0)


def allowed_block(flag, row0, rows, cols, short):
    r = row0 + lax.broadcasted_iota(jnp.int32, (rows, cols), 0)
    c = lax.broadcasted_iota(jnp.int32, (rows, cols), 1)
    shift = short.bit_length() - 1
    same = jnp.logical_or(flag == 1, lax.shift_right_logical(r, shift) == lax.shift_right_logical(c, shift))
    return jnp.logical_and(c <= r, same)


def attn_fwd_kernel(tile, flag_ref, q_ref, k_ref, v_ref, o_ref, lse_ref):
    length = q_ref.shape[0]
    flag = flag_ref[0]
    lane = lax.broadcasted_iota(jnp.int32, (1, PAIR), 1)
    first = lane < HEAD
    scale = HEAD ** (-0.5)
    for row0 in range(0, length, tile):
        cols = row0 + tile
        ok = allowed_block(flag, row0, tile, cols, length // SHORT_SEQS)
        q = q_ref[row0 : row0 + tile, :]
        k = k_ref[0:cols, :]
        v = v_ref[0:cols, :]
        outs, lses = [], []
        for h in range(2):
            qh = jnp.where(first if h == 0 else jnp.logical_not(first), q, jnp.zeros_like(q))
            s = jnp.where(ok, dot_nt(qh, k) * scale, NEG)
            peak = jnp.max(s, axis=-1, keepdims=True)
            p = jnp.exp(s - peak)
            total = jnp.sum(p, axis=-1, keepdims=True)
            outs.append(dot_nn((p * (1.0 / total)).astype(BF16), v))
            lses.append(peak + jnp.log(total))
        o_ref[row0 : row0 + tile, :] = jnp.where(first, outs[0], outs[1]).astype(BF16)
        lse_ref[row0 : row0 + tile, :] = jnp.where(first, lses[0], lses[1])


def attention_forward(qkv, flag, tile=256):
    length, width = qkv.shape[0], qkv.shape[1] // 3
    pairs = width // PAIR
    spec = lambda off: pl.BlockSpec((length, PAIR), lambda j: (0, off + j))
    return pl.pallas_call(
        functools.partial(attn_fwd_kernel, tile),
        grid=(pairs,),
        in_specs=[pl.BlockSpec(memory_space=pltpu.SMEM), spec(0), spec(pairs), spec(2 * pairs)],
        out_specs=[spec(0), spec(0)],
        out_shape=[jax.ShapeDtypeStruct((length, width), BF16), jax.ShapeDtypeStruct((length, width), F32)],
        compiler_params=params(32),
        cost_estimate=cost(8 * length * length * width, 10 * length * width),
        name="attn_fwd",
    )(flag, qkv, qkv, qkv)


def attn_bwd_kernel(tile, flag_ref, q_ref, k_ref, v_ref, g_ref, lse_ref, o_ref):
    length = q_ref.shape[0]
    width = o_ref.shape[1] // 3
    flag = flag_ref[0]
    lane = lax.broadcasted_iota(jnp.int32, (1, PAIR), 1)
    first = lane < HEAD
    scale = HEAD ** (-0.5)
    starts = list(range(0, length, tile))
    dk = [None] * len(starts)
    dv = [None] * len(starts)
    col = pl.multiple_of(pl.program_id(0) * PAIR, PAIR)
    for i, row0 in enumerate(starts):
        cols = row0 + tile
        ok = allowed_block(flag, row0, tile, cols, length // SHORT_SEQS)
        q = q_ref[row0 : row0 + tile, :]
        g = g_ref[row0 : row0 + tile, :]
        lse = lse_ref[row0 : row0 + tile, :]
        k = k_ref[0:cols, :]
        v = v_ref[0:cols, :]
        dqs, dks, dvs = [], [], []
        for h in range(2):
            mine = first if h == 0 else jnp.logical_not(first)
            qh = jnp.where(mine, q, jnp.zeros_like(q))
            gh = jnp.where(mine, g, jnp.zeros_like(g))
            s = jnp.where(ok, dot_nt(qh, k) * scale, NEG)
            p = jnp.exp(s - lse[:, h * HEAD : h * HEAD + 1])
            dp = dot_nt(gh, v)
            centre = jnp.sum(p * dp, axis=-1, keepdims=True)
            ds = (p * (dp - centre)).astype(BF16)
            dqs.append(dot_nn(ds, k))
            dks.append(dot_tn(ds, qh))
            dvs.append(dot_tn(p.astype(BF16), gh))
        o_ref[row0 : row0 + tile, pl.ds(col, PAIR)] = (
            jnp.where(first, dqs[0], dqs[1]) * scale
        ).astype(BF16)
        dk_all = dks[0] + dks[1]
        dv_all = dvs[0] + dvs[1]
        for j in range(i + 1):
            part_k = dk_all[j * tile : (j + 1) * tile]
            part_v = dv_all[j * tile : (j + 1) * tile]
            dk[j] = part_k if dk[j] is None else dk[j] + part_k
            dv[j] = part_v if dv[j] is None else dv[j] + part_v
    for j, row0 in enumerate(starts):
        o_ref[row0 : row0 + tile, pl.ds(width + col, PAIR)] = (dk[j] * scale).astype(BF16)
        o_ref[row0 : row0 + tile, pl.ds(2 * width + col, PAIR)] = dv[j].astype(BF16)


def attention_backward(qkv, flag, grad, lse, tile=256):
    length, width = qkv.shape[0], qkv.shape[1] // 3
    pairs = width // PAIR
    spec = lambda off: pl.BlockSpec((length, PAIR), lambda j: (0, off + j))
    return pl.pallas_call(
        functools.partial(attn_bwd_kernel, tile),
        grid=(pairs,),
        in_specs=[
            pl.BlockSpec(memory_space=pltpu.SMEM),
            spec(0),
            spec(pairs),
            spec(2 * pairs),
            spec(0),
            spec(0),
        ],
        out_specs=pl.BlockSpec((length, 3 * width), lambda j: (0, 0)),
        out_shape=jax.ShapeDtypeStruct((length, 3 * width), BF16),
        compiler_params=params(40),
        cost_estimate=cost(length, length),
        name="attn_bwd",
    )(flag, qkv, qkv, qkv, grad, lse)


def dense_kernel(mid_ref, dg_ref, up_ref, down_ref, out_ref, mg_ref, wu_ref, wd_ref):
    mid = mid_ref[...]
    dg = dg_ref[...]
    up = up_ref[...]
    down = down_ref[...]
    act, slope = gelu_pair(dot_nn(mid, up))
    act = act.astype(BF16)
    pg = (dot_nt(dg, down) * slope).astype(BF16)
    out = dot_nn(act, down)
    mg = dot_nt(pg, up)
    wu_ref[...] = dot_tn(mid, pg).astype(BF16)
    wd_ref[...] = dot_tn(act, dg).astype(BF16)

    @pl.when(pl.program_id(0) == 0)
    def _():
        out_ref[...] = out
        mg_ref[...] = mg

    @pl.when(pl.program_id(0) > 0)
    def _():
        out_ref[...] += out
        mg_ref[...] += mg


def dense_branch(mid, dg, up, down, tile=1024):
    length, width = mid.shape
    ff = up.shape[1]
    whole = pl.BlockSpec((length, width), lambda j: (0, 0))
    cols = pl.BlockSpec((width, tile), lambda j: (0, j))
    rows = pl.BlockSpec((tile, width), lambda j: (j, 0))
    return pl.pallas_call(
        dense_kernel,
        grid=(ff // tile,),
        in_specs=[whole, whole, cols, rows],
        out_specs=[whole, whole, cols, rows],
        out_shape=[
            jax.ShapeDtypeStruct((length, width), F32),
            jax.ShapeDtypeStruct((length, width), F32),
            jax.ShapeDtypeStruct((width, ff), BF16),
            jax.ShapeDtypeStruct((ff, width), BF16),
        ],
        compiler_params=params(48),
        cost_estimate=cost(length, length),
        name="dense_branch",
    )(mid, dg, up, down)


def expert_kernel(mid_ref, g_ref, mix_ref, up_ref, down_ref, po_ref, pi_ref, act_ref, pg_ref, eg_ref, dot_ref):
    mid = mid_ref[...]
    g = g_ref[...].astype(F32)
    logits = dot_nn(mid, mix_ref[...])
    share = 1.0 / (1.0 + jnp.exp(logits[:, 0:1] - logits[:, 1:2]))
    eg = (share * g).astype(BF16)
    eg_ref[...] = eg
    act, slope = gelu_pair(dot_nn(mid, up_ref[...]))
    act = act.astype(BF16)
    act_ref[...] = act
    pg = (dot_nt(eg, down_ref[...]) * slope).astype(BF16)
    pg_ref[...] = pg
    pi_ref[...] = dot_nt(pg, up_ref[...]).astype(BF16)
    po = dot_nn(act, down_ref[...])
    po_ref[...] = po.astype(BF16)
    dot_ref[...] = jnp.sum(po * g, axis=-1, keepdims=True)


def expert_chunk(mid, g, mix_pad, up, down, tile=320):
    rows, width = mid.shape
    hidden = up.shape[1]
    block = pl.BlockSpec((tile, width), lambda i: (i, 0))
    hblock = pl.BlockSpec((tile, hidden), lambda i: (i, 0))
    full = lambda a: pl.BlockSpec(a.shape, lambda i: (0, 0))
    return pl.pallas_call(
        expert_kernel,
        grid=(rows // tile,),
        in_specs=[block, block, full(mix_pad), full(up), full(down)],
        out_specs=[block, block, hblock, hblock, block, pl.BlockSpec((tile, 1), lambda i: (i, 0))],
        out_shape=[
            jax.ShapeDtypeStruct((rows, width), BF16),
            jax.ShapeDtypeStruct((rows, width), BF16),
            jax.ShapeDtypeStruct((rows, hidden), BF16),
            jax.ShapeDtypeStruct((rows, hidden), BF16),
            jax.ShapeDtypeStruct((rows, width), BF16),
            jax.ShapeDtypeStruct((rows, 1), F32),
        ],
        compiler_params=params(48),
        cost_estimate=cost(8 * rows * width * hidden, 14 * rows * width + 4 * width * hidden),
        name="expert_chunk",
    )(mid, g, mix_pad, up, down)


def expert_grad_kernel(count, *refs):
    mids, pgs, acts, egs = (refs[i * count : (i + 1) * count] for i in range(4))
    du_ref, dd_ref = refs[4 * count :]
    up_sum = dot_tn(mids[0][...], pgs[0][...])
    down_sum = dot_tn(acts[0][...], egs[0][...])
    for i in range(1, count):
        up_sum += dot_tn(mids[i][...], pgs[i][...])
        down_sum += dot_tn(acts[i][...], egs[i][...])
    du_ref[...] = up_sum
    dd_ref[...] = down_sum


def expert_weight_grads(mids, pgs, acts, egs, tile=256):
    count = len(mids)
    rows, width = mids[0].shape
    hidden = pgs[0].shape[1]
    full = lambda a: pl.BlockSpec(a.shape, lambda j: (0, 0))
    cols = lambda a: pl.BlockSpec((a.shape[0], tile), lambda j: (0, j))
    return pl.pallas_call(
        functools.partial(expert_grad_kernel, count),
        grid=(hidden // tile,),
        in_specs=[full(a) for a in mids]
        + [cols(a) for a in pgs]
        + [cols(a) for a in acts]
        + [full(a) for a in egs],
        out_specs=[
            pl.BlockSpec((width, tile), lambda j: (0, j)),
            pl.BlockSpec((tile, width), lambda j: (j, 0)),
        ],
        out_shape=[jax.ShapeDtypeStruct((width, hidden), F32), jax.ShapeDtypeStruct((hidden, width), F32)],
        compiler_params=params(48),
        cost_estimate=cost(4 * count * rows * width * hidden, 8 * count * rows * width + 8 * width * hidden),
        name="expert_weight_grads",
    )(*mids, *pgs, *acts, *egs)


def exchange_kernel(
    waves, layers, groups, slots_ref, *refs
):
    gathered = 2 * layers - 1
    g_low = [refs[0], *refs[1:layers]]
    g_high = [refs[0], *refs[layers:gathered]]
    mix_ref, up_ref, down_ref, back_ref, slab_ref = refs[gathered : gathered + 5]
    po_refs = refs[gathered + 5 : gathered + layers + 5]
    (
        du_ref, dd_ref, g_refs, buf, part, got, act_s, pg_s, eg_s, home, home_slab,
        g_sem, a_send, a_recv, z_send, z_recv, r_send, r_recv, b_send, b_recv,
    ) = refs[gathered + layers + 5 :]
    each = groups // waves
    capacity, width = slots_ref.shape[1:]
    rows = each * capacity
    last = layers - 1
    here, me = lax.axis_index("dp"), lax.axis_index("ep")
    up_id, down_id = lax.rem(here + 1, layers), lax.rem(here + last, layers)
    peer = lambda j: lax.rem(me + j, groups)
    source = lambda j: lax.rem(me + groups - j, groups)
    mesh_id = pl.DeviceIdType.MESH

    def a_copy(j):
        return pltpu.make_async_remote_copy(
            slots_ref.at[peer(j)], buf.at[j // each, 0, lax.rem(j, each)],
            a_send.at[j], a_recv.at[j], device_id={"ep": peer(j)}, device_id_type=mesh_id,
        )

    def z_copy(w, way, s):
        src, dst = ((layers - s + 1) % layers, layers - s) if way == 0 else (s - 1, s)
        return [
            pltpu.make_async_remote_copy(
                buf.at[w, src], buf.at[w, dst], z_send.at[w, way, s - 1], z_recv.at[w, way, s - 1],
                device_id={"dp": up_id if way == 0 else down_id}, device_id_type=mesh_id,
            )
        ]

    lanes = -(-rows // 128) * 128
    main, extra_rows = pl.ds(0, rows), pl.ds(rows, 16)

    def r_copy(w, way, s):
        k = layers - s if way == 0 else s
        return [
            pltpu.make_async_remote_copy(
                src, dst, r_send.at[w, way, s - 1, n], r_recv.at[w, way, s - 1, n],
                device_id={"dp": up_id if way == 0 else down_id}, device_id_type=mesh_id,
            )
            for n, (src, dst) in enumerate(
                (
                    (part.at[w, k, main], got.at[w, way, s - 1, main]),
                    (
                        part.at[w, k, extra_rows, pl.ds(0, lanes)],
                        got.at[w, way, s - 1, extra_rows, pl.ds(0, lanes)],
                    ),
                )
            )
        ]

    def b_copies(j):
        w, i = j // each, lax.rem(j, each)
        start = pl.multiple_of(i * capacity, 16)
        return [
            pltpu.make_async_remote_copy(
                src, dst, b_send.at[j, n], b_recv.at[j, n],
                device_id={"ep": source(j)}, device_id_type=mesh_id,
            )
            for n, (src, dst) in enumerate(
                (
                    (part.at[w, 0, pl.ds(start, capacity)], home.at[j]),
                    (part.at[w, 0, extra_rows, pl.ds(0, lanes)], home_slab.at[j]),
                )
            )
        ]

    def z_sends(way, s):
        if way == 0:
            return jnp.logical_and(here <= last - 1, here >= s - 1)
        return jnp.logical_and(here >= 1, here <= layers - s)

    def z_gets(way, s):
        return here >= s if way == 0 else here <= last - s

    def r_sends(way, s):
        return here <= s - 1 if way == 0 else here >= layers - s

    def r_gets(way, s):
        if way == 0:
            return jnp.logical_and(here >= 1, here <= s)
        return jnp.logical_and(here >= last - s, here <= last - 1)

    def g_copy(ref, k):
        return pltpu.make_async_copy(ref, g_refs.at[k], g_sem.at[k])

    for k in range(layers):
        pl.when(here + k <= last)(lambda k=k: g_copy(g_high[k], k).start())
        if k:
            pl.when(here + k > last)(lambda k=k: g_copy(g_low[layers - k], k).start())

    part[...] = jnp.zeros_like(part)
    got[:, :, last - 1] = jnp.zeros_like(got[:, :, last - 1])
    du_ref[...] = jnp.zeros_like(du_ref)
    dd_ref[...] = jnp.zeros_like(dd_ref)

    barrier = pltpu.get_barrier_semaphore()

    def greet(j, carry):
        pl.semaphore_signal(barrier, inc=1, device_id={"ep": peer(j)}, device_id_type=mesh_id)
        return carry

    lax.fori_loop(1, groups, greet, 0)

    @pl.when(here < last)
    def _():
        pl.semaphore_signal(barrier, inc=1, device_id={"dp": up_id}, device_id_type=mesh_id)

    @pl.when(here > 0)
    def _():
        pl.semaphore_signal(barrier, inc=1, device_id={"dp": down_id}, device_id_type=mesh_id)

    pl.semaphore_wait(barrier, groups - 1 + jnp.where(here < last, 1, 0) + jnp.where(here > 0, 1, 0))

    def over(first, count, act):
        lax.fori_loop(first, count, lambda j, c: (act(j), c)[1], 0)

    over(1, groups, lambda j: a_copy(j).start())
    buf[0, 0, 0] = slots_ref[me]
    for k in range(layers):
        g_copy(g_high[k], k).wait()

    def slab_of(row):
        high = row.astype(BF16).astype(F32)
        line = lax.broadcasted_iota(jnp.int32, (16, rows), 0)
        return jnp.where(line == 0, high, jnp.where(line == 1, row - high, 0.0)).astype(BF16)

    def piece(w, ks):
        mid = jnp.concatenate([buf[w, k].reshape(rows, width) for k in ks], axis=0)
        g = jnp.concatenate(
            [g_refs[k, source(w * each + i)] for k in ks for i in range(each)], axis=0
        ).astype(F32)
        logits = dot_nn(mid, mix_ref[...])
        share = 1.0 / (1.0 + jnp.exp(logits[:, 0:1] - logits[:, 1:2]))
        eg = (share * g).astype(BF16)
        act, slope = gelu_pair(dot_nn(mid, up_ref[...]))
        act = act.astype(BF16)
        pg = (dot_nt(eg, down_ref[...]) * slope).astype(BF16)
        pi = dot_nt(pg, up_ref[...]).astype(BF16)
        po = dot_nn(act, down_ref[...])
        sums = jnp.sum(po * g, axis=-1, keepdims=True)
        po = po.astype(BF16)
        diag = lax.broadcasted_iota(jnp.int32, (rows, rows), 0) == lax.broadcasted_iota(
            jnp.int32, (rows, rows), 1
        )
        for n, k in enumerate(ks):
            mine = slice(n * rows, (n + 1) * rows)
            spot = slice(k * rows, (k + 1) * rows)
            eg_s[spot] = eg[mine]
            act_s[spot] = act[mine]
            pg_s[spot] = pg[mine]
            part[w, k, 0:rows] = pi[mine]
            line = jnp.sum(jnp.where(diag, sums[mine], 0.0), axis=0, keepdims=True)
            part[w, k, rows : rows + 16, 0:rows] = slab_of(line)
            for i in range(each):
                at = n * rows + i * capacity
                po_refs[k][source(w * each + i)] = po[at : at + capacity]

    def weight_grads(w):
        mid = buf[w].reshape(layers * rows, width)
        du_ref[...] += dot_tn(mid, pg_s[...])
        dd_ref[...] += dot_tn(act_s[...], eg_s[...])

    def add_to(w, k, pieces):
        total = part[w, k, 0:rows].astype(F32)
        extra = part[w, k, rows : rows + 16, 0:rows].astype(F32)
        for way, s in pieces:
            total = total + got[w, way, s - 1, 0:rows].astype(F32)
            extra = extra + got[w, way, s - 1, rows : rows + 16, 0:rows].astype(F32)
        part[w, k, 0:rows] = total.astype(BF16)
        part[w, k, rows : rows + 16, 0:rows] = slab_of(jnp.sum(extra, axis=0, keepdims=True))

    def start_hop(copy, sends, w, s):
        for way in range(2):
            pl.when(sends(way, s))(lambda way=way: [c.start() for c in copy(w, way, s)][:0] or None)

    def get_hop(copy, gets, w, s):
        for way in range(2):
            pl.when(gets(way, s))(lambda way=way: [c.wait_recv() for c in copy(w, way, s)][:0] or None)

    def pass_on(w, s):
        for way in range(2):

            @pl.when(r_gets(way, s))
            def _():
                for copy in r_copy(w, way, s):
                    copy.wait_recv()
                add_to(w, layers - s - 1 if way == 0 else s + 1, [(way, s)])

        start_hop(r_copy, r_sends, w, s + 1)

    def finish(w):
        get_hop(r_copy, r_gets, w, last)
        add_to(w, 0, [(0, last), (1, last)])
        for i in range(each):
            j = w * each + i
            start = i * capacity

            @pl.when(j > 0)
            def _():
                for copy in b_copies(j):
                    copy.start()

            @pl.when(j == 0)
            def _():
                home[0] = part[0, 0, start : start + capacity]
                home_slab[0] = part[0, 0, rows : rows + 16, 0:lanes]

    def first_hop(w):
        for n in range(each):
            pl.when(w * each + n > 0)(lambda n=n: a_copy(w * each + n).wait_recv())
        start_hop(z_copy, z_sends, w, 1)

    far = [1, last]
    near = [k for k in range(layers) if k not in far]

    def valid(w):
        return jnp.logical_and(w >= 0, w < waves)

    def body(t, carry):
        for s in range(1, layers):
            pl.when(valid(t - s))(lambda s=s: get_hop(z_copy, z_gets, t - s, s))
        for s in range(2, layers):
            pl.when(valid(t + 1 - s))(lambda s=s: start_hop(z_copy, z_sends, t + 1 - s, s))
        pl.when(t + 1 < waves)(lambda: first_hop(t + 1))
        w = t - last

        @pl.when(valid(w))
        def _():
            piece(w, far)
            start_hop(r_copy, r_sends, w, 1)

        for s in range(1, last):
            pl.when(valid(w - s))(lambda s=s: pass_on(w - s, s))
        pl.when(valid(w - last))(lambda: finish(w - last))

        @pl.when(valid(w))
        def _():
            piece(w, near)
            weight_grads(w)

        return carry

    first_hop(0)
    lax.fori_loop(0, waves + 2 * last, body, 0)

    def land(j, carry):
        for copy in b_copies(j):
            copy.wait_recv()
            copy.wait_send()
        a_copy(j).wait_send()
        return carry

    lax.fori_loop(1, groups, land, 0)

    def sent(w, carry):
        for way in range(2):
            for s in range(1, layers):
                for copy, sends in ((z_copy, z_sends), (r_copy, r_sends)):

                    @pl.when(sends(way, s))
                    def _():
                        for one in copy(w, way, s):
                            one.wait_send()

        return carry

    lax.fori_loop(0, waves, sent, 0)

    def arrange(j, carry):
        back_ref[peer(j)] = home[j]
        slab_ref[peer(j)] = home_slab[j]
        return carry

    lax.fori_loop(0, groups, arrange, 0)


def exchange_waves(groups):
    return 8 if groups % 8 == 0 else 1


def expert_exchange(slots, g_low, g_high, mix_pad, up, down):
    layers, groups = lax.axis_size("dp"), lax.axis_size("ep")
    waves = exchange_waves(groups)
    each = groups // waves
    _, capacity, width = slots.shape
    hidden = up.shape[1]
    rows = each * capacity
    lanes = -(-rows // 128) * 128
    sem = pltpu.SemaphoreType.DMA
    block = jax.ShapeDtypeStruct((groups, capacity, width), BF16)
    vmem = pl.BlockSpec(memory_space=pltpu.VMEM)
    total_rows = layers * groups * capacity
    outs = pl.pallas_call(
        functools.partial(exchange_kernel, waves, layers, groups),
        in_specs=[vmem] + [pl.BlockSpec(memory_space=pl.ANY)] * (2 * layers - 1) + [vmem] * 3,
        out_specs=[vmem] * (4 + layers),
        out_shape=[block, jax.ShapeDtypeStruct((groups, 16, lanes), BF16)]
        + [block] * layers
        + [jax.ShapeDtypeStruct((width, hidden), F32), jax.ShapeDtypeStruct((hidden, width), F32)],
        scratch_shapes=[
            pltpu.VMEM((layers, groups, capacity, width), BF16),
            pltpu.VMEM((waves, layers, each, capacity, width), BF16),
            pltpu.VMEM((waves, layers, rows + 16, width), BF16),
            pltpu.VMEM((waves, 2, layers - 1, rows + 16, width), BF16),
            pltpu.VMEM((layers * rows, hidden), BF16),
            pltpu.VMEM((layers * rows, hidden), BF16),
            pltpu.VMEM((layers * rows, width), BF16),
            pltpu.VMEM((groups, capacity, width), BF16),
            pltpu.VMEM((groups, 16, lanes), BF16),
            sem((layers,)),
            sem((groups,)),
            sem((groups,)),
            sem((waves, 2, layers - 1)),
            sem((waves, 2, layers - 1)),
            sem((waves, 2, layers - 1, 2)),
            sem((waves, 2, layers - 1, 2)),
            sem((groups, 2)),
            sem((groups, 2)),
        ],
        compiler_params=pltpu.CompilerParams(
            collective_id=0, has_side_effects=True, vmem_limit_bytes=62 << 20
        ),
        cost_estimate=cost(12 * total_rows * width * hidden, 20 * total_rows * width),
        name="expert_exchange",
    )(slots, *g_low, *g_high[1:], mix_pad, up, down)
    return outs[0], outs[1], outs[2 : 2 + layers], outs[2 + layers], outs[3 + layers]


def sums_kernel(plan, split, layers, groups, small_ref, *refs):
    count = len(plan)
    mats, outs = refs[:count], refs[count : 2 * count]
    (
        small_out, own, sib, got, held, inner, final, small_two, small_chip, small_layer,
        own_sem, s_send, s_recv, x_send, x_recv, z_send, z_recv, t_send, t_recv, o_sem,
    ) = refs[2 * count :]
    chips = groups // 2
    width = held.shape[-1]
    total = held.shape[0]
    last = layers - 1
    here, me = lax.axis_index("dp"), lax.axis_index("ep")
    core, chip = lax.rem(me, 2), me // 2
    sibling = me + 1 - 2 * core
    mesh_id = pl.DeviceIdType.MESH
    chip_at = lambda j: lax.rem(chip + j, chips)
    pieces = [(m, i, n) for m in range(count) for i in range(plan[m]) for n in range(split)]
    lines = held.shape[1]
    square = chips == 4
    by_one = chip + 1 - 2 * lax.rem(chip, 2)
    by_two = chip + 2 - 4 * (chip // 2)
    at_end = jnp.logical_or(here == 0, here == last)
    inside = jnp.logical_and(here > 0, here < last)
    inward = 1 + (here // last) * (last - 2)
    outward = lax.rem((here - 1) * last + layers * last, layers)
    across = last - here

    def source(m, i, n, half):
        span = pl.ds(n * lines, lines)
        if len(mats[m].shape) == 5:
            return mats[m].at[:, half, i, span]
        return mats[m].at[:, half, span, pl.ds(i * width, width)]

    def remote(src, dst, send, recv, where):
        return pltpu.make_async_remote_copy(
            src, dst, send, recv, device_id=where, device_id_type=mesh_id
        )

    def s_copy(c):
        return remote(source(*pieces[c], 1 - core), sib.at[c], s_send.at[c], s_recv.at[c], {"ep": sibling})

    def x_copy(c, j):
        return remote(
            own.at[c, chip_at(j)], got.at[c, j - 1], x_send.at[c, j - 1], x_recv.at[c, j - 1],
            {"ep": 2 * chip_at(j) + core},
        )

    def near_chip(c):
        return by_one + lax.rem(c, 2) * (by_two - by_one)

    def next_chip(c):
        return by_two + lax.rem(c, 2) * (by_one - by_two)

    def y_copy(c, n):
        block = (near_chip(c), 3 - chip, next_chip(c))[n]
        where = next_chip(c) if n == 2 else near_chip(c)
        return remote(
            own.at[c, block], got.at[c, n], x_send.at[c, n], x_recv.at[c, n], {"ep": 2 * where + core}
        )

    lags = [LAG * n for n in range(1, 6)] if square else [0] + [LAG * n for n in range(1, 5)]

    def due(t, n):
        return jnp.logical_and(t >= lags[n], t < total + lags[n])

    def z_copy(c, n):
        src = (held, held, inner)[n]
        dst = (inner, final, final)[n]
        where = (inward, across, outward)[n]
        return remote(src.at[c], dst.at[c], z_send.at[c, n], z_recv.at[c, n], {"dp": where})

    def t_copy(n, j):
        if n == 0:
            return remote(small_ref, small_two, t_send.at[0, 0], t_recv.at[0, 0], {"ep": sibling})
        if n == 1:
            spot = small_chip.at[chip]
            return remote(spot, spot, t_send.at[1, j], t_recv.at[1, j], {"ep": 2 * chip_at(j) + core})
        spot = small_layer.at[here]
        return remote(
            spot, spot, t_send.at[2, j], t_recv.at[2, j], {"dp": lax.rem(here + j, layers)}
        )

    for c in range(total):
        pltpu.make_async_copy(source(*pieces[c], core), own.at[c], own_sem.at[c]).start()

    barrier = pltpu.get_barrier_semaphore()
    pl.semaphore_signal(barrier, inc=1, device_id={"ep": sibling}, device_id_type=mesh_id)

    def over(first, end, act):
        def step(j, carry):
            act(j)
            return carry

        lax.fori_loop(first, end, step, 0)

    over(
        1,
        chips,
        lambda j: pl.semaphore_signal(
            barrier, inc=1, device_id={"ep": 2 * chip_at(j) + core}, device_id_type=mesh_id
        ),
    )
    over(
        1,
        layers,
        lambda j: pl.semaphore_signal(
            barrier, inc=1, device_id={"dp": lax.rem(here + j, layers)}, device_id_type=mesh_id
        ),
    )
    pl.semaphore_wait(barrier, chips + last)

    t_copy(0, 0).start()
    for c in range(total):
        s_copy(c).start()

    def body(t, carry):
        @pl.when(t < total)
        def _():
            pltpu.make_async_copy(sib.at[t], own.at[t], own_sem.at[t]).wait()
            remote(own.at[t], sib.at[t], s_send.at[t], s_recv.at[t], {"ep": sibling}).wait_recv()

            def add(p):
                own[t, p] = own[t, p] + sib[t, p]

            over(0, chips, add)
            if square:
                y_copy(t, 1).start()
                y_copy(t, 0).start()
            else:
                over(1, chips, lambda j: x_copy(t, j).start())

        if square:

            @pl.when(due(t, 0))
            def _():
                c = t - lags[0]
                y_copy(c, 1).wait_recv()
                own[c, next_chip(c)] = own[c, next_chip(c)] + got[c, 1]
                y_copy(c, 2).start()
                y_copy(c, 0).wait_recv()
                own[c, chip] = own[c, chip] + got[c, 0]

        @pl.when(due(t, 1))
        def _():
            c = t - lags[1]
            if square:
                y_copy(c, 2).wait_recv()
                held[c] = own[c, chip] + got[c, 2]
            else:
                over(1, chips, lambda j: x_copy(c, j).wait_recv())
                held[c] = lax.fori_loop(
                    1, chips, lambda j, acc: acc + got[c, j - 1].astype(F32), own[c, chip].astype(F32)
                ).astype(BF16)
            pl.when(at_end)(lambda: z_copy(c, 0).start())

        @pl.when(jnp.logical_and(inside, due(t, 2)))
        def _():
            c = t - lags[2]
            z_copy(c, 0).wait_recv()
            held[c] = held[c] + inner[c]
            z_copy(c, 1).start()

        @pl.when(jnp.logical_and(inside, due(t, 3)))
        def _():
            c = t - lags[3]
            z_copy(c, 1).wait_recv()
            inner[c] = held[c] + final[c]
            z_copy(c, 2).start()

        @pl.when(jnp.logical_and(at_end, due(t, 4)))
        def _():
            c = t - lags[4]
            z_copy(c, 2).wait_recv()

        @pl.when(t == 1)
        def _():
            t_copy(0, 0).wait_recv()
            small_chip[chip] = small_ref[...] + small_two[...]
            over(1, chips, lambda j: t_copy(1, j).start())

        @pl.when(t == 3)
        def _():
            over(1, chips, lambda j: t_copy(1, j).wait_recv())
            acc = small_chip[0]
            for n in range(1, chips):
                acc = acc + small_chip[n]
            small_layer[here] = acc
            over(1, layers, lambda j: t_copy(2, j).start())

        return carry

    lax.fori_loop(0, total + lags[4], body, 0)

    def result(sums, c):
        m, i, n = pieces[c]
        span = pl.ds(n * lines, lines)
        if len(outs[m].shape) == 3:
            spot = outs[m].at[i, span]
        else:
            spot = outs[m].at[span, pl.ds(i * width, width)]
        return pltpu.make_async_copy(sums.at[c], spot, o_sem.at[c])

    @pl.when(inside)
    def _():
        for c in range(total):
            result(inner, c).start()

    @pl.when(at_end)
    def _():
        for c in range(total):
            result(final, c).start()

    over(1, layers, lambda j: t_copy(2, j).wait_recv())
    acc = small_layer[0]
    for n in range(1, layers):
        acc = acc + small_layer[n]
    small_out[...] = acc

    t_copy(0, 0).wait_send()
    over(1, chips, lambda j: t_copy(1, j).wait_send())
    over(1, layers, lambda j: t_copy(2, j).wait_send())

    def sent(c):
        remote(own.at[c], sib.at[c], s_send.at[c], s_recv.at[c], {"ep": sibling}).wait_send()
        if square:
            for n in range(3):
                y_copy(c, n).wait_send()
        else:
            over(1, chips, lambda j: x_copy(c, j).wait_send())
        pl.when(at_end)(lambda: z_copy(c, 0).wait_send())

        @pl.when(inside)
        def _():
            z_copy(c, 1).wait_send()
            z_copy(c, 2).wait_send()

    over(0, total, sent)
    for c in range(total):
        result(final, c).wait()


def gradient_sums(small, columns, rows_split):
    layers, groups = lax.axis_size("dp"), lax.axis_size("ep")
    chips = groups // 2
    width = small.shape[1]
    plan = [a.shape[1] // width for a in columns] + [a.shape[0] // width for a in rows_split]
    high = columns[0].shape[0] // groups
    split = SPLIT if high % (16 * SPLIT) == 0 else 1
    total, lines = sum(plan) * split, high // split
    views = [a.reshape(chips, 2, high, a.shape[1]) for a in columns] + [
        a.reshape(chips, 2, n, high, width) for a, n in zip(rows_split, plan[len(columns) :])
    ]
    shapes = [jax.ShapeDtypeStruct((high, a.shape[1]), BF16) for a in columns] + [
        jax.ShapeDtypeStruct((n, high, width), BF16) for n in plan[len(columns) :]
    ]
    sem = pltpu.SemaphoreType.DMA
    vmem = pl.BlockSpec(memory_space=pltpu.VMEM)
    anywhere = pl.BlockSpec(memory_space=pl.ANY)
    buffers = lambda *lead: pltpu.VMEM((total, *lead, lines, width), BF16)
    outs = pl.pallas_call(
        functools.partial(sums_kernel, plan, split, layers, groups),
        in_specs=[vmem] + [anywhere] * len(views),
        out_specs=[anywhere] * len(views) + [vmem],
        out_shape=shapes + [jax.ShapeDtypeStruct(small.shape, F32)],
        scratch_shapes=[
            buffers(chips),
            buffers(chips),
            buffers(chips - 1),
            buffers(),
            buffers(),
            buffers(),
            pltpu.VMEM(small.shape, F32),
            pltpu.VMEM((chips, *small.shape), F32),
            pltpu.VMEM((layers, *small.shape), F32),
            sem((total,)),
            sem((total,)),
            sem((total,)),
            sem((total, chips - 1)),
            sem((total, chips - 1)),
            sem((total, 3)),
            sem((total, 3)),
            sem((3, max(chips, layers))),
            sem((3, max(chips, layers))),
            sem((total,)),
        ],
        compiler_params=pltpu.CompilerParams(
            collective_id=1, has_side_effects=True, vmem_limit_bytes=62 << 20
        ),
        cost_estimate=cost(10 * total * chips * lines * width, 8 * total * chips * lines * width),
        name="gradient_sums",
    )(small, *views)
    rows_out = [a.reshape(-1, width) for a in outs[len(columns) : -1]]
    return (*outs[: len(columns)], *rows_out, outs[-1])


def spread_kernel(layers, groups, slots_ref, own_ref, low_ref, high_ref, a_send, a_recv, z_send, z_recv):
    last = layers - 1
    here, me = lax.axis_index("dp"), lax.axis_index("ep")
    peer = lambda j: lax.rem(me + j, groups)
    source = lambda j: lax.rem(me + groups - j, groups)
    up_id, down_id = lax.rem(here + 1, layers), lax.rem(here + last, layers)
    mesh_id = pl.DeviceIdType.MESH

    def a_copy(j):
        return pltpu.make_async_remote_copy(
            slots_ref.at[peer(j)], own_ref.at[me], a_send.at[j], a_recv.at[j],
            device_id={"ep": peer(j)}, device_id_type=mesh_id,
        )

    def z_copy(j, way):
        block = own_ref.at[source(j)]
        return pltpu.make_async_remote_copy(
            block, (low_ref, high_ref)[way].at[source(j)], z_send.at[j, way], z_recv.at[j, way],
            device_id={"dp": up_id if way == 0 else down_id}, device_id_type=mesh_id,
        )

    def over(first, count, act):
        def step(j, carry):
            act(j)
            return carry

        lax.fori_loop(first, count, step, 0)

    barrier = pltpu.get_barrier_semaphore()

    def greet(where):
        pl.semaphore_signal(barrier, inc=1, device_id=where, device_id_type=mesh_id)

    over(1, groups, lambda j: greet({"ep": peer(j)}))
    pl.when(here < last)(lambda: greet({"dp": up_id}))
    pl.when(here > 0)(lambda: greet({"dp": down_id}))
    pl.semaphore_wait(barrier, groups - 1 + jnp.where(here < last, 1, 0) + jnp.where(here > 0, 1, 0))

    over(1, groups, lambda j: a_copy(j).start())
    own_ref[me] = slots_ref[me]

    def pass_on(j):
        pl.when(here < last)(lambda: z_copy(j, 0).start())
        pl.when(here > 0)(lambda: z_copy(j, 1).start())

    pass_on(0)

    def arrived(j):
        a_copy(j).wait_recv()
        pass_on(j)

    over(1, groups, arrived)

    def settle(j):
        pl.when(here > 0)(lambda: z_copy(j, 0).wait_recv())
        pl.when(here < last)(lambda: z_copy(j, 1).wait_recv())
        pl.when(here < last)(lambda: z_copy(j, 0).wait_send())
        pl.when(here > 0)(lambda: z_copy(j, 1).wait_send())

    over(0, groups, settle)
    over(1, groups, lambda j: a_copy(j).wait_send())


def spread(slots):
    layers, groups = lax.axis_size("dp"), lax.axis_size("ep")
    vmem = pl.BlockSpec(memory_space=pltpu.VMEM)
    sem = pltpu.SemaphoreType.DMA
    return pl.pallas_call(
        functools.partial(spread_kernel, layers, groups),
        in_specs=[vmem],
        out_specs=[vmem] * 3,
        out_shape=[jax.ShapeDtypeStruct(slots.shape, BF16)] * 3,
        scratch_shapes=[sem((groups,)), sem((groups,)), sem((groups, 2)), sem((groups, 2))],
        compiler_params=pltpu.CompilerParams(
            collective_id=2, has_side_effects=True, vmem_limit_bytes=16 << 20
        ),
        cost_estimate=cost(slots.size, 4 * slots.size),
        name="spread",
    )(slots)


def normalise(values_in):
    centred = values_in - jnp.mean(values_in, axis=-1, keepdims=True)
    inverse = lax.rsqrt(jnp.mean(centred * centred, axis=-1, keepdims=True) + 1e-05)
    return centred * inverse, inverse


def norm_backward(grad, gain_vec, unit, inverse):
    m = grad * gain_vec
    return inverse * (
        m
        - jnp.mean(m, axis=-1, keepdims=True)
        - unit * jnp.mean(m * unit, axis=-1, keepdims=True)
    )


def hop(rows, step, stage):
    size = lax.axis_size("dp")
    if step > 0:
        pairs = [(i, i + 1) for i in range(stage - 1, size - 1)]
    else:
        pairs = [(i + 1, i) for i in range(0, size - stage)]
    return lax.ppermute(rows, "dp", pairs)


def both_hops(low, high, stage):
    return hop(low, 1, stage), hop(high, -1, stage)


def send_hop(rows, step, stage):
    size = lax.axis_size("dp")
    if step > 0:
        pairs = [(i, i + 1) for i in range(stage)]
    else:
        pairs = [(i, i - 1) for i in range(size - stage, size)]
    return lax.ppermute(rows, "dp", pairs)


def line_reduce(parts):
    size = lax.axis_size("dp")
    up = send_hop(parts[size - 1], 1, 1)
    down = send_hop(parts[1], -1, 1)
    for stage in range(2, size):
        up = send_hop(up + parts[size - stage], 1, stage)
        down = send_hop(down + parts[stage], -1, stage)
    return parts[0].astype(F32) + up.astype(F32) + down.astype(F32)


def shifted(rows, step):
    size = lax.axis_size("dp")
    return lax.ppermute(rows, "dp", [((i + step) % size, i) for i in range(size)])


def after(values, *earlier):
    many = isinstance(values, tuple)
    held = lax.optimization_barrier((*values, *earlier) if many else (values, *earlier))
    return held[: len(values)] if many else held[0]


def sum_layers(rows):
    size, here = lax.axis_size("dp"), lax.axis_index("dp")
    pieces = rows.reshape(size, rows.shape[0] // size, rows.shape[1])
    piece = lambda k: lax.dynamic_index_in_dim(pieces, lax.rem(here + k, size), 0, keepdims=False)
    acc = piece(0).astype(F32)
    for k in range(1, size):
        acc = acc + shifted(piece(k), size - k).astype(F32)
    mine = acc.astype(BF16)
    ring = jnp.stack([mine] + [shifted(mine, k) for k in range(1, size)])
    ordered = lax.dynamic_slice_in_dim(jnp.concatenate([ring, ring]), size - here, size, 0)
    return ordered.reshape(rows.shape).astype(F32)


def sum_everywhere(values):
    for axis in ("dp", "ep"):
        size = lax.axis_size(axis)
        step = 1
        while step < size:
            values = values + lax.ppermute(values, axis, [(i, i ^ step) for i in range(size)])
            step *= 2
    return values


def on_device(
    tokens,
    bucket,
    expert_ids,
    ln1_gain,
    qkv_weight,
    out_weight,
    ln2_gain,
    up_weight,
    down_weight,
    mix_weight,
    expert_up,
    expert_down,
    cotangent,
):
    length, width = tokens.shape
    groups = lax.axis_size("ep")
    layers = lax.axis_size("dp")
    experts = groups * expert_up.shape[0]
    capacity = 5 * length // (4 * experts)
    slots = experts * capacity
    gather = lambda w: lax.all_gather(w, "ep", axis=0, tiled=True)
    exchange_out = lambda a: lax.all_to_all(a, "ep", split_axis=0, concat_axis=1, tiled=True)
    expert_up2 = expert_up[0]
    expert_down2 = expert_down[0]
    mix_pad = jnp.pad(mix_weight, ((0, 0), (0, 126)))

    chosen = expert_ids[:, 0]
    one_hot = chosen[:, None] == jnp.arange(experts, dtype=jnp.int32)[None, :]
    place = jnp.arange(length, dtype=jnp.int32)
    earlier = (place[None, :] < place[:, None]).astype(BF16)
    before = dot_nn(earlier, one_hot.astype(BF16))
    slot_index = jnp.sum(jnp.where(one_hot, before, 0.0), axis=1).astype(jnp.int32)
    target = jnp.where(slot_index < capacity, chosen * capacity + slot_index, -1)
    table = (target[:, None] == jnp.arange(slots, dtype=jnp.int32)[None, :]).astype(BF16)

    pick = lambda rows: dot_tn(table, rows).astype(BF16).reshape(experts, capacity, width)
    join = lambda lows, highs: [highs[k] + lows[layers - k] for k in range(1, layers)]

    token_rows = tokens.astype(F32)
    unit1, inverse1 = normalise(token_rows)
    normed_in = (unit1 * ln1_gain).astype(BF16)
    qkv_full, out_full, up_full, down_full = (
        gather(qkv_weight),
        gather(out_weight),
        gather(up_weight),
        gather(down_weight),
    )
    by_kernels = capacity % 16 == 0
    if by_kernels:
        g_own, *g_first = [a.reshape(slots, width) for a in spread(pick(cotangent))]
        g_low, g_high = [g_own, g_first[0]], [g_own, g_first[1]]
    else:
        g_own = exchange_out(pick(cotangent)).reshape(slots, width)
        low, high = both_hops(g_own, g_own, 1)
        g_low, g_high = [g_own, low], [g_own, high]

    def step(lows, highs, *others):
        stage = len(lows)
        held = lax.optimization_barrier((lows[-1], highs[-1], *others))
        lows[-1], highs[-1] = held[:2]
        if stage < layers:
            low, high = both_hops(lows[-1], highs[-1], stage)
            lows.append(low)
            highs.append(high)
        return held[2:]

    (normed_in,) = step(g_low, g_high, normed_in)
    qkv_rows = dot_nn(normed_in, qkv_full).astype(BF16)
    (qkv_rows,) = step(g_low, g_high, qkv_rows)
    attended, lse = attention_forward(qkv_rows, bucket)
    hidden_res = token_rows + dot_nn(attended, out_full)
    unit2, inverse2 = normalise(hidden_res)
    mid_low = (unit2 * ln2_gain).astype(BF16)
    mid_slots = pick(mid_low)
    (mid_slots,) = step(g_low, g_high, mid_slots)

    grad_out = cotangent.astype(F32)
    logits = dot_nn(mid_low, mix_weight)
    mix1 = 1.0 / (1.0 + jnp.exp(logits[:, 0:1] - logits[:, 1:2]))
    mix0 = 1.0 / (1.0 + jnp.exp(logits[:, 1:2] - logits[:, 0:1]))
    dense_grad = (mix0 * grad_out).astype(BF16)
    scatter = lambda a: lax.psum_scatter(a.astype(BF16), "ep", scatter_dimension=0, tiled=True)
    back = lambda k, a: shifted(a, layers - k) if k else a

    def total(parts):
        acc = parts[0].astype(F32)
        for part in parts[1:]:
            acc = acc + part.astype(F32)
        return acc

    if by_kernels:
        blocks = lambda many: [g.reshape(groups, capacity, width) for g in many]
        returned, slab, partial_outs, expert_up_grad, expert_down_grad = expert_exchange(
            mid_slots, blocks(g_low), blocks(g_high), mix_pad, expert_up2, expert_down2
        )
        each = groups // exchange_waves(groups)
        offset = lax.rem(
            jnp.arange(groups, dtype=jnp.int32) + groups - lax.axis_index("ep"), groups
        )
        spot = lax.rem(offset, each)[:, None] == jnp.arange(each, dtype=jnp.int32)[None, :]
        lines = slab[:, 0, : each * capacity].astype(F32) + slab[:, 1, : each * capacity].astype(F32)
        dot_back = jnp.sum(
            jnp.where(spot[:, :, None], lines.reshape(groups, each, capacity), 0.0), axis=1
        ).reshape(1, slots)
        dense_grad, returned = lax.optimization_barrier((dense_grad, returned))
        outs = [a.reshape(slots, width) for a in partial_outs]
    else:
        gs = [g_own] + join(g_low, g_high)
        mid_own = exchange_out(mid_slots).reshape(slots, width)
        mids = [mid_own] + [shifted(mid_own, k) for k in range(1, layers)]
        chunks = [expert_chunk(mids[k], gs[k], mix_pad, expert_up2, expert_down2) for k in range(layers)]
        in_total = line_reduce([c[1] for c in chunks])
        dot_sum = total([back(k, chunks[k][5].reshape(groups, capacity)) for k in range(layers)])
        dot_high = lax.reduce_precision(dot_sum, 8, 7)
        extra = jnp.stack([dot_high, dot_sum - dot_high], axis=1)
        extra = jnp.pad(extra, ((0, 0), (0, 14), (0, width - capacity)))
        packed = jnp.concatenate([in_total.reshape(groups, capacity, width), extra], axis=1)
        both = lax.all_to_all(packed.astype(BF16), "ep", split_axis=0, concat_axis=0, tiled=True)
        returned = both[:, :capacity]
        dot_back = (
            both[:, capacity, :capacity].astype(F32) + both[:, capacity + 1, :capacity].astype(F32)
        ).reshape(1, slots)
        outs = [c[0] for c in chunks]
        expert_up_grad, expert_down_grad = expert_weight_grads(
            mids, [c[3] for c in chunks], [c[2] for c in chunks], [c[4] for c in chunks]
        )

    outs = [back(k, outs[k]) for k in range(layers)]
    dense_out, mid_grad_dense, up_grad, down_grad = dense_branch(mid_low, dense_grad, up_full, down_full)
    in_rows = returned.reshape(slots, width)
    mix_dot1 = jnp.sum(table.astype(F32) * dot_back, axis=1, keepdims=True)
    mix_dot0 = jnp.sum(grad_out * dense_out, axis=-1, keepdims=True)
    mean_dot = mix0 * mix_dot0 + mix1 * mix_dot1
    logit_grad = jnp.concatenate(
        [mix0 * (mix_dot0 - mean_dot), mix1 * (mix_dot1 - mean_dot)], axis=1
    ).astype(BF16)
    mix_weight_grad = dot_tn(mid_low, logit_grad)
    mid_grad = mid_grad_dense + dot_nt(logit_grad, mix_weight) + dot_nn(table, in_rows)
    ln2_gain_grad = jnp.sum(mid_grad * unit2, axis=0)
    res_grad = grad_out + norm_backward(mid_grad, ln2_gain, unit2, inverse2)
    attn_out_grad = res_grad.astype(BF16)
    out_weight_grad = dot_tn(attended, attn_out_grad)
    attended_grad = dot_nt(attn_out_grad, out_full).astype(BF16)
    qkv_grad = attention_backward(qkv_rows, bucket, attended_grad, lse)
    qkv_weight_grad = dot_tn(normed_in, qkv_grad)
    normed_grad = dot_nt(qkv_grad, qkv_full)
    ln1_gain_grad = jnp.sum(normed_grad * unit1, axis=0)
    tokens_grad = res_grad + norm_backward(normed_grad, ln1_gain, unit1, inverse1)

    small = jnp.concatenate([ln1_gain_grad[None], ln2_gain_grad[None], mix_weight_grad.T], axis=0)
    small = jnp.pad(small, ((0, 4), (0, 0)))
    if layers == 4 and length // groups >= 16:
        qkv_final, out_final, up_final, down_final, small_sums = gradient_sums(
            small,
            [a.astype(BF16) for a in (qkv_weight_grad, out_weight_grad, up_grad)],
            [down_grad],
        )
    else:
        sums = [sum_layers(scatter(a)) for a in (qkv_weight_grad, out_weight_grad, up_grad, down_grad)]
        qkv_final, out_final, up_final, down_final = sums
        small_sums = sum_everywhere(small)
    outs = list(after(tuple(outs), small_sums))
    out_sum = total(outs).astype(BF16).reshape(groups, capacity, width)
    out_back = lax.all_to_all(out_sum, "ep", split_axis=0, concat_axis=0, tiled=True)
    bucket, qkv_final, out_final, up_final, down_final = after(
        (bucket, qkv_final, out_final, up_final, down_final), out_sum
    )
    unit = jnp.where(bucket[0] < 0, 0.0, 1.0)
    expert_up_grad, expert_down_grad, qkv_final, out_final, up_final, down_final, out_back = (
        lax.optimization_barrier(
            (
                expert_up_grad * unit,
                expert_down_grad * unit,
                *(a.astype(F32) for a in (qkv_final, out_final, up_final, down_final)),
                out_back,
            )
        )
    )
    expert_out = dot_nn(table, out_back.reshape(slots, width))
    result = (hidden_res + mix0 * dense_out + mix1 * expert_out).astype(BF16)
    return (
        result,
        tokens_grad,
        small_sums[0],
        qkv_final,
        out_final,
        small_sums[1],
        up_final,
        down_final,
        small_sums[2:4].T,
        expert_up_grad[None],
        expert_down_grad[None],
    )


def solution(mesh):
    placed = (
        P(("dp", "ep"), None),
        P(("dp", "ep")),
        P(("dp", "ep"), None),
        P(),
        P("ep", None),
        P("ep", None),
        P(),
        P("ep", None),
        P("ep", None),
        P(),
        P("ep", None, "dp"),
        P("ep", "dp", None),
        P(("dp", "ep"), None),
    )
    return jax.shard_map(
        on_device,
        mesh=mesh,
        in_specs=placed,
        out_specs=(
            P(("dp", "ep"), None),
            P(("dp", "ep"), None),
            P(),
            P("ep", None),
            P("ep", None),
            P(),
            P("ep", None),
            P("ep", None),
            P(),
            P("ep", None, "dp"),
            P("ep", "dp", None),
        ),
        check_vma=False,
    )
```

```python
import functools

import jax
import jax.numpy as jnp
from jax import lax
from jax.experimental import pallas as pl
from jax.experimental.pallas import tpu as pltpu
from jax.sharding import PartitionSpec as P

HEAD = 64
SHORT_SEQS = 4
PAIR = 2 * HEAD
NEG = -1e30
SPLIT = 2
LAG = 2
ROOT = 0.7978845608028654
CUBE = 0.044715
F32 = jnp.float32
BF16 = jnp.bfloat16


def dot_nn(a, b):
    return lax.dot_general(a, b, (((1,), (0,)), ((), ())), preferred_element_type=F32)


def dot_nt(a, b):
    return lax.dot_general(a, b, (((1,), (1,)), ((), ())), preferred_element_type=F32)


def dot_tn(a, b):
    return lax.dot_general(a, b, (((0,), (0,)), ((), ())), preferred_element_type=F32)


def gelu_pair(v):
    sq = v * v
    t = jnp.tanh(v * (ROOT + (ROOT * CUBE) * sq))
    half = 0.5 * (1.0 + t)
    slope = half + (0.5 * v) * (1.0 - t * t) * (ROOT + (3.0 * ROOT * CUBE) * sq)
    return v * half, slope


def two_shares(first, second):
    small = jnp.exp(-jnp.abs(second - first))
    lead = 1.0 / (1.0 + small)
    ahead = second >= first
    return jnp.where(ahead, small * lead, lead), jnp.where(ahead, lead, small * lead)


def params(vmem_mib):
    return pltpu.CompilerParams(vmem_limit_bytes=vmem_mib << 20)


def cost(flops, nbytes):
    return pl.CostEstimate(flops=int(flops), bytes_accessed=int(nbytes), transcendentals=0)


def allowed_block(flag, row0, rows, cols, short):
    r = row0 + lax.broadcasted_iota(jnp.int32, (rows, cols), 0)
    c = lax.broadcasted_iota(jnp.int32, (rows, cols), 1)
    shift = short.bit_length() - 1
    same = jnp.logical_or(flag == 1, lax.shift_right_logical(r, shift) == lax.shift_right_logical(c, shift))
    return jnp.logical_and(c <= r, same)


def attn_fwd_kernel(tile, flag_ref, q_ref, k_ref, v_ref, o_ref, lse_ref):
    length = q_ref.shape[0]
    flag = flag_ref[0]
    lane = lax.broadcasted_iota(jnp.int32, (1, PAIR), 1)
    first = lane < HEAD
    scale = HEAD ** (-0.5)
    for row0 in range(0, length, tile):
        cols = row0 + tile
        ok = allowed_block(flag, row0, tile, cols, length // SHORT_SEQS)
        q = q_ref[row0 : row0 + tile, :]
        k = k_ref[0:cols, :]
        v = v_ref[0:cols, :]
        outs, lses = [], []
        for h in range(2):
            qh = jnp.where(first if h == 0 else jnp.logical_not(first), q, jnp.zeros_like(q))
            s = jnp.where(ok, dot_nt(qh, k) * scale, NEG)
            peak = jnp.max(s, axis=-1, keepdims=True)
            p = jnp.exp(s - peak)
            total = jnp.sum(p, axis=-1, keepdims=True)
            outs.append(dot_nn((p * (1.0 / total)).astype(BF16), v))
            lses.append(peak + jnp.log(total))
        o_ref[row0 : row0 + tile, :] = jnp.where(first, outs[0], outs[1]).astype(BF16)
        lse_ref[row0 : row0 + tile, :] = jnp.where(first, lses[0], lses[1])


def attention_forward(qkv, flag, tile=512):
    length, width = qkv.shape[0], qkv.shape[1] // 3
    pairs = width // PAIR
    spec = lambda off: pl.BlockSpec((length, PAIR), lambda j: (0, off + j))
    return pl.pallas_call(
        functools.partial(attn_fwd_kernel, tile),
        grid=(pairs,),
        in_specs=[pl.BlockSpec(memory_space=pltpu.SMEM), spec(0), spec(pairs), spec(2 * pairs)],
        out_specs=[spec(0), spec(0)],
        out_shape=[jax.ShapeDtypeStruct((length, width), BF16), jax.ShapeDtypeStruct((length, width), F32)],
        compiler_params=params(32),
        cost_estimate=cost(8 * length * length * width, 10 * length * width),
        name="attn_fwd",
    )(flag, qkv, qkv, qkv)


def attn_bwd_kernel(tile, flag_ref, q_ref, k_ref, v_ref, g_ref, lse_ref, o_ref):
    length = q_ref.shape[0]
    width = o_ref.shape[1] // 3
    flag = flag_ref[0]
    lane = lax.broadcasted_iota(jnp.int32, (1, PAIR), 1)
    first = lane < HEAD
    scale = HEAD ** (-0.5)
    starts = list(range(0, length, tile))
    dk = [None] * len(starts)
    dv = [None] * len(starts)
    col = pl.multiple_of(pl.program_id(0) * PAIR, PAIR)
    for i, row0 in enumerate(starts):
        cols = row0 + tile
        ok = allowed_block(flag, row0, tile, cols, length // SHORT_SEQS)
        q = q_ref[row0 : row0 + tile, :]
        g = g_ref[row0 : row0 + tile, :]
        lse = lse_ref[row0 : row0 + tile, :]
        k = k_ref[0:cols, :]
        v = v_ref[0:cols, :]
        dqs, dks, dvs = [], [], []
        for h in range(2):
            mine = first if h == 0 else jnp.logical_not(first)
            qh = jnp.where(mine, q, jnp.zeros_like(q))
            gh = jnp.where(mine, g, jnp.zeros_like(g))
            s = jnp.where(ok, dot_nt(qh, k) * scale, NEG)
            p = jnp.exp(s - lse[:, h * HEAD : h * HEAD + 1])
            dp = dot_nt(gh, v)
            centre = jnp.sum(p * dp, axis=-1, keepdims=True)
            ds = (p * (dp - centre)).astype(BF16)
            dqs.append(dot_nn(ds, k))
            dks.append(dot_tn(ds, qh))
            dvs.append(dot_tn(p.astype(BF16), gh))
        o_ref[row0 : row0 + tile, pl.ds(col, PAIR)] = (
            jnp.where(first, dqs[0], dqs[1]) * scale
        ).astype(BF16)
        dk_all = dks[0] + dks[1]
        dv_all = dvs[0] + dvs[1]
        for j in range(i + 1):
            part_k = dk_all[j * tile : (j + 1) * tile]
            part_v = dv_all[j * tile : (j + 1) * tile]
            dk[j] = part_k if dk[j] is None else dk[j] + part_k
            dv[j] = part_v if dv[j] is None else dv[j] + part_v
    for j, row0 in enumerate(starts):
        o_ref[row0 : row0 + tile, pl.ds(width + col, PAIR)] = (dk[j] * scale).astype(BF16)
        o_ref[row0 : row0 + tile, pl.ds(2 * width + col, PAIR)] = dv[j].astype(BF16)


def attention_backward(qkv, flag, grad, lse, tile=256):
    length, width = qkv.shape[0], qkv.shape[1] // 3
    pairs = width // PAIR
    spec = lambda off: pl.BlockSpec((length, PAIR), lambda j: (0, off + j))
    return pl.pallas_call(
        functools.partial(attn_bwd_kernel, tile),
        grid=(pairs,),
        in_specs=[
            pl.BlockSpec(memory_space=pltpu.SMEM),
            spec(0),
            spec(pairs),
            spec(2 * pairs),
            spec(0),
            spec(0),
        ],
        out_specs=pl.BlockSpec((length, 3 * width), lambda j: (0, 0)),
        out_shape=jax.ShapeDtypeStruct((length, 3 * width), BF16),
        compiler_params=params(40),
        cost_estimate=cost(length, length),
        name="attn_bwd",
    )(flag, qkv, qkv, qkv, grad, lse)


def dense_kernel(mid_ref, dg_ref, up_ref, down_ref, out_ref, mg_ref, wu_ref, wd_ref):
    mid = mid_ref[...]
    dg = dg_ref[...]
    up = up_ref[...]
    down = down_ref[...]
    act, slope = gelu_pair(dot_nn(mid, up))
    act = act.astype(BF16)
    pg = (dot_nt(dg, down) * slope).astype(BF16)
    out = dot_nn(act, down)
    mg = dot_nt(pg, up)
    wu_ref[...] = dot_tn(mid, pg).astype(BF16)
    wd_ref[...] = dot_tn(act, dg).astype(BF16)

    @pl.when(pl.program_id(0) == 0)
    def _():
        out_ref[...] = out
        mg_ref[...] = mg

    @pl.when(pl.program_id(0) > 0)
    def _():
        out_ref[...] += out
        mg_ref[...] += mg


def dense_branch(mid, dg, up, down, tile=1024):
    length, width = mid.shape
    ff = up.shape[1]
    whole = pl.BlockSpec((length, width), lambda j: (0, 0))
    cols = pl.BlockSpec((width, tile), lambda j: (0, j))
    rows = pl.BlockSpec((tile, width), lambda j: (j, 0))
    return pl.pallas_call(
        dense_kernel,
        grid=(ff // tile,),
        in_specs=[whole, whole, cols, rows],
        out_specs=[whole, whole, cols, rows],
        out_shape=[
            jax.ShapeDtypeStruct((length, width), F32),
            jax.ShapeDtypeStruct((length, width), F32),
            jax.ShapeDtypeStruct((width, ff), BF16),
            jax.ShapeDtypeStruct((ff, width), BF16),
        ],
        compiler_params=params(48),
        cost_estimate=cost(length, length),
        name="dense_branch",
    )(mid, dg, up, down)


def expert_kernel(mid_ref, g_ref, mix_ref, up_ref, down_ref, po_ref, pi_ref, act_ref, pg_ref, eg_ref, dot_ref):
    mid = mid_ref[...]
    g = g_ref[...].astype(F32)
    logits = dot_nn(mid, mix_ref[...])
    share = two_shares(logits[:, 0:1], logits[:, 1:2])[1]
    eg = (share * g).astype(BF16)
    eg_ref[...] = eg
    act, slope = gelu_pair(dot_nn(mid, up_ref[...]))
    act = act.astype(BF16)
    act_ref[...] = act
    pg = (dot_nt(eg, down_ref[...]) * slope).astype(BF16)
    pg_ref[...] = pg
    pi_ref[...] = dot_nt(pg, up_ref[...]).astype(BF16)
    po = dot_nn(act, down_ref[...])
    po_ref[...] = po.astype(BF16)
    dot_ref[...] = jnp.sum(po * g, axis=-1, keepdims=True)


def expert_chunk(mid, g, mix_pad, up, down, tile=320):
    rows, width = mid.shape
    hidden = up.shape[1]
    block = pl.BlockSpec((tile, width), lambda i: (i, 0))
    hblock = pl.BlockSpec((tile, hidden), lambda i: (i, 0))
    full = lambda a: pl.BlockSpec(a.shape, lambda i: (0, 0))
    return pl.pallas_call(
        expert_kernel,
        grid=(rows // tile,),
        in_specs=[block, block, full(mix_pad), full(up), full(down)],
        out_specs=[block, block, hblock, hblock, block, pl.BlockSpec((tile, 1), lambda i: (i, 0))],
        out_shape=[
            jax.ShapeDtypeStruct((rows, width), BF16),
            jax.ShapeDtypeStruct((rows, width), BF16),
            jax.ShapeDtypeStruct((rows, hidden), BF16),
            jax.ShapeDtypeStruct((rows, hidden), BF16),
            jax.ShapeDtypeStruct((rows, width), BF16),
            jax.ShapeDtypeStruct((rows, 1), F32),
        ],
        compiler_params=params(48),
        cost_estimate=cost(8 * rows * width * hidden, 14 * rows * width + 4 * width * hidden),
        name="expert_chunk",
    )(mid, g, mix_pad, up, down)


def expert_grad_kernel(count, *refs):
    mids, pgs, acts, egs = (refs[i * count : (i + 1) * count] for i in range(4))
    du_ref, dd_ref = refs[4 * count :]
    up_sum = dot_tn(mids[0][...], pgs[0][...])
    down_sum = dot_tn(acts[0][...], egs[0][...])
    for i in range(1, count):
        up_sum += dot_tn(mids[i][...], pgs[i][...])
        down_sum += dot_tn(acts[i][...], egs[i][...])
    du_ref[...] = up_sum
    dd_ref[...] = down_sum


def expert_weight_grads(mids, pgs, acts, egs, tile=256):
    count = len(mids)
    rows, width = mids[0].shape
    hidden = pgs[0].shape[1]
    full = lambda a: pl.BlockSpec(a.shape, lambda j: (0, 0))
    cols = lambda a: pl.BlockSpec((a.shape[0], tile), lambda j: (0, j))
    return pl.pallas_call(
        functools.partial(expert_grad_kernel, count),
        grid=(hidden // tile,),
        in_specs=[full(a) for a in mids]
        + [cols(a) for a in pgs]
        + [cols(a) for a in acts]
        + [full(a) for a in egs],
        out_specs=[
            pl.BlockSpec((width, tile), lambda j: (0, j)),
            pl.BlockSpec((tile, width), lambda j: (j, 0)),
        ],
        out_shape=[jax.ShapeDtypeStruct((width, hidden), F32), jax.ShapeDtypeStruct((hidden, width), F32)],
        compiler_params=params(48),
        cost_estimate=cost(4 * count * rows * width * hidden, 8 * count * rows * width + 8 * width * hidden),
        name="expert_weight_grads",
    )(*mids, *pgs, *acts, *egs)


def exchange_kernel(
    waves, layers, groups, slots_ref, *refs
):
    gathered = 2 * layers - 1
    g_low = [refs[0], *refs[1:layers]]
    g_high = [refs[0], *refs[layers:gathered]]
    mix_ref, up_ref, down_ref, back_ref, slab_ref = refs[gathered : gathered + 5]
    po_refs = refs[gathered + 5 : gathered + layers + 5]
    (
        du_ref, dd_ref, g_refs, buf, part, got, act_s, pg_s, eg_s, home, home_slab,
        g_sem, a_send, a_recv, z_send, z_recv, r_send, r_recv, b_send, b_recv,
    ) = refs[gathered + layers + 5 :]
    each = groups // waves
    capacity, width = slots_ref.shape[1:]
    rows = each * capacity
    last = layers - 1
    here, me = lax.axis_index("dp"), lax.axis_index("ep")
    up_id, down_id = lax.rem(here + 1, layers), lax.rem(here + last, layers)
    peer = lambda j: lax.rem(me + j, groups)
    source = lambda j: lax.rem(me + groups - j, groups)
    mesh_id = pl.DeviceIdType.MESH

    def a_copy(j):
        return pltpu.make_async_remote_copy(
            slots_ref.at[peer(j)], buf.at[j // each, 0, lax.rem(j, each)],
            a_send.at[j], a_recv.at[j], device_id={"ep": peer(j)}, device_id_type=mesh_id,
        )

    def z_copy(w, way, s):
        src, dst = ((layers - s + 1) % layers, layers - s) if way == 0 else (s - 1, s)
        return [
            pltpu.make_async_remote_copy(
                buf.at[w, src], buf.at[w, dst], z_send.at[w, way, s - 1], z_recv.at[w, way, s - 1],
                device_id={"dp": up_id if way == 0 else down_id}, device_id_type=mesh_id,
            )
        ]

    lanes = -(-rows // 128) * 128
    main, extra_rows = pl.ds(0, rows), pl.ds(rows, 16)

    def r_copy(w, way, s):
        k = layers - s if way == 0 else s
        return [
            pltpu.make_async_remote_copy(
                src, dst, r_send.at[w, way, s - 1, n], r_recv.at[w, way, s - 1, n],
                device_id={"dp": up_id if way == 0 else down_id}, device_id_type=mesh_id,
            )
            for n, (src, dst) in enumerate(
                (
                    (part.at[w, k, main], got.at[w, way, s - 1, main]),
                    (
                        part.at[w, k, extra_rows, pl.ds(0, lanes)],
                        got.at[w, way, s - 1, extra_rows, pl.ds(0, lanes)],
                    ),
                )
            )
        ]

    def b_copies(j):
        w, i = j // each, lax.rem(j, each)
        start = pl.multiple_of(i * capacity, 16)
        return [
            pltpu.make_async_remote_copy(
                src, dst, b_send.at[j, n], b_recv.at[j, n],
                device_id={"ep": source(j)}, device_id_type=mesh_id,
            )
            for n, (src, dst) in enumerate(
                (
                    (part.at[w, 0, pl.ds(start, capacity)], home.at[j]),
                    (part.at[w, 0, extra_rows, pl.ds(0, lanes)], home_slab.at[j]),
                )
            )
        ]

    def z_sends(way, s):
        if way == 0:
            return jnp.logical_and(here <= last - 1, here >= s - 1)
        return jnp.logical_and(here >= 1, here <= layers - s)

    def z_gets(way, s):
        return here >= s if way == 0 else here <= last - s

    def r_sends(way, s):
        return here <= s - 1 if way == 0 else here >= layers - s

    def r_gets(way, s):
        if way == 0:
            return jnp.logical_and(here >= 1, here <= s)
        return jnp.logical_and(here >= last - s, here <= last - 1)

    def g_copy(ref, k):
        return pltpu.make_async_copy(ref, g_refs.at[k], g_sem.at[k])

    for k in range(layers):
        pl.when(here + k <= last)(lambda k=k: g_copy(g_high[k], k).start())
        if k:
            pl.when(here + k > last)(lambda k=k: g_copy(g_low[layers - k], k).start())

    part[...] = jnp.zeros_like(part)
    got[:, :, last - 1] = jnp.zeros_like(got[:, :, last - 1])
    du_ref[...] = jnp.zeros_like(du_ref)
    dd_ref[...] = jnp.zeros_like(dd_ref)

    barrier = pltpu.get_barrier_semaphore()

    def greet(j, carry):
        pl.semaphore_signal(barrier, inc=1, device_id={"ep": peer(j)}, device_id_type=mesh_id)
        return carry

    lax.fori_loop(1, groups, greet, 0)

    @pl.when(here < last)
    def _():
        pl.semaphore_signal(barrier, inc=1, device_id={"dp": up_id}, device_id_type=mesh_id)

    @pl.when(here > 0)
    def _():
        pl.semaphore_signal(barrier, inc=1, device_id={"dp": down_id}, device_id_type=mesh_id)

    pl.semaphore_wait(barrier, groups - 1 + jnp.where(here < last, 1, 0) + jnp.where(here > 0, 1, 0))

    def over(first, count, act):
        lax.fori_loop(first, count, lambda j, c: (act(j), c)[1], 0)

    over(1, groups, lambda j: a_copy(j).start())
    buf[0, 0, 0] = slots_ref[me]
    for k in range(layers):
        g_copy(g_high[k], k).wait()

    def slab_of(row):
        high = row.astype(BF16).astype(F32)
        line = lax.broadcasted_iota(jnp.int32, (16, rows), 0)
        return jnp.where(line == 0, high, jnp.where(line == 1, row - high, 0.0)).astype(BF16)

    def piece(w, ks):
        mid = jnp.concatenate([buf[w, k].reshape(rows, width) for k in ks], axis=0)
        g = jnp.concatenate(
            [g_refs[k, source(w * each + i)] for k in ks for i in range(each)], axis=0
        ).astype(F32)
        logits = dot_nn(mid, mix_ref[...])
        share = two_shares(logits[:, 0:1], logits[:, 1:2])[1]
        eg = (share * g).astype(BF16)
        act, slope = gelu_pair(dot_nn(mid, up_ref[...]))
        act = act.astype(BF16)
        pg = (dot_nt(eg, down_ref[...]) * slope).astype(BF16)
        pi = dot_nt(pg, up_ref[...]).astype(BF16)
        po = dot_nn(act, down_ref[...])
        sums = jnp.sum(po * g, axis=-1, keepdims=True)
        po = po.astype(BF16)
        diag = lax.broadcasted_iota(jnp.int32, (rows, rows), 0) == lax.broadcasted_iota(
            jnp.int32, (rows, rows), 1
        )
        for n, k in enumerate(ks):
            mine = slice(n * rows, (n + 1) * rows)
            spot = slice(k * rows, (k + 1) * rows)
            eg_s[spot] = eg[mine]
            act_s[spot] = act[mine]
            pg_s[spot] = pg[mine]
            part[w, k, 0:rows] = pi[mine]
            line = jnp.sum(jnp.where(diag, sums[mine], 0.0), axis=0, keepdims=True)
            part[w, k, rows : rows + 16, 0:rows] = slab_of(line)
            for i in range(each):
                at = n * rows + i * capacity
                po_refs[k][source(w * each + i)] = po[at : at + capacity]

    def weight_grads(w):
        mid = buf[w].reshape(layers * rows, width)
        du_ref[...] += dot_tn(mid, pg_s[...])
        dd_ref[...] += dot_tn(act_s[...], eg_s[...])

    def add_to(w, k, pieces):
        total = part[w, k, 0:rows].astype(F32)
        extra = part[w, k, rows : rows + 16, 0:rows].astype(F32)
        for way, s in pieces:
            total = total + got[w, way, s - 1, 0:rows].astype(F32)
            extra = extra + got[w, way, s - 1, rows : rows + 16, 0:rows].astype(F32)
        part[w, k, 0:rows] = total.astype(BF16)
        part[w, k, rows : rows + 16, 0:rows] = slab_of(jnp.sum(extra, axis=0, keepdims=True))

    def start_hop(copy, sends, w, s):
        for way in range(2):
            pl.when(sends(way, s))(lambda way=way: [c.start() for c in copy(w, way, s)][:0] or None)

    def get_hop(copy, gets, w, s):
        for way in range(2):
            pl.when(gets(way, s))(lambda way=way: [c.wait_recv() for c in copy(w, way, s)][:0] or None)

    def pass_on(w, s):
        for way in range(2):

            @pl.when(r_gets(way, s))
            def _():
                for copy in r_copy(w, way, s):
                    copy.wait_recv()
                add_to(w, layers - s - 1 if way == 0 else s + 1, [(way, s)])

        start_hop(r_copy, r_sends, w, s + 1)

    def finish(w):
        get_hop(r_copy, r_gets, w, last)
        add_to(w, 0, [(0, last), (1, last)])
        for i in range(each):
            j = w * each + i
            start = i * capacity

            @pl.when(j > 0)
            def _():
                for copy in b_copies(j):
                    copy.start()

            @pl.when(j == 0)
            def _():
                home[0] = part[0, 0, start : start + capacity]
                home_slab[0] = part[0, 0, rows : rows + 16, 0:lanes]

    def first_hop(w):
        for n in range(each):
            pl.when(w * each + n > 0)(lambda n=n: a_copy(w * each + n).wait_recv())
        start_hop(z_copy, z_sends, w, 1)

    far = [1, last]
    near = [k for k in range(layers) if k not in far]

    def valid(w):
        return jnp.logical_and(w >= 0, w < waves)

    def body(t, carry):
        for s in range(1, layers):
            pl.when(valid(t - s))(lambda s=s: get_hop(z_copy, z_gets, t - s, s))
        for s in range(2, layers):
            pl.when(valid(t + 1 - s))(lambda s=s: start_hop(z_copy, z_sends, t + 1 - s, s))
        pl.when(t + 1 < waves)(lambda: first_hop(t + 1))
        w = t - last

        @pl.when(valid(w))
        def _():
            piece(w, far)
            start_hop(r_copy, r_sends, w, 1)

        for s in range(1, last):
            pl.when(valid(w - s))(lambda s=s: pass_on(w - s, s))
        pl.when(valid(w - last))(lambda: finish(w - last))

        @pl.when(valid(w))
        def _():
            piece(w, near)
            weight_grads(w)

        return carry

    first_hop(0)
    lax.fori_loop(0, waves + 2 * last, body, 0)

    def land(j, carry):
        for copy in b_copies(j):
            copy.wait_recv()
            copy.wait_send()
        a_copy(j).wait_send()
        return carry

    lax.fori_loop(1, groups, land, 0)

    def sent(w, carry):
        for way in range(2):
            for s in range(1, layers):
                for copy, sends in ((z_copy, z_sends), (r_copy, r_sends)):

                    @pl.when(sends(way, s))
                    def _():
                        for one in copy(w, way, s):
                            one.wait_send()

        return carry

    lax.fori_loop(0, waves, sent, 0)

    def arrange(j, carry):
        back_ref[peer(j)] = home[j]
        slab_ref[peer(j)] = home_slab[j]
        return carry

    lax.fori_loop(0, groups, arrange, 0)


def exchange_waves(groups):
    return 8 if groups % 8 == 0 else 1


def expert_exchange(slots, g_low, g_high, mix_pad, up, down):
    layers, groups = lax.axis_size("dp"), lax.axis_size("ep")
    waves = exchange_waves(groups)
    each = groups // waves
    _, capacity, width = slots.shape
    hidden = up.shape[1]
    rows = each * capacity
    lanes = -(-rows // 128) * 128
    sem = pltpu.SemaphoreType.DMA
    block = jax.ShapeDtypeStruct((groups, capacity, width), BF16)
    vmem = pl.BlockSpec(memory_space=pltpu.VMEM)
    total_rows = layers * groups * capacity
    outs = pl.pallas_call(
        functools.partial(exchange_kernel, waves, layers, groups),
        in_specs=[vmem] + [pl.BlockSpec(memory_space=pl.ANY)] * (2 * layers - 1) + [vmem] * 3,
        out_specs=[vmem] * (4 + layers),
        out_shape=[block, jax.ShapeDtypeStruct((groups, 16, lanes), BF16)]
        + [block] * layers
        + [jax.ShapeDtypeStruct((width, hidden), F32), jax.ShapeDtypeStruct((hidden, width), F32)],
        scratch_shapes=[
            pltpu.VMEM((layers, groups, capacity, width), BF16),
            pltpu.VMEM((waves, layers, each, capacity, width), BF16),
            pltpu.VMEM((waves, layers, rows + 16, width), BF16),
            pltpu.VMEM((waves, 2, layers - 1, rows + 16, width), BF16),
            pltpu.VMEM((layers * rows, hidden), BF16),
            pltpu.VMEM((layers * rows, hidden), BF16),
            pltpu.VMEM((layers * rows, width), BF16),
            pltpu.VMEM((groups, capacity, width), BF16),
            pltpu.VMEM((groups, 16, lanes), BF16),
            sem((layers,)),
            sem((groups,)),
            sem((groups,)),
            sem((waves, 2, layers - 1)),
            sem((waves, 2, layers - 1)),
            sem((waves, 2, layers - 1, 2)),
            sem((waves, 2, layers - 1, 2)),
            sem((groups, 2)),
            sem((groups, 2)),
        ],
        compiler_params=pltpu.CompilerParams(
            collective_id=0, has_side_effects=True, vmem_limit_bytes=62 << 20
        ),
        cost_estimate=cost(12 * total_rows * width * hidden, 20 * total_rows * width),
        name="expert_exchange",
    )(slots, *g_low, *g_high[1:], mix_pad, up, down)
    return outs[0], outs[1], outs[2 : 2 + layers], outs[2 + layers], outs[3 + layers]


def sums_kernel(plan, split, layers, groups, small_ref, *refs):
    count = len(plan)
    mats, outs = refs[:count], refs[count : 2 * count]
    (
        small_out, own, sib, got, held, inner, final, small_two, small_chip, small_layer,
        own_sem, s_send, s_recv, x_send, x_recv, z_send, z_recv, t_send, t_recv, o_sem,
    ) = refs[2 * count :]
    chips = groups // 2
    width = held.shape[-1]
    total = held.shape[0]
    last = layers - 1
    here, me = lax.axis_index("dp"), lax.axis_index("ep")
    core, chip = lax.rem(me, 2), me // 2
    sibling = me + 1 - 2 * core
    mesh_id = pl.DeviceIdType.MESH
    chip_at = lambda j: lax.rem(chip + j, chips)
    pieces = [(m, i, n) for m in range(count) for i in range(plan[m]) for n in range(split)]
    lines = held.shape[1]
    square = chips == 4
    by_one = chip + 1 - 2 * lax.rem(chip, 2)
    by_two = chip + 2 - 4 * (chip // 2)
    at_end = jnp.logical_or(here == 0, here == last)
    inside = jnp.logical_and(here > 0, here < last)
    inward = 1 + (here // last) * (last - 2)
    outward = lax.rem((here - 1) * last + layers * last, layers)
    across = last - here

    def source(m, i, n, half):
        span = pl.ds(n * lines, lines)
        if len(mats[m].shape) == 5:
            return mats[m].at[:, half, i, span]
        return mats[m].at[:, half, span, pl.ds(i * width, width)]

    def remote(src, dst, send, recv, where):
        return pltpu.make_async_remote_copy(
            src, dst, send, recv, device_id=where, device_id_type=mesh_id
        )

    def s_copy(c):
        return remote(source(*pieces[c], 1 - core), sib.at[c], s_send.at[c], s_recv.at[c], {"ep": sibling})

    def x_copy(c, j):
        return remote(
            own.at[c, chip_at(j)], got.at[c, j - 1], x_send.at[c, j - 1], x_recv.at[c, j - 1],
            {"ep": 2 * chip_at(j) + core},
        )

    def near_chip(c):
        return by_one + lax.rem(c, 2) * (by_two - by_one)

    def next_chip(c):
        return by_two + lax.rem(c, 2) * (by_one - by_two)

    def y_copy(c, n):
        block = (near_chip(c), 3 - chip, next_chip(c))[n]
        where = next_chip(c) if n == 2 else near_chip(c)
        return remote(
            own.at[c, block], got.at[c, n], x_send.at[c, n], x_recv.at[c, n], {"ep": 2 * where + core}
        )

    lags = [LAG * n for n in range(1, 6)] if square else [0] + [LAG * n for n in range(1, 5)]

    def due(t, n):
        return jnp.logical_and(t >= lags[n], t < total + lags[n])

    def z_copy(c, n):
        src = (held, held, inner)[n]
        dst = (inner, final, final)[n]
        where = (inward, across, outward)[n]
        return remote(src.at[c], dst.at[c], z_send.at[c, n], z_recv.at[c, n], {"dp": where})

    def t_copy(n, j):
        if n == 0:
            return remote(small_ref, small_two, t_send.at[0, 0], t_recv.at[0, 0], {"ep": sibling})
        if n == 1:
            spot = small_chip.at[chip]
            return remote(spot, spot, t_send.at[1, j], t_recv.at[1, j], {"ep": 2 * chip_at(j) + core})
        spot = small_layer.at[here]
        return remote(
            spot, spot, t_send.at[2, j], t_recv.at[2, j], {"dp": lax.rem(here + j, layers)}
        )

    for c in range(total):
        pltpu.make_async_copy(source(*pieces[c], core), own.at[c], own_sem.at[c]).start()

    barrier = pltpu.get_barrier_semaphore()
    pl.semaphore_signal(barrier, inc=1, device_id={"ep": sibling}, device_id_type=mesh_id)

    def over(first, end, act):
        def step(j, carry):
            act(j)
            return carry

        lax.fori_loop(first, end, step, 0)

    over(
        1,
        chips,
        lambda j: pl.semaphore_signal(
            barrier, inc=1, device_id={"ep": 2 * chip_at(j) + core}, device_id_type=mesh_id
        ),
    )
    over(
        1,
        layers,
        lambda j: pl.semaphore_signal(
            barrier, inc=1, device_id={"dp": lax.rem(here + j, layers)}, device_id_type=mesh_id
        ),
    )
    pl.semaphore_wait(barrier, chips + last)

    t_copy(0, 0).start()
    for c in range(total):
        s_copy(c).start()

    def body(t, carry):
        @pl.when(t < total)
        def _():
            pltpu.make_async_copy(sib.at[t], own.at[t], own_sem.at[t]).wait()
            remote(own.at[t], sib.at[t], s_send.at[t], s_recv.at[t], {"ep": sibling}).wait_recv()

            def add(p):
                own[t, p] = own[t, p] + sib[t, p]

            over(0, chips, add)
            if square:
                y_copy(t, 1).start()
                y_copy(t, 0).start()
            else:
                over(1, chips, lambda j: x_copy(t, j).start())

        if square:

            @pl.when(due(t, 0))
            def _():
                c = t - lags[0]
                y_copy(c, 1).wait_recv()
                own[c, next_chip(c)] = own[c, next_chip(c)] + got[c, 1]
                y_copy(c, 2).start()
                y_copy(c, 0).wait_recv()
                own[c, chip] = own[c, chip] + got[c, 0]

        @pl.when(due(t, 1))
        def _():
            c = t - lags[1]
            if square:
                y_copy(c, 2).wait_recv()
                held[c] = own[c, chip] + got[c, 2]
            else:
                over(1, chips, lambda j: x_copy(c, j).wait_recv())
                held[c] = lax.fori_loop(
                    1, chips, lambda j, acc: acc + got[c, j - 1].astype(F32), own[c, chip].astype(F32)
                ).astype(BF16)
            pl.when(at_end)(lambda: z_copy(c, 0).start())

        @pl.when(jnp.logical_and(inside, due(t, 2)))
        def _():
            c = t - lags[2]
            z_copy(c, 0).wait_recv()
            held[c] = held[c] + inner[c]
            z_copy(c, 1).start()

        @pl.when(jnp.logical_and(inside, due(t, 3)))
        def _():
            c = t - lags[3]
            z_copy(c, 1).wait_recv()
            inner[c] = held[c] + final[c]
            z_copy(c, 2).start()

        @pl.when(jnp.logical_and(at_end, due(t, 4)))
        def _():
            c = t - lags[4]
            z_copy(c, 2).wait_recv()

        @pl.when(t == 1)
        def _():
            t_copy(0, 0).wait_recv()
            small_chip[chip] = small_ref[...] + small_two[...]
            over(1, chips, lambda j: t_copy(1, j).start())

        @pl.when(t == 3)
        def _():
            over(1, chips, lambda j: t_copy(1, j).wait_recv())
            acc = small_chip[0]
            for n in range(1, chips):
                acc = acc + small_chip[n]
            small_layer[here] = acc
            over(1, layers, lambda j: t_copy(2, j).start())

        return carry

    lax.fori_loop(0, total + lags[4], body, 0)

    def result(sums, c):
        m, i, n = pieces[c]
        span = pl.ds(n * lines, lines)
        if len(outs[m].shape) == 3:
            spot = outs[m].at[i, span]
        else:
            spot = outs[m].at[span, pl.ds(i * width, width)]
        return pltpu.make_async_copy(sums.at[c], spot, o_sem.at[c])

    @pl.when(inside)
    def _():
        for c in range(total):
            result(inner, c).start()

    @pl.when(at_end)
    def _():
        for c in range(total):
            result(final, c).start()

    over(1, layers, lambda j: t_copy(2, j).wait_recv())
    acc = small_layer[0]
    for n in range(1, layers):
        acc = acc + small_layer[n]
    small_out[...] = acc

    t_copy(0, 0).wait_send()
    over(1, chips, lambda j: t_copy(1, j).wait_send())
    over(1, layers, lambda j: t_copy(2, j).wait_send())

    def sent(c):
        remote(own.at[c], sib.at[c], s_send.at[c], s_recv.at[c], {"ep": sibling}).wait_send()
        if square:
            for n in range(3):
                y_copy(c, n).wait_send()
        else:
            over(1, chips, lambda j: x_copy(c, j).wait_send())
        pl.when(at_end)(lambda: z_copy(c, 0).wait_send())

        @pl.when(inside)
        def _():
            z_copy(c, 1).wait_send()
            z_copy(c, 2).wait_send()

    over(0, total, sent)
    for c in range(total):
        result(final, c).wait()


def gradient_sums(small, columns, rows_split):
    layers, groups = lax.axis_size("dp"), lax.axis_size("ep")
    chips = groups // 2
    width = small.shape[1]
    plan = [a.shape[1] // width for a in columns] + [a.shape[0] // width for a in rows_split]
    high = columns[0].shape[0] // groups
    split = SPLIT if high % (16 * SPLIT) == 0 else 1
    total, lines = sum(plan) * split, high // split
    views = [a.reshape(chips, 2, high, a.shape[1]) for a in columns] + [
        a.reshape(chips, 2, n, high, width) for a, n in zip(rows_split, plan[len(columns) :])
    ]
    shapes = [jax.ShapeDtypeStruct((high, a.shape[1]), BF16) for a in columns] + [
        jax.ShapeDtypeStruct((n, high, width), BF16) for n in plan[len(columns) :]
    ]
    sem = pltpu.SemaphoreType.DMA
    vmem = pl.BlockSpec(memory_space=pltpu.VMEM)
    anywhere = pl.BlockSpec(memory_space=pl.ANY)
    buffers = lambda *lead: pltpu.VMEM((total, *lead, lines, width), BF16)
    outs = pl.pallas_call(
        functools.partial(sums_kernel, plan, split, layers, groups),
        in_specs=[vmem] + [anywhere] * len(views),
        out_specs=[anywhere] * len(views) + [vmem],
        out_shape=shapes + [jax.ShapeDtypeStruct(small.shape, F32)],
        scratch_shapes=[
            buffers(chips),
            buffers(chips),
            buffers(chips - 1),
            buffers(),
            buffers(),
            buffers(),
            pltpu.VMEM(small.shape, F32),
            pltpu.VMEM((chips, *small.shape), F32),
            pltpu.VMEM((layers, *small.shape), F32),
            sem((total,)),
            sem((total,)),
            sem((total,)),
            sem((total, chips - 1)),
            sem((total, chips - 1)),
            sem((total, 3)),
            sem((total, 3)),
            sem((3, max(chips, layers))),
            sem((3, max(chips, layers))),
            sem((total,)),
        ],
        compiler_params=pltpu.CompilerParams(
            collective_id=1, has_side_effects=True, vmem_limit_bytes=62 << 20
        ),
        cost_estimate=cost(10 * total * chips * lines * width, 8 * total * chips * lines * width),
        name="gradient_sums",
    )(small, *views)
    rows_out = [a.reshape(-1, width) for a in outs[len(columns) : -1]]
    return (*outs[: len(columns)], *rows_out, outs[-1])


def spread_kernel(
    layers, groups, slots_ref, own_ref, low_ref, high_ref, low_two, high_two, a_send, a_recv, z_send, z_recv
):
    last = layers - 1
    here, me = lax.axis_index("dp"), lax.axis_index("ep")
    peer = lambda j: lax.rem(me + j, groups)
    source = lambda j: lax.rem(me + groups - j, groups)
    up_id, down_id = lax.rem(here + 1, layers), lax.rem(here + last, layers)
    mesh_id = pl.DeviceIdType.MESH

    def a_copy(j):
        return pltpu.make_async_remote_copy(
            slots_ref.at[peer(j)], own_ref.at[me], a_send.at[j], a_recv.at[j],
            device_id={"ep": peer(j)}, device_id_type=mesh_id,
        )

    def z_copy(j, way, s=0):
        src = (own_ref, (low_ref, high_ref)[way])[s]
        dst = ((low_ref, high_ref), (low_two, high_two))[s][way]
        n = 2 * s + way
        return pltpu.make_async_remote_copy(
            src.at[source(j)], dst.at[source(j)], z_send.at[j, n], z_recv.at[j, n],
            device_id={"dp": up_id if way == 0 else down_id}, device_id_type=mesh_id,
        )

    def over(first, count, act):
        def step(j, carry):
            act(j)
            return carry

        lax.fori_loop(first, count, step, 0)

    barrier = pltpu.get_barrier_semaphore()

    def greet(where):
        pl.semaphore_signal(barrier, inc=1, device_id=where, device_id_type=mesh_id)

    over(1, groups, lambda j: greet({"ep": peer(j)}))
    pl.when(here < last)(lambda: greet({"dp": up_id}))
    pl.when(here > 0)(lambda: greet({"dp": down_id}))
    pl.semaphore_wait(barrier, groups - 1 + jnp.where(here < last, 1, 0) + jnp.where(here > 0, 1, 0))

    over(1, groups, lambda j: a_copy(j).start())
    own_ref[me] = slots_ref[me]

    def pass_on(j):
        pl.when(here < last)(lambda: z_copy(j, 0).start())
        pl.when(here > 0)(lambda: z_copy(j, 1).start())

    pass_on(0)

    def forward(j):
        pl.when(here > 0)(lambda: z_copy(j, 0).wait_recv())
        pl.when(here < last)(lambda: z_copy(j, 1).wait_recv())

        @pl.when(jnp.logical_and(here > 0, here < last))
        def _():
            z_copy(j, 0, 1).start()
            z_copy(j, 1, 1).start()

    def arrived(j):
        a_copy(j).wait_recv()
        pass_on(j)
        forward(j - 1)

    over(1, groups, arrived)
    forward(groups - 1)

    def settle(j):
        pl.when(here > 1)(lambda: z_copy(j, 0, 1).wait_recv())
        pl.when(here < last - 1)(lambda: z_copy(j, 1, 1).wait_recv())

        @pl.when(jnp.logical_and(here > 0, here < last))
        def _():
            z_copy(j, 0, 1).wait_send()
            z_copy(j, 1, 1).wait_send()

        pl.when(here < last)(lambda: z_copy(j, 0).wait_send())
        pl.when(here > 0)(lambda: z_copy(j, 1).wait_send())

    over(0, groups, settle)
    over(1, groups, lambda j: a_copy(j).wait_send())


def spread(slots):
    layers, groups = lax.axis_size("dp"), lax.axis_size("ep")
    vmem = pl.BlockSpec(memory_space=pltpu.VMEM)
    sem = pltpu.SemaphoreType.DMA
    return pl.pallas_call(
        functools.partial(spread_kernel, layers, groups),
        in_specs=[vmem],
        out_specs=[vmem] * 5,
        out_shape=[jax.ShapeDtypeStruct(slots.shape, BF16)] * 5,
        scratch_shapes=[sem((groups,)), sem((groups,)), sem((groups, 4)), sem((groups, 4))],
        compiler_params=pltpu.CompilerParams(
            collective_id=2, has_side_effects=True, vmem_limit_bytes=16 << 20
        ),
        cost_estimate=cost(slots.size, 4 * slots.size),
        name="spread",
    )(slots)


def normalise(values_in):
    centred = values_in - jnp.mean(values_in, axis=-1, keepdims=True)
    inverse = lax.rsqrt(jnp.mean(centred * centred, axis=-1, keepdims=True) + 1e-05)
    return centred * inverse, inverse


def norm_backward(grad, gain_vec, unit, inverse):
    m = grad * gain_vec
    return inverse * (
        m
        - jnp.mean(m, axis=-1, keepdims=True)
        - unit * jnp.mean(m * unit, axis=-1, keepdims=True)
    )


def hop(rows, step, stage):
    size = lax.axis_size("dp")
    if step > 0:
        pairs = [(i, i + 1) for i in range(stage - 1, size - 1)]
    else:
        pairs = [(i + 1, i) for i in range(0, size - stage)]
    return lax.ppermute(rows, "dp", pairs)


def both_hops(low, high, stage):
    return hop(low, 1, stage), hop(high, -1, stage)


def send_hop(rows, step, stage):
    size = lax.axis_size("dp")
    if step > 0:
        pairs = [(i, i + 1) for i in range(stage)]
    else:
        pairs = [(i, i - 1) for i in range(size - stage, size)]
    return lax.ppermute(rows, "dp", pairs)


def line_reduce(parts):
    size = lax.axis_size("dp")
    up = send_hop(parts[size - 1], 1, 1)
    down = send_hop(parts[1], -1, 1)
    for stage in range(2, size):
        up = send_hop(up + parts[size - stage], 1, stage)
        down = send_hop(down + parts[stage], -1, stage)
    return parts[0].astype(F32) + up.astype(F32) + down.astype(F32)


def shifted(rows, step):
    size = lax.axis_size("dp")
    return lax.ppermute(rows, "dp", [((i + step) % size, i) for i in range(size)])


def after(values, *earlier):
    many = isinstance(values, tuple)
    held = lax.optimization_barrier((*values, *earlier) if many else (values, *earlier))
    return held[: len(values)] if many else held[0]


def sum_layers(rows):
    size, here = lax.axis_size("dp"), lax.axis_index("dp")
    pieces = rows.reshape(size, rows.shape[0] // size, rows.shape[1])
    piece = lambda k: lax.dynamic_index_in_dim(pieces, lax.rem(here + k, size), 0, keepdims=False)
    acc = piece(0).astype(F32)
    for k in range(1, size):
        acc = acc + shifted(piece(k), size - k).astype(F32)
    mine = acc.astype(BF16)
    ring = jnp.stack([mine] + [shifted(mine, k) for k in range(1, size)])
    ordered = lax.dynamic_slice_in_dim(jnp.concatenate([ring, ring]), size - here, size, 0)
    return ordered.reshape(rows.shape).astype(F32)


def sum_everywhere(values):
    for axis in ("dp", "ep"):
        size = lax.axis_size(axis)
        step = 1
        while step < size:
            values = values + lax.ppermute(values, axis, [(i, i ^ step) for i in range(size)])
            step *= 2
    return values


def on_device(
    tokens,
    bucket,
    expert_ids,
    ln1_gain,
    qkv_weight,
    out_weight,
    ln2_gain,
    up_weight,
    down_weight,
    mix_weight,
    expert_up,
    expert_down,
    cotangent,
):
    length, width = tokens.shape
    groups = lax.axis_size("ep")
    layers = lax.axis_size("dp")
    experts = groups * expert_up.shape[0]
    capacity = 5 * length // (4 * experts)
    slots = experts * capacity
    gather = lambda w: lax.all_gather(w, "ep", axis=0, tiled=True)
    exchange_out = lambda a: lax.all_to_all(a, "ep", split_axis=0, concat_axis=1, tiled=True)
    expert_up2 = expert_up[0]
    expert_down2 = expert_down[0]
    mix_pad = jnp.pad(mix_weight, ((0, 0), (0, 126)))

    chosen = expert_ids[:, 0]
    one_hot = chosen[:, None] == jnp.arange(experts, dtype=jnp.int32)[None, :]
    place = jnp.arange(length, dtype=jnp.int32)
    earlier = (place[None, :] < place[:, None]).astype(BF16)
    before = dot_nn(earlier, one_hot.astype(BF16))
    slot_index = jnp.sum(jnp.where(one_hot, before, 0.0), axis=1).astype(jnp.int32)
    target = jnp.where(slot_index < capacity, chosen * capacity + slot_index, -1)
    table = (target[:, None] == jnp.arange(slots, dtype=jnp.int32)[None, :]).astype(BF16)

    pick = lambda rows: dot_tn(table, rows).astype(BF16).reshape(experts, capacity, width)
    join = lambda lows, highs: [highs[k] + lows[layers - k] for k in range(1, layers)]

    token_rows = tokens.astype(F32)
    unit1, inverse1 = normalise(token_rows)
    normed_in = (unit1 * ln1_gain).astype(BF16)
    qkv_full, out_full, up_full, down_full = (
        gather(qkv_weight),
        gather(out_weight),
        gather(up_weight),
        gather(down_weight),
    )
    by_kernels = capacity % 16 == 0 and layers > 2
    if by_kernels:
        g_own, *g_first = [a.reshape(slots, width) for a in spread(pick(cotangent))]
        g_low, g_high = [g_own, *g_first[0::2]], [g_own, *g_first[1::2]]
    else:
        g_own = exchange_out(pick(cotangent)).reshape(slots, width)
        low, high = both_hops(g_own, g_own, 1)
        g_low, g_high = [g_own, low], [g_own, high]

    def step(lows, highs, *others):
        stage = len(lows)
        held = lax.optimization_barrier((lows[-1], highs[-1], *others))
        lows[-1], highs[-1] = held[:2]
        if stage < layers:
            low, high = both_hops(lows[-1], highs[-1], stage)
            lows.append(low)
            highs.append(high)
        return held[2:]

    (normed_in,) = step(g_low, g_high, normed_in)
    qkv_rows = dot_nn(normed_in, qkv_full).astype(BF16)
    while len(g_low) < layers:
        (qkv_rows,) = step(g_low, g_high, qkv_rows)
    attended, lse = attention_forward(qkv_rows, bucket)
    hidden_res = token_rows + dot_nn(attended, out_full)
    unit2, inverse2 = normalise(hidden_res)
    mid_low = (unit2 * ln2_gain).astype(BF16)
    mid_slots = pick(mid_low)
    (mid_slots,) = step(g_low, g_high, mid_slots)

    grad_out = cotangent.astype(F32)
    logits = dot_nn(mid_low, mix_weight)
    mix0, mix1 = two_shares(logits[:, 0:1], logits[:, 1:2])
    dense_grad = (mix0 * grad_out).astype(BF16)
    scatter = lambda a: lax.psum_scatter(a.astype(BF16), "ep", scatter_dimension=0, tiled=True)
    back = lambda k, a: shifted(a, layers - k) if k else a

    def total(parts):
        acc = parts[0].astype(F32)
        for part in parts[1:]:
            acc = acc + part.astype(F32)
        return acc

    if by_kernels:
        blocks = lambda many: [g.reshape(groups, capacity, width) for g in many]
        returned, slab, partial_outs, expert_up_grad, expert_down_grad = expert_exchange(
            mid_slots, blocks(g_low), blocks(g_high), mix_pad, expert_up2, expert_down2
        )
        each = groups // exchange_waves(groups)
        offset = lax.rem(
            jnp.arange(groups, dtype=jnp.int32) + groups - lax.axis_index("ep"), groups
        )
        spot = lax.rem(offset, each)[:, None] == jnp.arange(each, dtype=jnp.int32)[None, :]
        lines = slab[:, 0, : each * capacity].astype(F32) + slab[:, 1, : each * capacity].astype(F32)
        dot_back = jnp.sum(
            jnp.where(spot[:, :, None], lines.reshape(groups, each, capacity), 0.0), axis=1
        ).reshape(1, slots)
        dense_grad, returned = lax.optimization_barrier((dense_grad, returned))
        outs = [a.reshape(slots, width) for a in partial_outs]
    else:
        gs = [g_own] + join(g_low, g_high)
        mid_own = exchange_out(mid_slots).reshape(slots, width)
        mids = [mid_own] + [shifted(mid_own, k) for k in range(1, layers)]
        chunks = [expert_chunk(mids[k], gs[k], mix_pad, expert_up2, expert_down2) for k in range(layers)]
        in_total = line_reduce([c[1] for c in chunks])
        dot_sum = total([back(k, chunks[k][5].reshape(groups, capacity)) for k in range(layers)])
        dot_high = lax.reduce_precision(dot_sum, 8, 7)
        extra = jnp.stack([dot_high, dot_sum - dot_high], axis=1)
        extra = jnp.pad(extra, ((0, 0), (0, 14), (0, width - capacity)))
        packed = jnp.concatenate([in_total.reshape(groups, capacity, width), extra], axis=1)
        both = lax.all_to_all(packed.astype(BF16), "ep", split_axis=0, concat_axis=0, tiled=True)
        returned = both[:, :capacity]
        dot_back = (
            both[:, capacity, :capacity].astype(F32) + both[:, capacity + 1, :capacity].astype(F32)
        ).reshape(1, slots)
        outs = [c[0] for c in chunks]
        expert_up_grad, expert_down_grad = expert_weight_grads(
            mids, [c[3] for c in chunks], [c[2] for c in chunks], [c[4] for c in chunks]
        )

    outs = [back(k, outs[k]) for k in range(layers)]
    dense_out, mid_grad_dense, up_grad, down_grad = dense_branch(mid_low, dense_grad, up_full, down_full)
    in_rows = returned.reshape(slots, width)
    mix_dot1 = jnp.sum(table.astype(F32) * dot_back, axis=1, keepdims=True)
    mix_dot0 = jnp.sum(grad_out * dense_out, axis=-1, keepdims=True)
    mean_dot = mix0 * mix_dot0 + mix1 * mix_dot1
    logit_grad = jnp.concatenate(
        [mix0 * (mix_dot0 - mean_dot), mix1 * (mix_dot1 - mean_dot)], axis=1
    ).astype(BF16)
    mix_weight_grad = dot_tn(mid_low, logit_grad)
    mid_grad = mid_grad_dense + dot_nt(logit_grad, mix_weight) + dot_nn(table, in_rows)
    ln2_gain_grad = jnp.sum(mid_grad * unit2, axis=0)
    res_grad = grad_out + norm_backward(mid_grad, ln2_gain, unit2, inverse2)
    attn_out_grad = res_grad.astype(BF16)
    out_weight_grad = dot_tn(attended, attn_out_grad)
    attended_grad = dot_nt(attn_out_grad, out_full).astype(BF16)
    qkv_grad = attention_backward(qkv_rows, bucket, attended_grad, lse)
    qkv_weight_grad = dot_tn(normed_in, qkv_grad)
    normed_grad = dot_nt(qkv_grad, qkv_full)
    ln1_gain_grad = jnp.sum(normed_grad * unit1, axis=0)
    tokens_grad = res_grad + norm_backward(normed_grad, ln1_gain, unit1, inverse1)

    small = jnp.concatenate([ln1_gain_grad[None], ln2_gain_grad[None], mix_weight_grad.T], axis=0)
    small = jnp.pad(small, ((0, 4), (0, 0)))
    if layers == 4 and length // groups >= 16:
        qkv_final, out_final, up_final, down_final, small_sums = gradient_sums(
            small,
            [a.astype(BF16) for a in (qkv_weight_grad, out_weight_grad, up_grad)],
            [down_grad],
        )
    else:
        sums = [sum_layers(scatter(a)) for a in (qkv_weight_grad, out_weight_grad, up_grad, down_grad)]
        qkv_final, out_final, up_final, down_final = sums
        small_sums = sum_everywhere(small)
    outs = list(after(tuple(outs), small_sums))
    out_sum = total(outs).astype(BF16).reshape(groups, capacity, width)
    out_back = lax.all_to_all(out_sum, "ep", split_axis=0, concat_axis=0, tiled=True)
    bucket, qkv_final, out_final, up_final, down_final = after(
        (bucket, qkv_final, out_final, up_final, down_final), out_sum
    )
    unit = jnp.where(bucket[0] < 0, 0.0, 1.0)
    expert_up_grad, expert_down_grad, qkv_final, out_final, up_final, down_final, out_back = (
        lax.optimization_barrier(
            (
                expert_up_grad * unit,
                expert_down_grad * unit,
                *(a.astype(F32) for a in (qkv_final, out_final, up_final, down_final)),
                out_back,
            )
        )
    )
    expert_out = dot_nn(table, out_back.reshape(slots, width))
    result = (hidden_res + mix0 * dense_out + mix1 * expert_out).astype(BF16)
    return (
        result,
        tokens_grad,
        small_sums[0],
        qkv_final,
        out_final,
        small_sums[1],
        up_final,
        down_final,
        small_sums[2:4].T,
        expert_up_grad[None],
        expert_down_grad[None],
    )


def solution(mesh):
    placed = (
        P(("dp", "ep"), None),
        P(("dp", "ep")),
        P(("dp", "ep"), None),
        P(),
        P("ep", None),
        P("ep", None),
        P(),
        P("ep", None),
        P("ep", None),
        P(),
        P("ep", None, "dp"),
        P("ep", "dp", None),
        P(("dp", "ep"), None),
    )
    return jax.shard_map(
        on_device,
        mesh=mesh,
        in_specs=placed,
        out_specs=(
            P(("dp", "ep"), None),
            P(("dp", "ep"), None),
            P(),
            P("ep", None),
            P("ep", None),
            P(),
            P("ep", None),
            P("ep", None),
            P(),
            P("ep", None, "dp"),
            P("ep", "dp", None),
        ),
        check_vma=False,
    )
```
